512 devices in a mesh: tm: 128 (over z_hi, y, x), space: 4 (over z_lo, core).
Axes of the slice: x: 4, y: 8, z: 8 (z_hi: 4, z_lo: 2; z = z_hi * 2 + z_lo), core: 2. Of those that a mesh axis runs over, the one named last changes fastest.
Arguments:
- patches: bfloat16 [256, 16, 16, 256], P('tm', 'space'), may hold values from -24 to 24
- stem_weight: bfloat16 [2304, 256], P('space'), may hold values from -0.125 to 0.125
- embed_weight: bfloat16 [256, 2048], P('space'), may hold values from -0.375 to 0.375
- frame_embed: bfloat16 [256, 2048], P('tm'), may hold values from -3 to 3
- attention_gain: bfloat16 [2048], replicated, may hold values from 0.5 to 1.5
- final_gain: bfloat16 [2048], replicated, may hold values from 0.5 to 1.5
- query_weight: bfloat16 [2048, 1024], P(None, 'space'), may hold values from -0.125 to 0.125
- key_weight: bfloat16 [2048, 1024], P(None, 'space'), may hold values from -0.125 to 0.125
- value_weight: bfloat16 [2048, 1024], P(None, 'space'), may hold values from -0.125 to 0.125
- output_weight: bfloat16 [1024, 2048], P('space'), may hold values from -0.1875 to 0.1875
- unembedding: bfloat16 [32768, 2048], P(('tm', 'space')), may hold values from -0.375 to 0.375
- rating_ids: int32 [5], replicated, may hold values from 0 to 32767
- target_score: int32 [1], replicated, may hold values from 1 to 5
Outputs:
- expected_score: float32 [1], replicated
- stem_gradient: float32 [589824], P(('tm', 'space'))
The draws below stay inside these ranges and needn't reach their ends.
All inputs are finite; a program needn't handle non-finite values.
Results may differ from the reference program's by a relative error of at most 0.008.
Values may be sent and summed in bfloat16 or wider, within the bound.
No kernel may reach another device: no remote copies, remote signals or barrier semaphores. Data moves between devices by JAX's collectives and lax.ppermute only.
A program may use at most 128 MiB of HBM per device.

```python
import math
import jax
import jax.numpy as jnp
from jax import lax

D = 2048
C = 256
HEAD = 128
HEADS = 8
VOCAB = 32768
RATINGS = 5
ROW_DEV = 4
COLS = 16
FRAMES = 256
ROWS = 16
N_SPACE = 4


def plant(array, own_key, smallest, top_value):
    place = [jax.random.randint(jax.random.fold_in(own_key, axis), (), 0, length) for axis, length in enumerate(array.shape)]
    widest = array.shape.index(max(array.shape))
    neighbour = place[:widest] + [(place[widest] + 1) % array.shape[widest]] + place[widest + 1:]
    return array.at[tuple(place)].set(smallest).at[tuple(neighbour)].set(top_value)


def strengthened(drawn, rng, source, target, blocks, factor):
    owner, partner = [(jnp.arange(drawn.shape[dim]) // (drawn.shape[dim] // blocks)).reshape([-1 if axis == dim else 1 for axis in range(drawn.ndim)]) for dim in (source, target)]
    chosen = jax.random.permutation(rng, blocks)[partner]
    strong = (owner == chosen) | (owner == (partner + blocks // 2) % blocks)
    return jnp.where(strong, factor * drawn, drawn)


def level_of(own_key, shape, shards, least, largest):
    loudness, own = 1.0, jax.random.fold_in(own_key, 6)
    for position, blocks in shards:
        steps = jnp.exp(jax.random.uniform(jax.random.fold_in(own, position), (blocks,), jnp.float32, least / len(shards), largest / len(shards)))
        loudness = loudness * jnp.repeat(steps, shape[position] // blocks).reshape([-1 if axis == position else 1 for axis in range(len(shape))])
    return loudness


def noise(rng, shape, deviation, limit, cuts=(), kind=jnp.bfloat16):
    drawn = jax.random.normal(rng, shape, jnp.float32) * deviation
    if len(cuts) > 0:
        drawn = level_of(rng, shape, cuts, -0.22, 0.18) * drawn
    return jnp.clip(drawn, min=-limit, max=limit).astype(kind)


def gaussian_with(key, extent, scale, bound, cuts, heavy, dtype=jnp.bfloat16):
    drawn = scale * jax.random.normal(key, extent, jnp.float32)
    if cuts:
        drawn = drawn * level_of(key, extent, cuts, -0.22, 0.18)
    return jnp.clip(strengthened(drawn, jax.random.fold_in(key, 3), *heavy), -bound, bound).astype(dtype)


def setup_inputs(seed: int = 0) -> dict:
    key_list = jax.random.split(jax.random.key(seed), 14)
    return {
        "patches": gaussian_with(key_list[0], (FRAMES, ROWS, COLS, C), 1.0, 24.0, ((0, 128), (1, 4)), (0, 3, 128, 5.5)),
        "stem_weight": noise(key_list[1], (9 * C, C), (9 * C) ** -0.5, 0.125, ((0, 4),)),
        "embed_weight": noise(key_list[2], (C, D), C ** -0.5, 0.375, ((0, 4),)),
        "frame_embed": noise(key_list[3], (FRAMES, D), 0.5, 3.0, ((0, 128),)),
        "attention_gain": jnp.clip(1.0 + 0.1 * jax.random.normal(key_list[4], (D,), jnp.float32), 0.5, 1.5).astype(jnp.bfloat16),
        "final_gain": jnp.clip(1.0 + 0.1 * jax.random.normal(key_list[5], (D,), jnp.float32), 0.5, 1.5).astype(jnp.bfloat16),
        "query_weight": noise(key_list[6], (D, HEADS * HEAD), D ** -0.5, 0.125, ((1, 4),)),
        "key_weight": noise(key_list[7], (D, HEADS * HEAD), D ** -0.5, 0.125, ((1, 4),)),
        "value_weight": noise(key_list[8], (D, HEADS * HEAD), D ** -0.5, 0.125, ((1, 4),)),
        "output_weight": noise(key_list[9], (HEADS * HEAD, D), (HEADS * HEAD) ** -0.5, 0.1875, ((0, 4),)),
        "unembedding": noise(key_list[10], (VOCAB, D), (D // 9) ** -0.5, 0.375, ((0, 512),)),
        "rating_ids": plant(jax.random.randint(key_list[11], (RATINGS,), 0, VOCAB), jax.random.fold_in(key_list[11], 1), 0, VOCAB - 1).astype(jnp.int32),
        "target_score": jax.random.randint(key_list[12], (1,), 1, 6).astype(jnp.int32),
    }


epsilon = 1e-05
highest = lax.Precision.HIGHEST

def rms_scale(values):
    return lax.rsqrt(lax.optimization_barrier(jnp.mean(values * values, axis=-1, keepdims=True)) + epsilon)

def rms_back(values, gain, upstream):
    inverse_rms = rms_scale(values)
    unit_rows = values * inverse_rms
    gained = gain * upstream
    return inverse_rms * (gained - unit_rows * lax.optimization_barrier(jnp.mean(gained * unit_rows, axis=-1, keepdims=True)))

def attend(queries, key_rows, value_rows):
    factor = 1.0 / math.sqrt(queries.shape[-1])
    scores = jnp.einsum('fih,gih->ifg', queries.astype(jnp.float32), key_rows.astype(jnp.float32)) * factor
    exact_weights = jax.nn.softmax(scores, axis=-1)
    rounded_weights = exact_weights.astype(jnp.bfloat16)
    mixture = jnp.einsum('ifg,gih->fih', rounded_weights.astype(jnp.float32), value_rows.astype(jnp.float32))
    return (exact_weights, rounded_weights, mixture.astype(jnp.bfloat16))

def attend_back(queries, key_rows, value_rows, exact_weights, rounded_weights, grad_mixture):
    factor = 1.0 / math.sqrt(queries.shape[-1])
    grad_weights = jnp.einsum('ih,gih->ig', grad_mixture, value_rows.astype(jnp.float32), precision=highest)
    column_mass = lax.optimization_barrier(jnp.sum(rounded_weights.astype(jnp.float32), axis=1))
    grad_values = jnp.transpose(column_mass)[:, :, None] * grad_mixture[None, :, :]
    centred = grad_weights[:, None, :] - lax.optimization_barrier(jnp.sum(exact_weights * grad_weights[:, None, :], axis=-1, keepdims=True))
    grad_scores = exact_weights * centred * factor
    grad_queries = jnp.einsum('ifg,gih->fih', grad_scores, key_rows.astype(jnp.float32), precision=highest)
    grad_keys = jnp.einsum('ifg,fih->gih', grad_scores, queries.astype(jnp.float32), precision=highest)
    return (grad_queries.astype(jnp.bfloat16), grad_keys.astype(jnp.bfloat16), grad_values.astype(jnp.bfloat16))

def head_terms(pooled_total, rating_rows, final_gain, target_score, tokens):
    pooled_raw = pooled_total / tokens
    inverse_rms = lax.rsqrt(jnp.mean(pooled_raw * pooled_raw) + epsilon)
    unit_rows = pooled_raw * inverse_rms
    gain = final_gain.astype(jnp.float32)
    pooled = unit_rows * gain
    logits = jnp.dot(rating_rows, pooled, precision=highest)
    rating_probs = jax.nn.softmax(logits)
    ladder = jnp.arange(1, rating_rows.shape[0] + 1).astype(jnp.float32)
    expected = jnp.sum(rating_probs * ladder)
    target = (jnp.arange(rating_rows.shape[0]).astype(jnp.int32) == target_score[0] - 1).astype(jnp.float32)
    grad_pooled = jnp.dot(rating_probs - target, rating_rows, precision=highest)
    gained = gain * grad_pooled
    grad_raw = inverse_rms * (gained - unit_rows * jnp.mean(gained * unit_rows))
    return (expected.reshape(1), grad_raw / math.sqrt(tokens))

def reference(patches, stem_weight, embed_weight, frame_embed, attention_gain, final_gain, query_weight, key_weight, value_weight, output_weight, unembedding, rating_ids, target_score):
    all_frames = patches.shape[0]
    positions = ROWS * COLS
    tokens = all_frames * positions
    inner = HEADS * HEAD
    group_width = inner // N_SPACE
    block = 16
    block_count = positions // block
    padded = jnp.pad(patches, ((0, 0), (1, 1), (1, 1), (0, 0)))
    stem_taps = stem_weight.reshape(9, C, C)
    stem_pre = jnp.zeros((tokens, C), jnp.float32)
    for tap_index in range(9):
        row_off = tap_index // 3
        col_off = tap_index % 3
        shifted = padded[:, row_off:row_off + ROWS, col_off:col_off + COLS, :].reshape(-1, C)
        stem_pre = stem_pre + jnp.dot(shifted, stem_taps[tap_index], preferred_element_type=jnp.float32)
    stem_act = jax.nn.gelu(stem_pre, approximate=True).astype(jnp.bfloat16)
    act_blocks = stem_act.reshape(all_frames, block_count, block, C).transpose(1, 0, 2, 3)
    pre_blocks = stem_pre.reshape(all_frames, block_count, block, C).transpose(1, 0, 2, 3)
    gain = attention_gain.astype(jnp.float32)
    frame_rows = frame_embed.astype(jnp.float32)[:, None, :]

    def embed_block(act_block):
        embedded = jnp.dot(act_block.reshape(-1, C), embed_weight, preferred_element_type=jnp.float32).reshape(all_frames, block, D)
        embedded = (embedded + frame_rows).astype(jnp.bfloat16)
        wide = embedded.astype(jnp.float32)
        normed = (wide * rms_scale(wide) * gain).astype(jnp.bfloat16).reshape(-1, D)
        queries = jnp.dot(normed, query_weight, preferred_element_type=jnp.float32).astype(jnp.bfloat16)
        key_rows = jnp.dot(normed, key_weight, preferred_element_type=jnp.float32).astype(jnp.bfloat16)
        value_rows = jnp.dot(normed, value_weight, preferred_element_type=jnp.float32).astype(jnp.bfloat16)
        shape_items = (all_frames, block * HEADS, HEAD)
        return (embedded, queries.reshape(shape_items), key_rows.reshape(shape_items), value_rows.reshape(shape_items))

    def forward_block(act_block):
        embedded, queries, key_rows, value_rows = embed_block(act_block)
        mixture = attend(queries, key_rows, value_rows)[2]
        embed_sum = lax.optimization_barrier(jnp.sum(embedded.astype(jnp.float32), axis=(0, 1)))
        mixture_sum = lax.optimization_barrier(jnp.sum(mixture.astype(jnp.float32), axis=0)).reshape(block, inner).sum(axis=0)
        return (embed_sum, mixture_sum)
    embed_sums, mixture_sums = lax.map(forward_block, act_blocks)
    output_wide = output_weight.astype(jnp.float32)
    pooled_total = lax.optimization_barrier(jnp.sum(embed_sums, axis=0)) + jnp.dot(lax.optimization_barrier(jnp.sum(mixture_sums, axis=0)), output_wide, precision=highest)
    rating_rows = unembedding[rating_ids].astype(jnp.float32)
    expected_score, cotangent = head_terms(pooled_total, rating_rows, final_gain, target_score, tokens)
    grad_heads = jnp.dot(output_wide, cotangent, precision=highest).reshape(HEADS, HEAD)
    grad_mixture = jnp.tile(grad_heads, (block, 1))

    def backward_block(block_args):
        act_block, pre_block, block_index = block_args
        embedded, queries, key_rows, value_rows = embed_block(act_block)
        exact_weights, rounded_weights, mixture = attend(queries, key_rows, value_rows)
        grad_q, grad_k, grad_v = attend_back(queries, key_rows, value_rows, exact_weights, rounded_weights, grad_mixture)
        grad_q = grad_q.reshape(-1, inner)
        grad_k = grad_k.reshape(-1, inner)
        grad_v = grad_v.reshape(-1, inner)
        wide = embedded.astype(jnp.float32)
        slots = block_index * block + jnp.arange(block).astype(jnp.int32)
        owner_tile = slots // COLS // ROW_DEV
        _, gelu_back = jax.vjp(lambda value: jax.nn.gelu(value, approximate=True), pre_block.reshape(-1, C))
        total = jnp.zeros((all_frames * block, C), jnp.float32)
        for group in range(N_SPACE):
            low = group * group_width
            high = low + group_width
            grad_normed = jnp.dot(grad_q[:, low:high], query_weight[:, low:high].T, preferred_element_type=jnp.float32)
            grad_normed = grad_normed + jnp.dot(grad_k[:, low:high], key_weight[:, low:high].T, preferred_element_type=jnp.float32)
            grad_normed = grad_normed + jnp.dot(grad_v[:, low:high], value_weight[:, low:high].T, preferred_element_type=jnp.float32)
            grad_normed = grad_normed.reshape(all_frames, block, D)
            own_tile = (owner_tile == group).astype(jnp.float32)[None, :, None]
            grad_embed = (rms_back(wide, gain, grad_normed) + own_tile * cotangent).astype(jnp.bfloat16)
            grad_act = jnp.dot(grad_embed.reshape(-1, D), embed_weight.T, preferred_element_type=jnp.float32)
            grad_pre = lax.optimization_barrier(gelu_back(grad_act)[0].astype(jnp.bfloat16))
            total = total + grad_pre.astype(jnp.float32)
        return total.reshape(all_frames, block, C)
    block_numbers = jnp.arange(block_count).astype(jnp.int32)
    grad_blocks = lax.map(backward_block, (act_blocks, pre_blocks, block_numbers))
    grad_pre_sum = grad_blocks.transpose(1, 0, 2, 3).reshape(tokens, C)
    pieces = []
    for tap_index in range(9):
        row_off = tap_index // 3
        col_off = tap_index % 3
        shifted = padded[:, row_off:row_off + ROWS, col_off:col_off + COLS, :].reshape(-1, C).astype(jnp.float32)
        pieces.append(jnp.dot(shifted.T, grad_pre_sum, precision=highest))
    stem_gradient = jnp.stack(pieces, axis=0).reshape(-1)
    return (expected_score, stem_gradient)
```

```python
import functools
import math

import jax
import jax.numpy as jnp
from jax import lax
from jax.experimental import pallas as pl
from jax.experimental.pallas import tpu as pltpu
from jax.sharding import Mesh, PartitionSpec as P

HEAD = 128
LANES = 128
EPSILON = 1e-05
BF = jnp.bfloat16
F32 = jnp.float32
T_AXES = ("zh", "y", "x")
S_AXES = ("zl", "core")
FACTORS = {128: (4, 8, 4), 8: (2, 2, 2)}
NT = (((1,), (1,)), ((), ()))
TN = (((0,), (0,)), ((), ()))
VMEM_LIMIT = 48 * 1024 * 1024


def dot(lhs, rhs, dims=(((1,), (0,)), ((), ()))):
    return lax.dot_general(lhs, rhs, dims, preferred_element_type=F32)


def thirds(row):
    first = row.astype(BF)
    rest = row - first.astype(F32)
    second = rest.astype(BF)
    third = (rest - second.astype(F32)).astype(BF)
    zero = jnp.zeros((5, row.shape[1]), F32)
    parts = [first.astype(F32), second.astype(F32), third.astype(F32), zero]
    return jnp.concatenate(parts, axis=0).astype(BF)


def halves(values):
    first = values.astype(BF)
    return first, (values - first.astype(F32)).astype(BF)


def neighbourhoods(frames):
    count_rows = frames.shape[1]
    count_cols = frames.shape[2]
    padded = jnp.pad(frames, ((0, 0), (1, 1), (1, 1), (0, 0)))
    pieces = [
        padded[:, row_off : row_off + count_rows, col_off : col_off + count_cols, :]
        for row_off in range(3)
        for col_off in range(3)
    ]
    return jnp.concatenate(pieces, axis=-1)


def split_heads(block, heads):
    inner = heads * HEAD
    for head in range(heads):
        at = head * HEAD
        yield (
            head,
            block[:, at : at + HEAD],
            block[:, inner + at : inner + at + HEAD],
            block[:, 2 * inner + at : 2 * inner + at + HEAD],
        )


def forward_kernel(heads, qkv_ref, out_weight_ref, embed_sum_ref, weights_ref, pooled_ref):
    slots = qkv_ref.shape[0]
    factor = 1.0 / math.sqrt(HEAD)
    sums = [0.0] * heads
    for slot in range(slots):
        for head, query, key, value in split_heads(qkv_ref[slot], heads):
            scores = dot(key, query, NT) * factor
            top = jnp.max(scores, axis=0, keepdims=True)
            raised = jnp.exp(scores - top)
            weights = raised / jnp.sum(raised, axis=0, keepdims=True)
            weights_ref[slot * heads + head] = weights
            mixture = dot(weights.astype(BF), value, TN).astype(BF).astype(F32)
            sums[head] = sums[head] + jnp.sum(mixture, axis=0, keepdims=True)
    mixture_sum = thirds(jnp.concatenate(sums, axis=1))
    mixed = jnp.sum(dot(mixture_sum, out_weight_ref[...]), axis=0, keepdims=True)
    pooled_ref[...] = embed_sum_ref[...] + mixed


def backward_kernel(
    heads,
    tokens,
    ratings,
    target_ref,
    pooled_ref,
    rating_ref,
    gain_ref,
    out_weight_ref,
    own_embed_ref,
    qkv_ref,
    weights_ref,
    back_first_ref,
    back_second_ref,
    expected_ref,
    direct_ref,
    sent_ref,
    mean_ref,
):
    width = pooled_ref.shape[1]
    pooled_raw = pooled_ref[...] / tokens
    inverse_rms = lax.rsqrt(jnp.mean(pooled_raw * pooled_raw, axis=1, keepdims=True) + EPSILON)
    unit = pooled_raw * inverse_rms
    gain = gain_ref[...].astype(F32)
    rows = rating_ref[...]
    logits = jnp.sum(rows * (unit * gain), axis=1, keepdims=True)
    index = lax.broadcasted_iota(jnp.int32, logits.shape, 0)
    real = index < ratings
    logits = jnp.where(real, logits, -jnp.inf)
    raised = jnp.exp(logits - jnp.max(logits, axis=0, keepdims=True))
    probs = raised / jnp.sum(raised, axis=0, keepdims=True)
    ladder = (index + 1).astype(F32)
    expected = jnp.sum(probs * ladder, axis=0, keepdims=True)
    expected_ref[...] = jnp.broadcast_to(expected, expected_ref.shape)
    hit = (index == target_ref[0] - 1).astype(F32)
    gained = gain * jnp.sum((probs - hit) * rows, axis=0, keepdims=True)
    centre = jnp.mean(gained * unit, axis=1, keepdims=True)
    cotangent = inverse_rms * (gained - unit * centre) / math.sqrt(tokens)
    parts = thirds(cotangent)
    direct = jnp.sum(dot(own_embed_ref[...], parts, NT), axis=1, keepdims=True)
    direct_ref[...] = jnp.broadcast_to(direct, direct_ref.shape)
    grad_heads = jnp.sum(dot(parts, out_weight_ref[...], NT), axis=0, keepdims=True)
    factor = 1.0 / math.sqrt(HEAD)
    slots, frames = qkv_ref.shape[0], qkv_ref.shape[1]
    half = frames // 2
    for slot in range(slots):
        grads_q, grads_k, grads_v = [], [], []
        total = jnp.zeros((frames, 1), F32)
        for head, query, key, value in split_heads(qkv_ref[slot], heads):
            grad_mixture = grad_heads[:, head * HEAD : (head + 1) * HEAD]
            weights = weights_ref[slot * heads + head]
            wide_value = value.astype(F32)
            grad_weights = jnp.sum(wide_value * grad_mixture, axis=1, keepdims=True)
            centre = jnp.sum(weights * grad_weights, axis=0, keepdims=True)
            upper, lower = halves(weights * (grad_weights - centre) * factor)
            grad_query = dot(upper, key, TN) + dot(lower, key, TN)
            grad_key = dot(upper, query) + dot(lower, query)
            mass = jnp.sum(weights.astype(BF).astype(F32), axis=1, keepdims=True)
            grad_value = mass * grad_mixture
            total = total + jnp.sum(
                grad_query * query.astype(F32)
                + grad_key * key.astype(F32)
                + grad_value * wide_value,
                axis=1,
                keepdims=True,
            )
            grads_q.append(grad_query.astype(BF))
            grads_k.append(grad_key.astype(BF))
            grads_v.append(grad_value.astype(BF))
        grads = jnp.concatenate(grads_q + grads_k + grads_v, axis=1)
        sent = dot(grads[:half], back_first_ref[...]) + dot(grads[half:], back_second_ref[...])
        sent_ref[slot] = sent.astype(BF)
        mean_ref[slot] = jnp.broadcast_to(total / width, (frames, mean_ref.shape[2]))


def on_device(
    patches,
    stem_weight,
    embed_weight,
    frame_embed,
    attention_gain,
    final_gain,
    query_weight,
    key_weight,
    value_weight,
    output_weight,
    unembedding,
    rating_ids,
    target_score,
):
    n_t = lax.axis_size(T_AXES)
    n_s = lax.axis_size(S_AXES)
    everyone = T_AXES + S_AXES
    space_index = lax.axis_index(S_AXES)
    frames_dev, rows_dev, cols, channels = patches.shape
    own_channels = channels // n_s
    count_rows = rows_dev * n_s
    positions = count_rows * cols
    slots = positions // n_t
    width = embed_weight.shape[1]
    inner = query_weight.shape[1]
    heads = inner // HEAD
    all_frames = frames_dev * n_t
    tokens = all_frames * positions
    tokens_dev = frames_dev * positions
    assert frames_dev == 2 and slots == 2

    pair = lax.all_gather(embed_weight, "core", axis=0, tiled=True)
    other = lax.ppermute(pair, "zl", [(0, 1), (1, 0)])

    lane_blocks = channels // LANES
    patch_rows = patches.reshape(-1, channels)
    patch_part = jnp.concatenate(
        [patch_rows[:, i * LANES : (i + 1) * LANES] for i in range(lane_blocks)], axis=0
    )
    stem_rows = stem_weight.shape[0]
    stem_half = stem_rows // 2
    stem_part = stem_weight.reshape(2, stem_half, n_s, own_channels).transpose(2, 1, 0, 3)
    stem_part = stem_part.reshape(n_s, stem_half, 2 * own_channels)
    packed = jnp.concatenate(
        [jnp.broadcast_to(patch_part[None], (n_s,) + patch_part.shape), stem_part], axis=1
    )
    packed = lax.all_to_all(packed, S_AXES, 0, 0, tiled=True)
    count = patch_part.shape[0]
    got = packed[:, :count].reshape(n_s, lane_blocks, frames_dev, rows_dev, cols, LANES)
    full_patches = got.transpose(2, 0, 3, 4, 1, 5).reshape(
        frames_dev, count_rows, cols, channels
    )
    stem_cols = packed[:, count:].reshape(n_s, stem_half, 2, own_channels)
    stem_cols = stem_cols.transpose(0, 2, 1, 3).reshape(n_s * stem_rows, own_channels)

    beside = neighbourhoods(full_patches).reshape(tokens_dev, 9 * channels)
    stem_pre = dot(stem_cols, beside, (((0,), (1,)), ((), ())))
    stem_act, gelu_back = jax.vjp(lambda value: jax.nn.gelu(value, approximate=True), stem_pre)
    (gelu_slope,) = gelu_back(jnp.ones_like(stem_pre))
    act = lax.all_gather(stem_act.astype(BF), S_AXES, axis=0, tiled=True)

    lower = lax.axis_index("zl") == 0
    full_embed = jnp.concatenate(
        [jnp.where(lower, pair, other), jnp.where(lower, other, pair)], axis=0
    )
    gain = attention_gain.astype(F32)
    embedded = dot(act, full_embed, TN).reshape(frames_dev, positions, width)
    embedded = (embedded + frame_embed.astype(F32)[:, None, :]).astype(BF)
    embedded = embedded.reshape(tokens_dev, width)
    wide = embedded.astype(F32)
    scale = lax.rsqrt(jnp.mean(wide * wide, axis=-1, keepdims=True) + EPSILON)
    normed = (wide * scale * gain).astype(BF)
    qkv = jnp.concatenate(
        [dot(normed, w).astype(BF) for w in (query_weight, key_weight, value_weight)], axis=1
    )
    embed_sum = jnp.sum(wide, axis=0, keepdims=True) * (1.0 / n_s)
    scale_row = scale.reshape(1, tokens_dev)
    back_unit = dot(embed_weight, embedded, NT) * scale_row

    vocab_dev = unembedding.shape[0]
    ratings = rating_ids.shape[0]
    first_row = lax.axis_index(everyone) * vocab_dev
    picks = (rating_ids[:, None] - first_row == jnp.arange(vocab_dev)[None, :]).astype(BF)
    rows_part = dot(picks, unembedding).astype(BF)
    groups = width // n_t
    rating_part = rows_part.reshape(ratings * groups, n_t).T
    rating_part = jnp.pad(rating_part, ((0, 0), (0, LANES - ratings * groups)))
    rating_part = jnp.pad(rating_part[:, None, :], ((0, 0), (0, slots * frames_dev - 1), (0, 0)))

    qkv = qkv.reshape(frames_dev, slots, n_t, 3 * inner).transpose(2, 1, 0, 3)
    qkv = qkv.reshape(n_t, slots * frames_dev, 3 * inner)
    moved = jnp.concatenate([qkv, rating_part], axis=2)
    moved = lax.all_to_all(moved, T_AXES, 0, 0, tiled=True)
    qkv = moved[:, :, : 3 * inner].transpose(1, 0, 2).reshape(slots, all_frames, 3 * inner)
    rating_slice = jnp.sum(moved[:, 0, 3 * inner :].astype(F32), axis=0, keepdims=True)

    items = slots * heads
    whole = pl.BlockSpec(memory_space=pltpu.VMEM)
    weights, pooled_part = pl.pallas_call(
        functools.partial(forward_kernel, heads),
        name="attend",
        out_shape=(
            jax.ShapeDtypeStruct((items, all_frames, all_frames), F32),
            jax.ShapeDtypeStruct((1, width), F32),
        ),
        in_specs=[whole] * 3,
        out_specs=(whole, whole),
        compiler_params=pltpu.CompilerParams(vmem_limit_bytes=VMEM_LIMIT),
    )(qkv, output_weight, embed_sum)

    pooled_rows = pooled_part.reshape(width // LANES, LANES)
    rating_rows = rating_slice
    for axes in (("x",) + S_AXES, ("y",), ("zh",)):
        size = lax.axis_size(axes)
        packed = jnp.concatenate([pooled_rows, rating_rows], axis=0)
        packed = jnp.broadcast_to(packed[None], (size,) + packed.shape)
        packed = lax.all_to_all(packed, axes, 0, 0, tiled=True)
        pooled_rows = jnp.sum(packed[:, : width // LANES], axis=0)
        rating_rows = packed[:, width // LANES :]
        if len(axes) > 1:
            rating_rows = rating_rows.reshape(size // n_s, n_s, LANES).sum(axis=1)
        rating_rows = rating_rows.reshape(-1, LANES)
    rating_rows = rating_rows[:, : ratings * groups].T.reshape(ratings, width)
    rating_rows = jnp.pad(rating_rows, ((0, 8 - ratings), (0, 0)))

    scaled = (full_embed.astype(F32) * gain).astype(BF)
    back = jnp.concatenate(
        [
            dot(w, scaled, (((0,), (1,)), ((), ()))).astype(BF)
            for w in (query_weight, key_weight, value_weight)
        ],
        axis=0,
    ).reshape(3 * inner, n_s, own_channels)
    blank = jnp.zeros_like(back)
    sent_width = n_s * frames_dev * own_channels
    back_first = jnp.concatenate([back, blank], axis=2).reshape(3 * inner, sent_width)
    back_second = jnp.concatenate([blank, back], axis=2).reshape(3 * inner, sent_width)

    expected, direct, sent, means = pl.pallas_call(
        functools.partial(backward_kernel, heads, float(tokens), ratings),
        name="attend_back",
        out_shape=(
            jax.ShapeDtypeStruct((8, LANES), F32),
            jax.ShapeDtypeStruct((own_channels, LANES), F32),
            jax.ShapeDtypeStruct((slots, n_t, sent_width), BF),
            jax.ShapeDtypeStruct((slots, all_frames, 8), F32),
        ),
        in_specs=[pl.BlockSpec(memory_space=pltpu.SMEM)] + [whole] * 9,
        out_specs=(whole,) * 4,
        compiler_params=pltpu.CompilerParams(vmem_limit_bytes=VMEM_LIMIT),
    )(
        target_score,
        pooled_rows.reshape(1, width),
        rating_rows,
        final_gain[None, :],
        output_weight,
        embed_weight,
        qkv,
        weights,
        back_first,
        back_second,
    )

    pair_lanes = frames_dev * own_channels
    sent = sent.reshape(slots, n_t, n_s, pair_lanes).transpose(1, 2, 0, 3)
    means = means[:, :, 0].reshape(slots * frames_dev, n_t).T.astype(BF)
    means = jnp.pad(means, ((0, 0), (0, pair_lanes - slots * frames_dev)))
    means = jnp.broadcast_to(means[:, None, None, :], (n_t, n_s, 1, pair_lanes))
    sent = jnp.concatenate([sent, means], axis=2).reshape(n_t * n_s, slots + 1, pair_lanes)
    sent = lax.all_to_all(sent, everyone, 0, 0, tiled=True)
    sent = jnp.sum(sent.reshape(n_t, n_s, slots + 1, pair_lanes).astype(F32), axis=1)
    turned = sent.transpose(1, 2, 0)
    grad_unit = turned[:slots].reshape(slots, frames_dev, own_channels, n_t)
    grad_unit = grad_unit.transpose(2, 1, 0, 3).reshape(own_channels, tokens_dev)
    mean_row = turned[slots, : slots * frames_dev].reshape(slots, frames_dev, n_t)
    mean_row = mean_row.transpose(1, 0, 2).reshape(1, tokens_dev)
    grad_act = scale_row * (grad_unit - mean_row * back_unit) + direct[:, :1]
    grad_pre = (gelu_slope * grad_act).astype(BF)

    local_grad = dot(beside, grad_pre, (((0,), (1,)), ((), ())))
    lines = local_grad.reshape(n_t, -1, LANES).astype(BF)
    step = lines.shape[1] // n_s
    window = -(-lines.shape[1] // n_s)
    lines = jnp.stack([lines[:, step * s : step * s + window] for s in range(n_s)], axis=1)
    lines = lines.reshape(n_t * n_s, window, LANES)
    lines = lax.all_to_all(lines, everyone, 0, 0, tiled=True)
    lines = jnp.sum(lines.reshape(n_t, n_s, window, LANES).astype(F32), axis=0)
    flat = lines.reshape(n_s, -1, own_channels).transpose(1, 0, 2).reshape(-1)
    length = 9 * channels * channels // (n_t * n_s)
    start = space_index * (length - step * LANES * n_s)
    stem_gradient = lax.dynamic_slice_in_dim(flat, start, length, 0)
    return (expected[0, :1], stem_gradient)


def solution(mesh):
    shape = FACTORS[mesh.shape["tm"]] + (2, 2)
    split = Mesh(mesh.devices.reshape(shape), T_AXES + S_AXES)
    both = T_AXES + S_AXES
    in_specs = (
        P(T_AXES, S_AXES, None, None),
        P(S_AXES, None),
        P(S_AXES, None),
        P(T_AXES, None),
        P(),
        P(),
        P(None, S_AXES),
        P(None, S_AXES),
        P(None, S_AXES),
        P(S_AXES, None),
        P(both, None),
        P(),
        P(),
    )
    return jax.shard_map(
        on_device, mesh=split, in_specs=in_specs, out_specs=(P(), P(both)), check_vma=False
    )
```

```python
import functools
import math

import jax
import jax.numpy as jnp
from jax import lax
from jax.experimental import pallas as pl
from jax.experimental.pallas import tpu as pltpu
from jax.sharding import Mesh, PartitionSpec as P

HEAD = 128
LANES = 128
EPSILON = 1e-05
BF = jnp.bfloat16
F32 = jnp.float32
T_AXES = ("zh", "y", "x")
S_AXES = ("zl", "core")
FACTORS = {128: (4, 8, 4), 8: (2, 2, 2)}
NT = (((1,), (1,)), ((), ()))
TN = (((0,), (0,)), ((), ()))
VMEM_LIMIT = 20 * 1024 * 1024
LINES = 4
N_S = 4
SPACE_OF_BLOCK = (0, 2, 1, 3)


def dot(lhs, rhs, dims=(((1,), (0,)), ((), ()))):
    return lax.dot_general(lhs, rhs, dims, preferred_element_type=F32)


def thirds(row):
    first = row.astype(BF)
    rest = row - first.astype(F32)
    second = rest.astype(BF)
    third = (rest - second.astype(F32)).astype(BF)
    zero = jnp.zeros((5, row.shape[1]), F32)
    parts = [first.astype(F32), second.astype(F32), third.astype(F32), zero]
    return jnp.concatenate(parts, axis=0).astype(BF)


def halves(values):
    first = values.astype(BF)
    return first, (values - first.astype(F32)).astype(BF)


def in_window(lanes, cols, rows, row_off, col_off):
    lane = lax.broadcasted_iota(jnp.int32, (1, lanes), 1) % (rows * cols)
    row = lane // cols + row_off
    col = lane % cols + col_off
    return ((row >= 0) & (row < rows) & (col >= 0) & (col < cols)).astype(F32)


def offsets():
    return [(a, b) for a in (-1, 0, 1) for b in (-1, 0, 1)]


def stem_kernel(cols, rows, packed_ref, act_ref, slope_ref, tokens_ref, weight_ref):
    n_s = packed_ref.shape[0]
    lanes, channels = tokens_ref.shape
    own = act_ref.shape[0]
    frames = lanes // (rows * cols)
    block = lanes // (frames * n_s)
    lane_blocks = channels // LANES
    count = lane_blocks * frames * block
    half = packed_ref.shape[1] - count
    for s in range(n_s):
        for part in range(lane_blocks):
            for frame in range(frames):
                source = (part * frames + frame) * block
                target = (frame * n_s + s) * block
                tokens_ref[target : target + block, part * LANES : (part + 1) * LANES] = packed_ref[
                    s, source : source + block, :
                ]
        pairs = packed_ref[s, count:, :]
        at = 2 * s * half
        weight_ref[at : at + half, :] = pairs[:, :own]
        weight_ref[at + half : at + 2 * half, :] = pairs[:, own:]
    tokens = tokens_ref[...]
    total = jnp.zeros((own, lanes), F32)
    for tap, (row_off, col_off) in enumerate(offsets()):
        weight = weight_ref[tap * channels : (tap + 1) * channels, :]
        part = dot(weight, tokens, (((0,), (1,)), ((), ())))
        shift = row_off * cols + col_off
        if shift:
            part = pltpu.roll(part, (-shift) % lanes, 1)
        total = total + in_window(lanes, cols, rows, row_off, col_off) * part
    root = math.sqrt(2.0 / math.pi)
    square = total * total
    bent = jnp.tanh(root * (total + 0.044715 * (square * total)))
    half_up = 0.5 * (1.0 + bent)
    act_ref[...] = (total * half_up).astype(BF)
    slope_ref[...] = half_up + 0.5 * total * (1.0 - bent * bent) * (
        root * (1.0 + 3 * 0.044715 * square)
    )


def stem_back_kernel(
    cols,
    rows,
    slots,
    frames,
    got_ref,
    back_unit_ref,
    scale_ref,
    direct_ref,
    slope_ref,
    tokens_ref,
    out_ref,
    grad_ref,
    lines_ref,
):
    lanes, channels = tokens_ref.shape
    own = slope_ref.shape[0]
    depth = got_ref.shape[0] // LINES
    turned = [got_ref[pl.ds(i, depth, stride=LINES), :].T for i in range(slots + 1)]
    unit = jnp.concatenate(
        [turned[s][f * own : (f + 1) * own] for f in range(frames) for s in range(slots)], axis=1
    )
    mean = jnp.concatenate(
        [
            turned[slots][s * frames + f : s * frames + f + 1]
            for f in range(frames)
            for s in range(slots)
        ],
        axis=1,
    )
    grad_act = scale_ref[...] * (unit - mean * back_unit_ref[...]) + direct_ref[:, :1]
    grad_pre = (slope_ref[...] * grad_act).astype(BF).astype(F32)
    tokens = tokens_ref[...]
    for tap, (row_off, col_off) in enumerate(offsets()):
        moved = in_window(lanes, cols, rows, row_off, col_off) * grad_pre
        shift = row_off * cols + col_off
        if shift:
            moved = pltpu.roll(moved, shift % lanes, 1)
        part = dot(tokens, moved.astype(BF), (((0,), (1,)), ((), ())))
        grad_ref[tap * channels : (tap + 1) * channels, :] = part
    count = lines_ref.shape[0]
    lines_ref[...] = jnp.concatenate(
        [grad_ref[pl.ds(i, count, stride=2), :] for i in range(2)], axis=1
    )
    step, window = line_window(count, depth)
    out_lines = out_ref.shape[0] // (N_S * depth)
    blank = jnp.zeros((depth, LANES), F32)
    for s in range(N_S):
        for line in range(out_lines):
            value = blank
            if line < window:
                value = lines_ref[pl.ds(step * s + line, depth, stride=count // depth), :]
            out_ref[pl.ds(s * out_lines + line, depth, stride=N_S * out_lines), :] = value


def line_window(count, depth):
    per = count // depth
    return per // N_S, -(-per // N_S)


def split_heads(block, heads):
    inner = heads * HEAD
    for head in range(heads):
        at = head * HEAD
        yield (
            head,
            block[:, at : at + HEAD],
            block[:, inner + at : inner + at + HEAD],
            block[:, 2 * inner + at : 2 * inner + at + HEAD],
        )


def as_lines(row):
    return jnp.concatenate(
        [row[:, i : i + LANES] for i in range(0, row.shape[1], LANES)], axis=0
    )


def as_row(lines):
    return jnp.concatenate([lines[i : i + 1] for i in range(lines.shape[0])], axis=1)


def forward_kernel(
    heads, qkv_ref, out_weight_ref, embed_sum_ref, rating_ref, back_ref, weights_ref, packed_ref
):
    del back_ref
    slots = qkv_ref.shape[0]
    factor = 1.0 / math.sqrt(HEAD)
    sums = [0.0] * heads
    for slot in range(slots):
        for head, query, key, value in split_heads(qkv_ref[slot], heads):
            scores = dot(key, query, NT) * factor
            top = jnp.max(scores, axis=0, keepdims=True)
            raised = jnp.exp(scores - top)
            weights = raised / jnp.sum(raised, axis=0, keepdims=True)
            weights_ref[slot * heads + head] = weights
            mixture = dot(weights.astype(BF), value, TN).astype(BF).astype(F32)
            sums[head] = sums[head] + jnp.sum(mixture, axis=0, keepdims=True)
    mixture_sum = thirds(jnp.concatenate(sums, axis=1))
    mixed = jnp.sum(dot(mixture_sum, out_weight_ref[...]), axis=0, keepdims=True)
    pooled = as_lines(embed_sum_ref[...] + mixed)
    rating = jnp.sum(rating_ref[...].astype(F32), axis=0, keepdims=True)
    blank = jnp.zeros((packed_ref.shape[1] - pooled.shape[0] - 1, LANES), F32)
    packed = jnp.concatenate([pooled, rating, blank], axis=0)
    for i in range(packed_ref.shape[0]):
        packed_ref[i] = packed


def combine_kernel(lines, per, joint, in_ref, out_ref):
    size = in_ref.shape[0]
    pooled = in_ref[0, :lines]
    for i in range(1, size):
        pooled = pooled + in_ref[i, :lines]
    ratings = []
    for i in range(0, size, joint):
        rating = in_ref[i, lines : lines + per]
        for j in range(1, joint):
            rating = rating + in_ref[i + j, lines : lines + per]
        ratings.append(rating)
    parts = [pooled] + ratings
    left = out_ref.shape[1] - lines - per * len(ratings)
    if left:
        parts.append(jnp.zeros((left, LANES), F32))
    packed = jnp.concatenate(parts, axis=0)
    for i in range(out_ref.shape[0]):
        out_ref[i] = packed


def backward_kernel(
    heads,
    tokens,
    ratings,
    target_ref,
    packed_ref,
    gain_ref,
    out_weight_ref,
    own_embed_ref,
    qkv_ref,
    weights_ref,
    back_ref,
    expected_ref,
    direct_ref,
    sent_ref,
):
    lines = gain_ref.shape[0]
    width = lines * LANES
    pooled = packed_ref[0, :lines]
    for i in range(1, packed_ref.shape[0]):
        pooled = pooled + packed_ref[i, :lines]
    turned = jnp.concatenate([packed_ref[i, lines:] for i in range(packed_ref.shape[0])], axis=0)
    pad = LANES - turned.shape[0]
    if pad:
        turned = jnp.concatenate([turned, jnp.zeros((pad, LANES), F32)], axis=0)
    n_t = packed_ref.shape[0] * (packed_ref.shape[1] - lines)
    turned = turned.T[:, :n_t]
    groups = width // n_t
    rows = [turned[r * groups : (r + 1) * groups] for r in range(ratings)]
    if n_t != LANES:
        rows = [as_lines(as_row(row)) for row in rows]

    def total_of(values):
        return jnp.sum(jnp.sum(values, axis=1, keepdims=True), axis=0, keepdims=True)

    pooled_raw = pooled / tokens
    inverse_rms = lax.rsqrt(total_of(pooled_raw * pooled_raw) / width + EPSILON)
    unit = pooled_raw * inverse_rms
    gain = gain_ref[...].astype(F32)
    gained_unit = unit * gain
    logits = [total_of(row * gained_unit) for row in rows]
    top = functools.reduce(jnp.maximum, logits)
    raised = [jnp.exp(logit - top) for logit in logits]
    norm = sum(raised)
    probs = [value / norm for value in raised]
    expected = sum((r + 1.0) * prob for r, prob in enumerate(probs))
    expected_ref[...] = jnp.broadcast_to(expected, expected_ref.shape)
    target = target_ref[0]
    mixed = sum(
        (prob - jnp.where(target == r + 1, 1.0, 0.0)) * rows[r] for r, prob in enumerate(probs)
    )
    gained = gain * mixed
    centre = total_of(gained * unit) / width
    cotangent = inverse_rms * (gained - unit * centre) / math.sqrt(tokens)
    parts = thirds(as_row(cotangent))
    direct = jnp.sum(dot(own_embed_ref[...], parts, NT), axis=1, keepdims=True)
    direct_ref[...] = jnp.broadcast_to(direct, direct_ref.shape)
    grad_heads = jnp.sum(dot(parts, out_weight_ref[...], NT), axis=0, keepdims=True)
    factor = 1.0 / math.sqrt(HEAD)
    slots, frames = qkv_ref.shape[0], qkv_ref.shape[1]
    depth = frames // 2
    back_upper, back_lower = halves(back_ref[...])
    own = back_ref.shape[1] // N_S
    lane = lax.broadcasted_iota(jnp.int32, (1, LANES), 1)
    means = jnp.zeros((depth, LANES), F32)
    for slot in range(slots):
        grads_q, grads_k, grads_v = [], [], []
        total = jnp.zeros((frames, 1), F32)
        for head, query, key, value in split_heads(qkv_ref[slot], heads):
            grad_mixture = grad_heads[:, head * HEAD : (head + 1) * HEAD]
            weights = weights_ref[slot * heads + head]
            wide_value = value.astype(F32)
            grad_weights = jnp.sum(wide_value * grad_mixture, axis=1, keepdims=True)
            centre = jnp.sum(weights * grad_weights, axis=0, keepdims=True)
            upper, lower = halves(weights * (grad_weights - centre) * factor)
            grad_query = dot(upper, key, TN) + dot(lower, key, TN)
            grad_key = dot(upper, query) + dot(lower, query)
            mass = jnp.sum(weights.astype(BF).astype(F32), axis=1, keepdims=True)
            grad_value = mass * grad_mixture
            total = total + jnp.sum(
                grad_query * query.astype(F32)
                + grad_key * key.astype(F32)
                + grad_value * wide_value,
                axis=1,
                keepdims=True,
            )
            grads_q.append(grad_query.astype(BF))
            grads_k.append(grad_key.astype(BF))
            grads_v.append(grad_value.astype(BF))
        grads = jnp.concatenate(grads_q + grads_k + grads_v, axis=1)
        sent = dot(grads, back_upper) + dot(grads, back_lower)
        for block in range(N_S):
            s = SPACE_OF_BLOCK[block]
            both = [
                sent[f * depth : (f + 1) * depth, block * own : (block + 1) * own]
                for f in range(2)
            ]
            sent_ref[pl.ds(s * LINES + slot, depth, stride=N_S * LINES), :] = jnp.concatenate(
                both, axis=1
            )
        for f in range(2):
            column = total[f * depth : (f + 1) * depth] / width
            means = means + jnp.where(lane == slot * 2 + f, 1.0, 0.0) * column
    blank = jnp.zeros((depth, LANES), F32)
    for s in range(N_S):
        sent_ref[pl.ds(s * LINES + slots, depth, stride=N_S * LINES), :] = means
        for line in range(slots + 1, LINES):
            sent_ref[pl.ds(s * LINES + line, depth, stride=N_S * LINES), :] = blank


def on_device(
    patches,
    stem_weight,
    embed_weight,
    frame_embed,
    attention_gain,
    final_gain,
    query_weight,
    key_weight,
    value_weight,
    output_weight,
    unembedding,
    rating_ids,
    target_score,
):
    n_t = lax.axis_size(T_AXES)
    n_s = lax.axis_size(S_AXES)
    everyone = T_AXES + S_AXES
    space_index = lax.axis_index(S_AXES)
    frames_dev, rows_dev, cols, channels = patches.shape
    own_channels = channels // n_s
    count_rows = rows_dev * n_s
    positions = count_rows * cols
    slots = positions // n_t
    width = embed_weight.shape[1]
    inner = query_weight.shape[1]
    heads = inner // HEAD
    all_frames = frames_dev * n_t
    tokens = all_frames * positions
    tokens_dev = frames_dev * positions
    assert frames_dev == 2 and slots == 2

    whole = pl.BlockSpec(memory_space=pltpu.VMEM)
    params = pltpu.CompilerParams(vmem_limit_bytes=VMEM_LIMIT)
    other = lax.ppermute(embed_weight, "zl", [(0, 1), (1, 0)])

    lane_blocks = channels // LANES
    patch_rows = patches.reshape(-1, channels)
    patch_part = jnp.concatenate(
        [patch_rows[:, i * LANES : (i + 1) * LANES] for i in range(lane_blocks)], axis=0
    )
    stem_half = stem_weight.shape[0] // 2
    stem_part = jnp.stack(
        [
            jnp.concatenate(
                [
                    stem_weight[h * stem_half : (h + 1) * stem_half, c : c + own_channels]
                    for h in range(2)
                ],
                axis=1,
            )
            for c in range(0, channels, own_channels)
        ],
        axis=0,
    )
    packed = jnp.concatenate(
        [jnp.broadcast_to(patch_part[None], (n_s,) + patch_part.shape), stem_part], axis=1
    )
    packed = lax.all_to_all(packed, S_AXES, 0, 0, tiled=True)

    act, gelu_slope, patch_tokens = pl.pallas_call(
        functools.partial(stem_kernel, cols, count_rows),
        name="stem",
        out_shape=(
            jax.ShapeDtypeStruct((own_channels, tokens_dev), BF),
            jax.ShapeDtypeStruct((own_channels, tokens_dev), F32),
            jax.ShapeDtypeStruct((tokens_dev, channels), BF),
        ),
        in_specs=[whole],
        out_specs=(whole,) * 3,
        scratch_shapes=[pltpu.VMEM((9 * channels, own_channels), BF)],
        compiler_params=params,
    )(packed)
    act = lax.all_gather(act, ("core", "zl"), axis=0, tiled=True)

    lower = lax.axis_index("zl") == 0
    pair = jnp.concatenate(
        [jnp.where(lower, embed_weight, other), jnp.where(lower, other, embed_weight)], axis=0
    )
    full_embed = lax.all_gather(pair, "core", axis=0, tiled=True)
    gain = attention_gain.astype(F32)
    embedded = dot(act, full_embed, TN).reshape(frames_dev, positions, width)
    embedded = (embedded + frame_embed.astype(F32)[:, None, :]).astype(BF)
    embedded = embedded.reshape(tokens_dev, width)
    wide = embedded.astype(F32)
    scale = lax.rsqrt(jnp.mean(wide * wide, axis=-1, keepdims=True) + EPSILON)
    normed = (wide * scale * gain).astype(BF)
    qkv = jnp.concatenate(
        [dot(normed, w).astype(BF) for w in (query_weight, key_weight, value_weight)], axis=1
    )
    embed_sum = jnp.sum(wide, axis=0, keepdims=True) * (1.0 / n_s)
    scale_row = scale.reshape(1, tokens_dev)
    back_unit = dot(embed_weight, embedded, NT) * scale_row

    vocab_dev = unembedding.shape[0]
    ratings = rating_ids.shape[0]
    first_row = lax.axis_index(everyone) * vocab_dev
    picks = (rating_ids[:, None] - first_row == jnp.arange(vocab_dev)[None, :]).astype(BF)
    rows_part = dot(picks, unembedding).astype(BF)
    groups = width // n_t
    rating_part = rows_part.reshape(ratings * groups, n_t).T
    rating_part = jnp.pad(rating_part, ((0, 0), (0, LANES - ratings * groups)))
    rating_part = jnp.pad(rating_part[:, None, :], ((0, 0), (0, slots - 1), (0, 0)))

    qkv = qkv.reshape(frames_dev, slots, n_t, 3 * inner)
    moved = jnp.concatenate(
        [qkv[f].transpose(1, 0, 2) for f in range(frames_dev)] + [rating_part], axis=2
    )
    moved = lax.all_to_all(moved, T_AXES, 0, 0, tiled=True)
    qkv = jnp.concatenate(
        [
            moved[:, :, f * 3 * inner : (f + 1) * 3 * inner].transpose(1, 0, 2)
            for f in range(frames_dev)
        ],
        axis=1,
    )
    rating_got = moved[:, 0, frames_dev * 3 * inner :]

    scaled = full_embed.astype(F32) * gain
    back = jnp.concatenate(
        [
            sum(dot(w, part, (((0,), (1,)), ((), ()))) for part in halves(scaled))
            for w in (query_weight, key_weight, value_weight)
        ],
        axis=0,
    )

    items = slots * heads
    lines = width // LANES
    first = lax.axis_size(("x",) + S_AXES)
    weights, packed = pl.pallas_call(
        functools.partial(forward_kernel, heads),
        name="attend",
        out_shape=(
            jax.ShapeDtypeStruct((items, all_frames, all_frames), F32),
            jax.ShapeDtypeStruct((first, lines + 8, LANES), F32),
        ),
        in_specs=[whole] * 4 + [pl.BlockSpec(memory_space=pl.ANY)],
        out_specs=(whole, whole),
        compiler_params=params,
    )(qkv, output_weight, embed_sum, rating_got, back)

    packed = lax.all_to_all(packed, ("x",) + S_AXES, 0, 0, tiled=True)
    size_x, size_y, size_z = (lax.axis_size(axis) for axis in ("x", "y", "zh"))
    for axis, before, joint, out_lines, out_size in (
        ("y", 1, n_s, lines + 8, size_y),
        ("zh", size_x, 1, lines + size_x * size_y, size_z),
    ):
        packed = pl.pallas_call(
            functools.partial(combine_kernel, lines, before, joint),
            name="combine_" + axis,
            out_shape=jax.ShapeDtypeStruct((out_size, out_lines, LANES), F32),
            in_specs=[whole],
            out_specs=whole,
            compiler_params=params,
        )(packed)
        packed = lax.all_to_all(packed, axis, 0, 0, tiled=True)

    expected, direct, sent = pl.pallas_call(
        functools.partial(backward_kernel, heads, float(tokens), ratings),
        name="attend_back",
        out_shape=(
            jax.ShapeDtypeStruct((8, LANES), F32),
            jax.ShapeDtypeStruct((own_channels, LANES), F32),
            jax.ShapeDtypeStruct((n_t * n_s * LINES, LANES), F32),
        ),
        in_specs=[pl.BlockSpec(memory_space=pltpu.SMEM)] + [whole] * 7,
        out_specs=(whole,) * 3,
        compiler_params=params,
    )(
        target_score,
        packed,
        final_gain.reshape(lines, LANES),
        output_weight,
        embed_weight,
        qkv,
        weights,
        back,
    )

    sent = sent.astype(BF).reshape(n_t * n_s, LINES, LANES)
    sent = lax.all_to_all(sent, everyone, 0, 0, tiled=True)
    got = jnp.sum(sent.reshape(n_t, n_s, LINES, LANES).astype(F32), axis=1)

    count = 9 * channels * own_channels // LANES
    step, window = line_window(count, n_t)
    out_lines = -(-window // 4) * 4
    sums = pl.pallas_call(
        functools.partial(stem_back_kernel, cols, count_rows, slots, frames_dev),
        name="stem_back",
        out_shape=jax.ShapeDtypeStruct((n_t * n_s * out_lines, LANES), F32),
        in_specs=[whole] * 6,
        out_specs=whole,
        scratch_shapes=[
            pltpu.VMEM((9 * channels, own_channels), F32),
            pltpu.VMEM((count, LANES), F32),
        ],
        compiler_params=params,
    )(got.reshape(n_t * LINES, LANES), back_unit, scale_row, direct, gelu_slope, patch_tokens)
    sums = sums.astype(BF).reshape(n_t * n_s, out_lines, LANES)
    sums = lax.all_to_all(sums, everyone, 0, 0, tiled=True)
    sums = jnp.sum(sums.reshape(n_t, n_s, out_lines, LANES).astype(F32), axis=0)[:, :window]
    flat = sums.reshape(n_s, -1, own_channels).transpose(1, 0, 2).reshape(-1)
    length = 9 * channels * channels // (n_t * n_s)
    start = space_index * (length - step * LANES * n_s)
    stem_gradient = lax.dynamic_slice_in_dim(flat, start, length, 0)
    return (expected[0, :1], stem_gradient)


def solution(mesh):
    shape = FACTORS[mesh.shape["tm"]] + (2, 2)
    split = Mesh(mesh.devices.reshape(shape), T_AXES + S_AXES)
    both = T_AXES + S_AXES
    in_specs = (
        P(T_AXES, S_AXES, None, None),
        P(S_AXES, None),
        P(S_AXES, None),
        P(T_AXES, None),
        P(),
        P(),
        P(None, S_AXES),
        P(None, S_AXES),
        P(None, S_AXES),
        P(S_AXES, None),
        P(both, None),
        P(),
        P(),
    )
    return jax.shard_map(
        on_device, mesh=split, in_specs=in_specs, out_specs=(P(), P(both)), check_vma=False
    )
```

```python
import functools
import math

import jax
import jax.numpy as jnp
from jax import lax
from jax.experimental import pallas as pl
from jax.experimental.pallas import tpu as pltpu
from jax.sharding import Mesh, PartitionSpec as P

HEAD = 128
LANES = 128
EPSILON = 1e-05
BF = jnp.bfloat16
F32 = jnp.float32
T_AXES = ("zh", "y", "x")
S_AXES = ("zl", "core")
FACTORS = {128: (4, 8, 4), 8: (2, 2, 2)}
NT = (((1,), (1,)), ((), ()))
TN = (((0,), (0,)), ((), ()))
VMEM_LIMIT = 40 * 1024 * 1024
LINES = 4
N_S = 4
SPACE_OF_BLOCK = (0, 2, 1, 3)


def dot(lhs, rhs, dims=(((1,), (0,)), ((), ()))):
    return lax.dot_general(lhs, rhs, dims, preferred_element_type=F32)


def thirds(row):
    first = row.astype(BF)
    rest = row - first.astype(F32)
    second = rest.astype(BF)
    third = (rest - second.astype(F32)).astype(BF)
    zero = jnp.zeros((5, row.shape[1]), F32)
    parts = [first.astype(F32), second.astype(F32), third.astype(F32), zero]
    return jnp.concatenate(parts, axis=0).astype(BF)


def halves(values):
    first = values.astype(BF)
    return first, (values - first.astype(F32)).astype(BF)


def in_window(lanes, cols, rows, row_off, col_off):
    lane = lax.broadcasted_iota(jnp.int32, (1, lanes), 1) % (rows * cols)
    row = lane // cols + row_off
    col = lane % cols + col_off
    return ((row >= 0) & (row < rows) & (col >= 0) & (col < cols)).astype(F32)


def offsets():
    return [(a, b) for a in (-1, 0, 1) for b in (-1, 0, 1)]


def stem_kernel(cols, rows, packed_ref, act_ref, slope_ref, tokens_ref, weight_ref):
    n_s = packed_ref.shape[0]
    lanes, channels = tokens_ref.shape
    own = act_ref.shape[0]
    frames = lanes // (rows * cols)
    block = lanes // (frames * n_s)
    lane_blocks = channels // LANES
    count = lane_blocks * frames * block
    half = packed_ref.shape[1] - count
    for s in range(n_s):
        for part in range(lane_blocks):
            for frame in range(frames):
                source = (part * frames + frame) * block
                target = (frame * n_s + s) * block
                tokens_ref[target : target + block, part * LANES : (part + 1) * LANES] = packed_ref[
                    s, source : source + block, :
                ]
        pairs = packed_ref[s, count:, :]
        at = 2 * s * half
        weight_ref[at : at + half, :] = pairs[:, :own]
        weight_ref[at + half : at + 2 * half, :] = pairs[:, own:]
    tokens = tokens_ref[...]
    total = jnp.zeros((own, lanes), F32)
    for tap, (row_off, col_off) in enumerate(offsets()):
        weight = weight_ref[tap * channels : (tap + 1) * channels, :]
        part = dot(weight, tokens, (((0,), (1,)), ((), ())))
        shift = row_off * cols + col_off
        if shift:
            part = pltpu.roll(part, (-shift) % lanes, 1)
        total = total + in_window(lanes, cols, rows, row_off, col_off) * part
    root = math.sqrt(2.0 / math.pi)
    square = total * total
    bent = jnp.tanh(root * (total + 0.044715 * (square * total)))
    half_up = 0.5 * (1.0 + bent)
    act_ref[...] = (total * half_up).astype(BF)
    slope_ref[...] = half_up + 0.5 * total * (1.0 - bent * bent) * (
        root * (1.0 + 3 * 0.044715 * square)
    )


def stem_back_kernel(
    cols,
    rows,
    slots,
    frames,
    got_ref,
    back_unit_ref,
    scale_ref,
    direct_ref,
    slope_ref,
    tokens_ref,
    out_ref,
    grad_ref,
    lines_ref,
    wide_ref,
):
    lanes, channels = tokens_ref.shape
    own = slope_ref.shape[0]
    depth = got_ref.shape[0] // LINES
    turned = [got_ref[pl.ds(i, depth, stride=LINES), :].T for i in range(slots + 1)]
    unit = jnp.concatenate(
        [turned[s][f * own : (f + 1) * own] for f in range(frames) for s in range(slots)], axis=1
    )
    mean = jnp.concatenate(
        [
            turned[slots][s * frames + f : s * frames + f + 1]
            for f in range(frames)
            for s in range(slots)
        ],
        axis=1,
    )
    grad_act = scale_ref[...] * (unit - mean * back_unit_ref[...]) + direct_ref[:, :1]
    grad_pre = (slope_ref[...] * grad_act).astype(BF).astype(F32)
    tokens = tokens_ref[...]
    for tap, (row_off, col_off) in enumerate(offsets()):
        moved = in_window(lanes, cols, rows, row_off, col_off) * grad_pre
        shift = row_off * cols + col_off
        if shift:
            moved = pltpu.roll(moved, shift % lanes, 1)
        part = dot(tokens, moved.astype(BF), (((0,), (1,)), ((), ())))
        grad_ref[tap * channels : (tap + 1) * channels, :] = part
    count = lines_ref.shape[0]
    lines_ref[...] = jnp.concatenate(
        [grad_ref[pl.ds(i, count, stride=2), :] for i in range(2)], axis=1
    )
    step, window = line_window(count, depth)
    out_lines = out_ref.shape[0] // (N_S * depth)
    blank = jnp.zeros((depth, LANES), F32)
    for s in range(N_S):
        for line in range(out_lines):
            value = blank
            if line < window:
                value = lines_ref[pl.ds(step * s + line, depth, stride=count // depth), :]
            wide_ref[pl.ds(s * out_lines + line, depth, stride=N_S * out_lines), :] = value
    out_ref[...] = wide_ref[...].astype(BF)


def line_window(count, depth):
    per = count // depth
    return per // N_S, -(-per // N_S)


def split_heads(block, heads):
    inner = heads * HEAD
    for head in range(heads):
        at = head * HEAD
        yield (
            head,
            block[:, at : at + HEAD],
            block[:, inner + at : inner + at + HEAD],
            block[:, 2 * inner + at : 2 * inner + at + HEAD],
        )


def as_lines(row):
    return jnp.concatenate(
        [row[:, i : i + LANES] for i in range(0, row.shape[1], LANES)], axis=0
    )


def as_row(lines):
    return jnp.concatenate([lines[i : i + 1] for i in range(lines.shape[0])], axis=1)


def pack_kernel(patches_ref, stem_ref, out_ref):
    count = patches_ref.shape[0]
    lane_blocks = patches_ref.shape[1] // LANES
    half = stem_ref.shape[0] // 2
    own = stem_ref.shape[1] // N_S
    for s in range(N_S):
        for i in range(lane_blocks):
            out_ref[s, i * count : (i + 1) * count, :] = patches_ref[:, i * LANES : (i + 1) * LANES]
        pair = [stem_ref[h * half : (h + 1) * half, s * own : (s + 1) * own] for h in range(2)]
        out_ref[s, lane_blocks * count :, :] = jnp.concatenate(pair, axis=1)


def chunk_rows(n_t, chunks, chunk, frame):
    return pl.ds(2 * chunk + frame, n_t, stride=2 * chunks)


def embed_kernel(
    n_t,
    slots,
    place_ref,
    ids_ref,
    act_ref,
    pair_ref,
    across_ref,
    frame_ref,
    gain_ref,
    query_ref,
    key_ref,
    value_ref,
    own_embed_ref,
    vocab_ref,
    moved_ref,
    embed_sum_ref,
    scale_ref,
    back_unit_ref,
    wide_ref,
):
    core = place_ref[0]
    width = frame_ref.shape[1]
    frames = frame_ref.shape[0]
    tokens = act_ref.shape[1] // frames
    inner = query_ref.shape[1]
    near = pair_ref.shape[0]
    per = 3 * inner // LANES
    chunks = slots * per + 1
    gain = gain_ref[...].astype(F32)
    here = pl.multiple_of(core * near, near)
    there = pl.multiple_of((1 - core) * near, near)
    embed_sum = jnp.zeros((1, width), F32)
    for frame in range(frames):
        at = frame * tokens
        mine = act_ref[pl.ds(here, near), at : at + tokens]
        other = act_ref[pl.ds(there, near), at : at + tokens]
        made = dot(mine, pair_ref[...], TN) + dot(other, across_ref[...], TN)
        embedded = (made + frame_ref[frame : frame + 1, :].astype(F32)).astype(BF)
        wide = embedded.astype(F32)
        embed_sum = embed_sum + jnp.sum(wide, axis=0, keepdims=True)
        scale = lax.rsqrt(jnp.mean(wide * wide, axis=1, keepdims=True) + EPSILON)
        normed = (wide * scale * gain).astype(BF)
        scale_row = jnp.broadcast_to(scale, (tokens, LANES)).T[:1]
        scale_ref[:, at : at + tokens] = scale_row
        back_unit_ref[:, at : at + tokens] = dot(own_embed_ref[...], embedded, NT) * scale_row
        for part, weight_ref in enumerate((query_ref, key_ref, value_ref)):
            made = dot(normed, weight_ref[...])
            for slot in range(slots):
                for i in range(inner // LANES):
                    chunk = slot * per + part * (inner // LANES) + i
                    wide_ref[chunk_rows(n_t, chunks, chunk, frame), :] = made[
                        slot * n_t : (slot + 1) * n_t, i * LANES : (i + 1) * LANES
                    ]
    embed_sum_ref[...] = embed_sum * (1.0 / N_S)
    vocab = vocab_ref.shape[0]
    ratings = ids_ref.shape[0]
    column = lax.broadcasted_iota(jnp.int32, (1, vocab), 1)
    picks = [(column == ids_ref[r] - place_ref[1]).astype(F32) for r in range(ratings)]
    picks.append(jnp.zeros((8 - ratings, vocab), F32))
    rows = dot(jnp.concatenate(picks, axis=0).astype(BF), vocab_ref[...])
    groups = width // n_t
    lines = [
        rows[r : r + 1, g * n_t : (g + 1) * n_t] for r in range(ratings) for g in range(groups)
    ]
    lines.append(jnp.zeros((LANES - ratings * groups, n_t), F32))
    wide_ref[chunk_rows(n_t, chunks, chunks - 1, 0), :] = jnp.concatenate(lines, axis=0).T
    wide_ref[chunk_rows(n_t, chunks, chunks - 1, 1), :] = jnp.zeros((n_t, LANES), F32)
    moved_ref[...] = wide_ref[...].astype(BF)


def attention_weights(key, query):
    scores = dot(key, query, NT) * (1.0 / math.sqrt(HEAD))
    raised = jnp.exp(scores - jnp.max(scores, axis=0, keepdims=True))
    return raised / jnp.sum(raised, axis=0, keepdims=True)


def forward_kernel(
    heads, moved_ref, out_weight_ref, embed_sum_ref, back_ref, qkv_ref, packed_ref, wide_ref
):
    del back_ref
    slots, frames = qkv_ref.shape[0], qkv_ref.shape[1]
    n_t = frames // 2
    per = 3 * heads
    chunks = slots * per + 1
    wide_ref[...] = moved_ref[...].astype(F32)
    sums = [0.0] * heads
    for slot in range(slots):
        for chunk in range(per):
            for frame in range(2):
                rows = chunk_rows(n_t, chunks, slot * per + chunk, frame)
                qkv_ref[
                    slot, frame * n_t : (frame + 1) * n_t, chunk * LANES : (chunk + 1) * LANES
                ] = wide_ref[rows, :].astype(BF)
        for head, query, key, value in split_heads(qkv_ref[slot], heads):
            weights = attention_weights(key, query)
            mixture = dot(weights.astype(BF), value, TN).astype(BF).astype(F32)
            sums[head] = sums[head] + jnp.sum(mixture, axis=0, keepdims=True)
    mixture_sum = thirds(jnp.concatenate(sums, axis=1))
    mixed = jnp.sum(dot(mixture_sum, out_weight_ref[...]), axis=0, keepdims=True)
    pooled = as_lines(embed_sum_ref[...] + mixed)
    rating = jnp.sum(wide_ref[chunk_rows(n_t, chunks, chunks - 1, 0), :], axis=0, keepdims=True)
    blank = jnp.zeros((packed_ref.shape[1] - pooled.shape[0] - 1, LANES), F32)
    packed = jnp.concatenate([pooled, rating, blank], axis=0)
    for i in range(packed_ref.shape[0]):
        packed_ref[i] = packed


def combine_kernel(lines, per, joint, in_ref, out_ref):
    size = in_ref.shape[0]
    pooled = in_ref[0, :lines]
    for i in range(1, size):
        pooled = pooled + in_ref[i, :lines]
    ratings = []
    for i in range(0, size, joint):
        rating = in_ref[i, lines : lines + per]
        for j in range(1, joint):
            rating = rating + in_ref[i + j, lines : lines + per]
        ratings.append(rating)
    parts = [pooled] + ratings
    left = out_ref.shape[1] - lines - per * len(ratings)
    if left:
        parts.append(jnp.zeros((left, LANES), F32))
    packed = jnp.concatenate(parts, axis=0)
    for i in range(out_ref.shape[0]):
        out_ref[i] = packed


def backward_kernel(
    heads,
    tokens,
    ratings,
    target_ref,
    packed_ref,
    gain_ref,
    out_weight_ref,
    own_embed_ref,
    qkv_ref,
    back_ref,
    expected_ref,
    direct_ref,
    out_ref,
    sent_ref,
):
    lines = gain_ref.shape[0]
    width = lines * LANES
    pooled = packed_ref[0, :lines]
    for i in range(1, packed_ref.shape[0]):
        pooled = pooled + packed_ref[i, :lines]
    turned = jnp.concatenate([packed_ref[i, lines:] for i in range(packed_ref.shape[0])], axis=0)
    pad = LANES - turned.shape[0]
    if pad:
        turned = jnp.concatenate([turned, jnp.zeros((pad, LANES), F32)], axis=0)
    n_t = packed_ref.shape[0] * (packed_ref.shape[1] - lines)
    turned = turned.T[:, :n_t]
    groups = width // n_t
    rows = [turned[r * groups : (r + 1) * groups] for r in range(ratings)]
    if n_t != LANES:
        rows = [as_lines(as_row(row)) for row in rows]

    def total_of(values):
        return jnp.sum(jnp.sum(values, axis=1, keepdims=True), axis=0, keepdims=True)

    pooled_raw = pooled / tokens
    inverse_rms = lax.rsqrt(total_of(pooled_raw * pooled_raw) / width + EPSILON)
    unit = pooled_raw * inverse_rms
    gain = gain_ref[...].astype(F32)
    gained_unit = unit * gain
    logits = [total_of(row * gained_unit) for row in rows]
    top = functools.reduce(jnp.maximum, logits)
    raised = [jnp.exp(logit - top) for logit in logits]
    norm = sum(raised)
    probs = [value / norm for value in raised]
    expected = sum((r + 1.0) * prob for r, prob in enumerate(probs))
    expected_ref[...] = jnp.broadcast_to(expected, expected_ref.shape)
    target = target_ref[0]
    mixed = sum(
        (prob - jnp.where(target == r + 1, 1.0, 0.0)) * rows[r] for r, prob in enumerate(probs)
    )
    gained = gain * mixed
    centre = total_of(gained * unit) / width
    cotangent = inverse_rms * (gained - unit * centre) / math.sqrt(tokens)
    parts = thirds(as_row(cotangent))
    direct = jnp.sum(dot(own_embed_ref[...], parts, NT), axis=1, keepdims=True)
    direct_ref[...] = jnp.broadcast_to(direct, direct_ref.shape)
    grad_heads = jnp.sum(dot(parts, out_weight_ref[...], NT), axis=0, keepdims=True)
    factor = 1.0 / math.sqrt(HEAD)
    slots, frames = qkv_ref.shape[0], qkv_ref.shape[1]
    depth = frames // 2
    back_upper, back_lower = halves(back_ref[...])
    own = back_ref.shape[1] // N_S
    lane = lax.broadcasted_iota(jnp.int32, (1, LANES), 1)
    means = jnp.zeros((depth, LANES), F32)
    for slot in range(slots):
        grads_q, grads_k, grads_v = [], [], []
        total = jnp.zeros((frames, 1), F32)
        for head, query, key, value in split_heads(qkv_ref[slot], heads):
            grad_mixture = grad_heads[:, head * HEAD : (head + 1) * HEAD]
            weights = attention_weights(key, query)
            wide_value = value.astype(F32)
            grad_weights = jnp.sum(wide_value * grad_mixture, axis=1, keepdims=True)
            centre = jnp.sum(weights * grad_weights, axis=0, keepdims=True)
            upper, lower = halves(weights * (grad_weights - centre) * factor)
            grad_query = dot(upper, key, TN) + dot(lower, key, TN)
            grad_key = dot(upper, query) + dot(lower, query)
            mass = jnp.sum(weights.astype(BF).astype(F32), axis=1, keepdims=True)
            grad_value = mass * grad_mixture
            total = total + jnp.sum(
                grad_query * query.astype(F32)
                + grad_key * key.astype(F32)
                + grad_value * wide_value,
                axis=1,
                keepdims=True,
            )
            grads_q.append(grad_query.astype(BF))
            grads_k.append(grad_key.astype(BF))
            grads_v.append(grad_value.astype(BF))
        grads = jnp.concatenate(grads_q + grads_k + grads_v, axis=1)
        sent = dot(grads, back_upper) + dot(grads, back_lower)
        for block in range(N_S):
            s = SPACE_OF_BLOCK[block]
            both = [
                sent[f * depth : (f + 1) * depth, block * own : (block + 1) * own]
                for f in range(2)
            ]
            sent_ref[pl.ds(s * LINES + slot, depth, stride=N_S * LINES), :] = jnp.concatenate(
                both, axis=1
            )
        for f in range(2):
            column = total[f * depth : (f + 1) * depth] / width
            means = means + jnp.where(lane == slot * 2 + f, 1.0, 0.0) * column
    blank = jnp.zeros((depth, LANES), F32)
    for s in range(N_S):
        sent_ref[pl.ds(s * LINES + slots, depth, stride=N_S * LINES), :] = means
        for line in range(slots + 1, LINES):
            sent_ref[pl.ds(s * LINES + line, depth, stride=N_S * LINES), :] = blank
    out_ref[...] = sent_ref[...].astype(BF)


def on_device(
    patches,
    stem_weight,
    embed_weight,
    frame_embed,
    attention_gain,
    final_gain,
    query_weight,
    key_weight,
    value_weight,
    output_weight,
    unembedding,
    rating_ids,
    target_score,
):
    n_t = lax.axis_size(T_AXES)
    n_s = lax.axis_size(S_AXES)
    everyone = T_AXES + S_AXES
    space_index = lax.axis_index(S_AXES)
    frames_dev, rows_dev, cols, channels = patches.shape
    own_channels = channels // n_s
    count_rows = rows_dev * n_s
    positions = count_rows * cols
    slots = positions // n_t
    width = embed_weight.shape[1]
    inner = query_weight.shape[1]
    heads = inner // HEAD
    all_frames = frames_dev * n_t
    tokens = all_frames * positions
    tokens_dev = frames_dev * positions
    assert frames_dev == 2 and slots == 2

    whole = pl.BlockSpec(memory_space=pltpu.VMEM)
    params = pltpu.CompilerParams(vmem_limit_bytes=VMEM_LIMIT)
    other = lax.ppermute(embed_weight, "zl", [(0, 1), (1, 0)])

    patch_rows = patches.reshape(-1, channels)
    stem_half = stem_weight.shape[0] // 2
    packed_rows = patch_rows.shape[0] * (channels // LANES) + stem_half
    packed = pl.pallas_call(
        pack_kernel,
        name="pack",
        out_shape=jax.ShapeDtypeStruct((n_s, packed_rows, LANES), BF),
        in_specs=[whole] * 2,
        out_specs=whole,
        compiler_params=params,
    )(patch_rows, stem_weight)
    packed = lax.all_to_all(packed, S_AXES, 0, 0, tiled=True)

    act, gelu_slope, patch_tokens = pl.pallas_call(
        functools.partial(stem_kernel, cols, count_rows),
        name="stem",
        out_shape=(
            jax.ShapeDtypeStruct((own_channels, tokens_dev), BF),
            jax.ShapeDtypeStruct((own_channels, tokens_dev), F32),
            jax.ShapeDtypeStruct((tokens_dev, channels), BF),
        ),
        in_specs=[whole],
        out_specs=(whole,) * 3,
        scratch_shapes=[pltpu.VMEM((9 * channels, own_channels), BF)],
        compiler_params=params,
    )(packed)
    act = lax.all_gather(act, ("core", "zl"), axis=0, tiled=True)

    lower = lax.axis_index("zl") == 0
    pair = jnp.concatenate(
        [jnp.where(lower, embed_weight, other), jnp.where(lower, other, embed_weight)], axis=0
    )
    across = lax.ppermute(pair, "core", [(0, 1), (1, 0)])
    core_index = lax.axis_index("core")
    vocab_dev = unembedding.shape[0]
    ratings = rating_ids.shape[0]
    place = jnp.stack([core_index, lax.axis_index(everyone) * vocab_dev]).astype(jnp.int32)

    chunks = slots * 3 * inner // LANES + 1
    scalars = pl.BlockSpec(memory_space=pltpu.SMEM)
    moved, embed_sum, scale_row, back_unit = pl.pallas_call(
        functools.partial(embed_kernel, n_t, slots),
        name="embed",
        out_shape=(
            jax.ShapeDtypeStruct((n_t * chunks * 2, LANES), BF),
            jax.ShapeDtypeStruct((1, width), F32),
            jax.ShapeDtypeStruct((1, tokens_dev), F32),
            jax.ShapeDtypeStruct((own_channels, tokens_dev), F32),
        ),
        in_specs=[scalars] * 2 + [whole] * 10,
        out_specs=(whole,) * 4,
        scratch_shapes=[pltpu.VMEM((n_t * chunks * 2, LANES), F32)],
        compiler_params=params,
    )(
        place,
        rating_ids,
        act,
        pair,
        across,
        frame_embed,
        attention_gain[None, :],
        query_weight,
        key_weight,
        value_weight,
        embed_weight,
        unembedding,
    )

    moved = moved.reshape(n_t * chunks, 2, LANES)
    moved = lax.all_to_all(moved, T_AXES, 0, 0, tiled=True)
    moved = moved.reshape(n_t * chunks * 2, LANES)

    gain = attention_gain.astype(F32)
    sides = []
    for part in (pair, across):
        upper, lower_half = halves(part.astype(F32) * gain)
        sides.append(
            jnp.concatenate(
                [
                    dot(w, upper, (((0,), (1,)), ((), ())))
                    + dot(w, lower_half, (((0,), (1,)), ((), ())))
                    for w in (query_weight, key_weight, value_weight)
                ],
                axis=0,
            )
        )
    first_core = core_index == 0
    back = jnp.concatenate(
        [jnp.where(first_core, sides[0], sides[1]), jnp.where(first_core, sides[1], sides[0])],
        axis=1,
    )

    lines = width // LANES
    first = lax.axis_size(("x",) + S_AXES)
    qkv, packed = pl.pallas_call(
        functools.partial(forward_kernel, heads),
        name="attend",
        out_shape=(
            jax.ShapeDtypeStruct((slots, all_frames, 3 * inner), BF),
            jax.ShapeDtypeStruct((first, lines + 8, LANES), F32),
        ),
        in_specs=[whole] * 3 + [pl.BlockSpec(memory_space=pl.ANY)],
        out_specs=(whole, whole),
        scratch_shapes=[pltpu.VMEM((n_t * chunks * 2, LANES), F32)],
        compiler_params=params,
    )(moved, output_weight, embed_sum, back)

    packed = lax.all_to_all(packed, ("x",) + S_AXES, 0, 0, tiled=True)
    size_x, size_y, size_z = (lax.axis_size(axis) for axis in ("x", "y", "zh"))
    for axis, before, joint, out_lines, out_size in (
        ("y", 1, n_s, lines + 8, size_y),
        ("zh", size_x, 1, lines + size_x * size_y, size_z),
    ):
        packed = pl.pallas_call(
            functools.partial(combine_kernel, lines, before, joint),
            name="combine_" + axis,
            out_shape=jax.ShapeDtypeStruct((out_size, out_lines, LANES), F32),
            in_specs=[whole],
            out_specs=whole,
            compiler_params=params,
        )(packed)
        packed = lax.all_to_all(packed, axis, 0, 0, tiled=True)

    expected, direct, sent = pl.pallas_call(
        functools.partial(backward_kernel, heads, float(tokens), ratings),
        name="attend_back",
        out_shape=(
            jax.ShapeDtypeStruct((8, LANES), F32),
            jax.ShapeDtypeStruct((own_channels, LANES), F32),
            jax.ShapeDtypeStruct((n_t * n_s * LINES, LANES), BF),
        ),
        in_specs=[scalars] + [whole] * 6,
        out_specs=(whole,) * 3,
        scratch_shapes=[pltpu.VMEM((n_t * n_s * LINES, LANES), F32)],
        compiler_params=params,
    )(
        target_score,
        packed,
        final_gain.reshape(lines, LANES),
        output_weight,
        embed_weight,
        qkv,
        back,
    )

    sent = sent.reshape(n_t * n_s, LINES, LANES)
    sent = lax.all_to_all(sent, everyone, 0, 0, tiled=True)
    got = jnp.sum(sent.reshape(n_t, n_s, LINES, LANES).astype(F32), axis=1)

    count = 9 * channels * own_channels // LANES
    step, window = line_window(count, n_t)
    out_lines = -(-window // 4) * 4
    sums = pl.pallas_call(
        functools.partial(stem_back_kernel, cols, count_rows, slots, frames_dev),
        name="stem_back",
        out_shape=jax.ShapeDtypeStruct((n_t * n_s * out_lines, LANES), BF),
        in_specs=[whole] * 6,
        out_specs=whole,
        scratch_shapes=[
            pltpu.VMEM((9 * channels, own_channels), F32),
            pltpu.VMEM((count, LANES), F32),
            pltpu.VMEM((n_t * n_s * out_lines, LANES), F32),
        ],
        compiler_params=params,
    )(got.reshape(n_t * LINES, LANES), back_unit, scale_row, direct, gelu_slope, patch_tokens)
    sums = sums.reshape(n_t * n_s, out_lines, LANES)
    sums = lax.all_to_all(sums, everyone, 0, 0, tiled=True)
    sums = jnp.sum(sums.reshape(n_t, n_s, out_lines, LANES).astype(F32), axis=0)[:, :window]
    flat = sums.reshape(n_s, -1, own_channels).transpose(1, 0, 2).reshape(-1)
    length = 9 * channels * channels // (n_t * n_s)
    start = space_index * (length - step * LANES * n_s)
    stem_gradient = lax.dynamic_slice_in_dim(flat, start, length, 0)
    return (expected[0, :1], stem_gradient)


def solution(mesh):
    shape = FACTORS[mesh.shape["tm"]] + (2, 2)
    split = Mesh(mesh.devices.reshape(shape), T_AXES + S_AXES)
    both = T_AXES + S_AXES
    in_specs = (
        P(T_AXES, S_AXES, None, None),
        P(S_AXES, None),
        P(S_AXES, None),
        P(T_AXES, None),
        P(),
        P(),
        P(None, S_AXES),
        P(None, S_AXES),
        P(None, S_AXES),
        P(S_AXES, None),
        P(both, None),
        P(),
        P(),
    )
    return jax.shard_map(
        on_device, mesh=split, in_specs=in_specs, out_specs=(P(), P(both)), check_vma=False
    )
```

```python
import functools
import math

import jax
import jax.numpy as jnp
from jax import lax
from jax.experimental import pallas as pl
from jax.experimental.pallas import tpu as pltpu
from jax.sharding import Mesh, PartitionSpec as P

HEAD = 128
LANES = 128
EPSILON = 1e-05
BF = jnp.bfloat16
F32 = jnp.float32
T_AXES = ("zh", "y", "x")
S_AXES = ("zl", "core")
FACTORS = {128: (4, 8, 4), 8: (2, 2, 2)}
NT = (((1,), (1,)), ((), ()))
TN = (((0,), (0,)), ((), ()))
VMEM_LIMIT = 40 * 1024 * 1024
LINES = 4
N_S = 4
SPACE_OF_BLOCK = (0, 2, 1, 3)


def dot(lhs, rhs, dims=(((1,), (0,)), ((), ()))):
    return lax.dot_general(lhs, rhs, dims, preferred_element_type=F32)


def thirds(row):
    first = row.astype(BF)
    rest = row - first.astype(F32)
    second = rest.astype(BF)
    third = (rest - second.astype(F32)).astype(BF)
    zero = jnp.zeros((5, row.shape[1]), F32)
    parts = [first.astype(F32), second.astype(F32), third.astype(F32), zero]
    return jnp.concatenate(parts, axis=0).astype(BF)


def halves(values):
    first = values.astype(BF)
    return first, (values - first.astype(F32)).astype(BF)


def in_window(lanes, cols, rows, row_off, col_off):
    lane = lax.broadcasted_iota(jnp.int32, (1, lanes), 1) % (rows * cols)
    row = lane // cols + row_off
    col = lane % cols + col_off
    return ((row >= 0) & (row < rows) & (col >= 0) & (col < cols)).astype(F32)


def offsets():
    return [(a, b) for a in (-1, 0, 1) for b in (-1, 0, 1)]


def stem_kernel(cols, rows, packed_ref, act_ref, slope_ref, tokens_ref, weight_ref):
    n_s = packed_ref.shape[0]
    lanes, channels = tokens_ref.shape
    own = act_ref.shape[0]
    frames = lanes // (rows * cols)
    block = lanes // (frames * n_s)
    lane_blocks = channels // LANES
    count = lane_blocks * frames * block
    half = packed_ref.shape[1] - count
    for s in range(n_s):
        for part in range(lane_blocks):
            for frame in range(frames):
                source = (part * frames + frame) * block
                target = (frame * n_s + s) * block
                tokens_ref[target : target + block, part * LANES : (part + 1) * LANES] = packed_ref[
                    s, source : source + block, :
                ]
        pairs = packed_ref[s, count:, :]
        at = 2 * s * half
        weight_ref[at : at + half, :] = pairs[:, :own]
        weight_ref[at + half : at + 2 * half, :] = pairs[:, own:]
    tokens = tokens_ref[...]
    total = jnp.zeros((own, lanes), F32)
    for tap, (row_off, col_off) in enumerate(offsets()):
        weight = weight_ref[tap * channels : (tap + 1) * channels, :]
        part = dot(weight, tokens, (((0,), (1,)), ((), ())))
        shift = row_off * cols + col_off
        if shift:
            part = pltpu.roll(part, (-shift) % lanes, 1)
        total = total + in_window(lanes, cols, rows, row_off, col_off) * part
    root = math.sqrt(2.0 / math.pi)
    square = total * total
    bent = jnp.tanh(root * (total + 0.044715 * (square * total)))
    half_up = 0.5 * (1.0 + bent)
    act_ref[...] = (total * half_up).astype(BF)
    slope_ref[...] = half_up + 0.5 * total * (1.0 - bent * bent) * (
        root * (1.0 + 3 * 0.044715 * square)
    )


def stem_back_kernel(
    cols,
    rows,
    slots,
    frames,
    got_ref,
    back_unit_ref,
    scale_ref,
    direct_ref,
    slope_ref,
    tokens_ref,
    out_ref,
    grad_ref,
    lines_ref,
    wide_ref,
    got_wide_ref,
):
    lanes, channels = tokens_ref.shape
    own = slope_ref.shape[0]
    depth = got_ref.shape[0] // LINES
    got_wide_ref[...] = got_ref[...].astype(F32)
    turned = [got_wide_ref[pl.ds(i, depth, stride=LINES), :].T for i in range(slots + 1)]
    unit = jnp.concatenate(
        [turned[s][f * own : (f + 1) * own] for f in range(frames) for s in range(slots)], axis=1
    )
    mean = jnp.concatenate(
        [
            turned[slots][s * frames + f : s * frames + f + 1]
            for f in range(frames)
            for s in range(slots)
        ],
        axis=1,
    )
    grad_act = scale_ref[...] * (unit - mean * back_unit_ref[...]) + direct_ref[:, :1]
    grad_pre = (slope_ref[...] * grad_act).astype(BF).astype(F32)
    tokens = tokens_ref[...]
    for tap, (row_off, col_off) in enumerate(offsets()):
        moved = in_window(lanes, cols, rows, row_off, col_off) * grad_pre
        shift = row_off * cols + col_off
        if shift:
            moved = pltpu.roll(moved, shift % lanes, 1)
        part = dot(tokens, moved.astype(BF), (((0,), (1,)), ((), ())))
        grad_ref[tap * channels : (tap + 1) * channels, :] = part
    count = lines_ref.shape[0]
    lines_ref[...] = jnp.concatenate(
        [grad_ref[pl.ds(i, count, stride=2), :] for i in range(2)], axis=1
    )
    per, out_lines = count // depth, out_ref.shape[0] // depth
    blank = jnp.zeros((depth, LANES), F32)
    for line in range(out_lines):
        value = blank
        if line < per:
            value = lines_ref[pl.ds(line, depth, stride=per), :]
        wide_ref[pl.ds(line, depth, stride=out_lines), :] = value
    out_ref[...] = wide_ref[...].astype(BF)


def split_heads(block, heads):
    inner = heads * HEAD
    for head in range(heads):
        at = head * HEAD
        yield (
            head,
            block[:, at : at + HEAD],
            block[:, inner + at : inner + at + HEAD],
            block[:, 2 * inner + at : 2 * inner + at + HEAD],
        )


def as_lines(row):
    return jnp.concatenate(
        [row[:, i : i + LANES] for i in range(0, row.shape[1], LANES)], axis=0
    )


def as_row(lines):
    return jnp.concatenate([lines[i : i + 1] for i in range(lines.shape[0])], axis=1)


def pack_kernel(patches_ref, stem_ref, out_ref):
    count = patches_ref.shape[0]
    lane_blocks = patches_ref.shape[1] // LANES
    half = stem_ref.shape[0] // 2
    own = stem_ref.shape[1] // N_S
    for s in range(N_S):
        for i in range(lane_blocks):
            out_ref[s, i * count : (i + 1) * count, :] = patches_ref[:, i * LANES : (i + 1) * LANES]
        pair = [stem_ref[h * half : (h + 1) * half, s * own : (s + 1) * own] for h in range(2)]
        out_ref[s, lane_blocks * count :, :] = jnp.concatenate(pair, axis=1)


def chunk_rows(n_t, chunks, chunk, frame):
    return pl.ds(2 * chunk + frame, n_t, stride=2 * chunks)


def embed_kernel(
    n_t,
    slots,
    place_ref,
    ids_ref,
    act_ref,
    pair_ref,
    across_ref,
    frame_ref,
    gain_ref,
    query_ref,
    key_ref,
    value_ref,
    own_embed_ref,
    vocab_ref,
    moved_ref,
    embed_sum_ref,
    scale_ref,
    back_unit_ref,
    wide_ref,
):
    core = place_ref[0]
    width = frame_ref.shape[1]
    frames = frame_ref.shape[0]
    tokens = act_ref.shape[1] // frames
    inner = query_ref.shape[1]
    near = pair_ref.shape[0]
    per = 3 * inner // LANES
    chunks = slots * per + 1
    gain = gain_ref[...].astype(F32)
    own = own_embed_ref.shape[0]

    def rows_of(which, at):
        starts = [pl.multiple_of((zl * 2 + which) * own, own) for zl in range(near // own)]
        return jnp.concatenate([act_ref[pl.ds(i, own), at : at + tokens] for i in starts], axis=0)

    embed_sum = jnp.zeros((1, width), F32)
    for frame in range(frames):
        at = frame * tokens
        made = dot(rows_of(core, at), pair_ref[...], TN)
        made = made + dot(rows_of(1 - core, at), across_ref[...], TN)
        embedded = (made + frame_ref[frame : frame + 1, :].astype(F32)).astype(BF)
        wide = embedded.astype(F32)
        embed_sum = embed_sum + jnp.sum(wide, axis=0, keepdims=True)
        scale = lax.rsqrt(jnp.mean(wide * wide, axis=1, keepdims=True) + EPSILON)
        normed = (wide * scale * gain).astype(BF)
        scale_row = jnp.broadcast_to(scale, (tokens, LANES)).T[:1]
        scale_ref[:, at : at + tokens] = scale_row
        back_unit_ref[:, at : at + tokens] = dot(own_embed_ref[...], embedded, NT) * scale_row
        for part, weight_ref in enumerate((query_ref, key_ref, value_ref)):
            made = dot(normed, weight_ref[...])
            for slot in range(slots):
                for i in range(inner // LANES):
                    chunk = slot * per + part * (inner // LANES) + i
                    wide_ref[chunk_rows(n_t, chunks, chunk, frame), :] = made[
                        slot * n_t : (slot + 1) * n_t, i * LANES : (i + 1) * LANES
                    ]
    embed_sum_ref[...] = embed_sum * (1.0 / N_S)
    vocab = vocab_ref.shape[0]
    ratings = ids_ref.shape[0]
    column = lax.broadcasted_iota(jnp.int32, (1, vocab), 1)
    picks = [(column == ids_ref[r] - place_ref[1]).astype(F32) for r in range(ratings)]
    picks.append(jnp.zeros((8 - ratings, vocab), F32))
    rows = dot(jnp.concatenate(picks, axis=0).astype(BF), vocab_ref[...])
    groups = width // n_t
    lines = [
        rows[r : r + 1, g * n_t : (g + 1) * n_t] for r in range(ratings) for g in range(groups)
    ]
    lines.append(jnp.zeros((LANES - ratings * groups, n_t), F32))
    wide_ref[chunk_rows(n_t, chunks, chunks - 1, 0), :] = jnp.concatenate(lines, axis=0).T
    wide_ref[chunk_rows(n_t, chunks, chunks - 1, 1), :] = jnp.zeros((n_t, LANES), F32)
    moved_ref[...] = wide_ref[...].astype(BF)


def attention_weights(key, query):
    scores = dot(key, query, NT) * (1.0 / math.sqrt(HEAD))
    raised = jnp.exp(scores - jnp.max(scores, axis=0, keepdims=True))
    return raised / jnp.sum(raised, axis=0, keepdims=True)


def forward_kernel(
    heads, moved_ref, out_weight_ref, embed_sum_ref, back_ref, qkv_ref, packed_ref, wide_ref
):
    del back_ref
    slots, frames = qkv_ref.shape[0], qkv_ref.shape[1]
    n_t = frames // 2
    per = 3 * heads
    chunks = slots * per + 1
    wide_ref[...] = moved_ref[...].astype(F32)
    sums = [0.0] * heads
    for slot in range(slots):
        for chunk in range(per):
            for frame in range(2):
                rows = chunk_rows(n_t, chunks, slot * per + chunk, frame)
                qkv_ref[
                    slot, frame * n_t : (frame + 1) * n_t, chunk * LANES : (chunk + 1) * LANES
                ] = wide_ref[rows, :].astype(BF)
        for head, query, key, value in split_heads(qkv_ref[slot], heads):
            weights = attention_weights(key, query)
            mixture = dot(weights.astype(BF), value, TN).astype(BF).astype(F32)
            sums[head] = sums[head] + jnp.sum(mixture, axis=0, keepdims=True)
    mixture_sum = thirds(jnp.concatenate(sums, axis=1))
    mixed = jnp.sum(dot(mixture_sum, out_weight_ref[...]), axis=0, keepdims=True)
    pooled = as_lines(embed_sum_ref[...] + mixed)
    rating = jnp.sum(wide_ref[chunk_rows(n_t, chunks, chunks - 1, 0), :], axis=0, keepdims=True)
    blank = jnp.zeros((packed_ref.shape[1] - pooled.shape[0] - 1, LANES), F32)
    packed = jnp.concatenate([pooled, rating, blank], axis=0)
    for i in range(packed_ref.shape[0]):
        packed_ref[i] = packed


def combine_kernel(lines, per, joint, in_ref, out_ref):
    size = in_ref.shape[0]
    pooled = in_ref[0, :lines]
    for i in range(1, size):
        pooled = pooled + in_ref[i, :lines]
    ratings = []
    for i in range(0, size, joint):
        rating = in_ref[i, lines : lines + per]
        for j in range(1, joint):
            rating = rating + in_ref[i + j, lines : lines + per]
        ratings.append(rating)
    parts = [pooled] + ratings
    left = out_ref.shape[1] - lines - per * len(ratings)
    if left:
        parts.append(jnp.zeros((left, LANES), F32))
    packed = jnp.concatenate(parts, axis=0)
    for i in range(out_ref.shape[0]):
        out_ref[i] = packed


def backward_kernel(
    heads,
    tokens,
    ratings,
    target_ref,
    packed_ref,
    gain_ref,
    out_weight_ref,
    own_embed_ref,
    qkv_ref,
    back_ref,
    expected_ref,
    direct_ref,
    sent_ref,
):
    lines = gain_ref.shape[0]
    width = lines * LANES
    pooled = packed_ref[0, :lines]
    for i in range(1, packed_ref.shape[0]):
        pooled = pooled + packed_ref[i, :lines]
    turned = jnp.concatenate([packed_ref[i, lines:] for i in range(packed_ref.shape[0])], axis=0)
    pad = LANES - turned.shape[0]
    if pad:
        turned = jnp.concatenate([turned, jnp.zeros((pad, LANES), F32)], axis=0)
    n_t = packed_ref.shape[0] * (packed_ref.shape[1] - lines)
    turned = turned.T[:, :n_t]
    groups = width // n_t
    rows = [turned[r * groups : (r + 1) * groups] for r in range(ratings)]
    if n_t != LANES:
        rows = [as_lines(as_row(row)) for row in rows]

    def total_of(values):
        return jnp.sum(jnp.sum(values, axis=1, keepdims=True), axis=0, keepdims=True)

    pooled_raw = pooled / tokens
    inverse_rms = lax.rsqrt(total_of(pooled_raw * pooled_raw) / width + EPSILON)
    unit = pooled_raw * inverse_rms
    gain = gain_ref[...].astype(F32)
    gained_unit = unit * gain
    logits = [total_of(row * gained_unit) for row in rows]
    top = functools.reduce(jnp.maximum, logits)
    raised = [jnp.exp(logit - top) for logit in logits]
    norm = sum(raised)
    probs = [value / norm for value in raised]
    expected = sum((r + 1.0) * prob for r, prob in enumerate(probs))
    expected_ref[...] = jnp.broadcast_to(expected, expected_ref.shape)
    target = target_ref[0]
    mixed = sum(
        (prob - jnp.where(target == r + 1, 1.0, 0.0)) * rows[r] for r, prob in enumerate(probs)
    )
    gained = gain * mixed
    centre = total_of(gained * unit) / width
    cotangent = inverse_rms * (gained - unit * centre) / math.sqrt(tokens)
    parts = thirds(as_row(cotangent))
    direct = jnp.sum(dot(own_embed_ref[...], parts, NT), axis=1, keepdims=True)
    direct_ref[...] = jnp.broadcast_to(direct, direct_ref.shape)
    grad_heads = jnp.sum(dot(parts, out_weight_ref[...], NT), axis=0, keepdims=True)
    factor = 1.0 / math.sqrt(HEAD)
    slots, frames = qkv_ref.shape[0], qkv_ref.shape[1]
    depth = frames // 2
    back_upper, back_lower = halves(back_ref[...])
    own = back_ref.shape[1] // N_S
    lane = lax.broadcasted_iota(jnp.int32, (1, LANES), 1)
    means = jnp.zeros((depth, LANES), F32)
    for slot in range(slots):
        grads_q, grads_k, grads_v = [], [], []
        total = jnp.zeros((frames, 1), F32)
        for head, query, key, value in split_heads(qkv_ref[slot], heads):
            grad_mixture = grad_heads[:, head * HEAD : (head + 1) * HEAD]
            weights = attention_weights(key, query)
            wide_value = value.astype(F32)
            grad_weights = jnp.sum(wide_value * grad_mixture, axis=1, keepdims=True)
            centre = jnp.sum(weights * grad_weights, axis=0, keepdims=True)
            upper, lower = halves(weights * (grad_weights - centre) * factor)
            grad_query = dot(upper, key, TN) + dot(lower, key, TN)
            grad_key = dot(upper, query) + dot(lower, query)
            mass = jnp.sum(weights.astype(BF).astype(F32), axis=1, keepdims=True)
            grad_value = mass * grad_mixture
            total = total + jnp.sum(
                grad_query * query.astype(F32)
                + grad_key * key.astype(F32)
                + grad_value * wide_value,
                axis=1,
                keepdims=True,
            )
            grads_q.append(grad_query.astype(BF))
            grads_k.append(grad_key.astype(BF))
            grads_v.append(grad_value.astype(BF))
        grads = jnp.concatenate(grads_q + grads_k + grads_v, axis=1)
        sent = dot(grads, back_upper) + dot(grads, back_lower)
        for block in range(N_S):
            s = SPACE_OF_BLOCK[block]
            both = [
                sent[f * depth : (f + 1) * depth, block * own : (block + 1) * own]
                for f in range(2)
            ]
            sent_ref[s, slot * depth : (slot + 1) * depth, :] = jnp.concatenate(
                both, axis=1
            ).astype(BF)
        for f in range(2):
            column = total[f * depth : (f + 1) * depth] / width
            means = means + jnp.where(lane == slot * 2 + f, 1.0, 0.0) * column
    turned = means.T[:16]
    if depth < LANES:
        turned = jnp.concatenate([turned, jnp.zeros((16, LANES - depth), F32)], axis=1)
    turned = turned.astype(BF)
    for s in range(N_S):
        sent_ref[s, slots * depth :, :] = turned


def gather_kernel(slots, in_ref, out_ref, wide_ref):
    depth = out_ref.shape[0] // LINES
    total = in_ref[0].astype(F32)
    for i in range(1, in_ref.shape[0]):
        total = total + in_ref[i].astype(F32)
    for slot in range(slots):
        wide_ref[pl.ds(slot, depth, stride=LINES), :] = total[slot * depth : (slot + 1) * depth]
    means = total[slots * depth :]
    blank = jnp.zeros((LANES - means.shape[0], LANES), F32)
    means = jnp.concatenate([means, blank], axis=0)
    wide_ref[pl.ds(slots, depth, stride=LINES), :] = means.T[:depth]
    wide_ref[pl.ds(slots + 1, depth, stride=LINES), :] = jnp.zeros((depth, LANES), F32)
    out_ref[...] = wide_ref[...].astype(BF)


def on_device(
    patches,
    stem_weight,
    embed_weight,
    frame_embed,
    attention_gain,
    final_gain,
    query_weight,
    key_weight,
    value_weight,
    output_weight,
    unembedding,
    rating_ids,
    target_score,
):
    n_t = lax.axis_size(T_AXES)
    n_s = lax.axis_size(S_AXES)
    everyone = T_AXES + S_AXES
    space_index = lax.axis_index(S_AXES)
    frames_dev, rows_dev, cols, channels = patches.shape
    own_channels = channels // n_s
    count_rows = rows_dev * n_s
    positions = count_rows * cols
    slots = positions // n_t
    width = embed_weight.shape[1]
    inner = query_weight.shape[1]
    heads = inner // HEAD
    all_frames = frames_dev * n_t
    tokens = all_frames * positions
    tokens_dev = frames_dev * positions
    assert frames_dev == 2 and slots == 2

    whole = pl.BlockSpec(memory_space=pltpu.VMEM)
    params = pltpu.CompilerParams(vmem_limit_bytes=VMEM_LIMIT)
    other = lax.ppermute(embed_weight, "zl", [(0, 1), (1, 0)])

    patch_rows = patches.reshape(-1, channels)
    stem_half = stem_weight.shape[0] // 2
    packed_rows = patch_rows.shape[0] * (channels // LANES) + stem_half
    packed = pl.pallas_call(
        pack_kernel,
        name="pack",
        out_shape=jax.ShapeDtypeStruct((n_s, packed_rows, LANES), BF),
        in_specs=[whole] * 2,
        out_specs=whole,
        compiler_params=params,
    )(patch_rows, stem_weight)
    packed = lax.all_to_all(packed, S_AXES, 0, 0, tiled=True)

    act, gelu_slope, patch_tokens = pl.pallas_call(
        functools.partial(stem_kernel, cols, count_rows),
        name="stem",
        out_shape=(
            jax.ShapeDtypeStruct((own_channels, tokens_dev), BF),
            jax.ShapeDtypeStruct((own_channels, tokens_dev), F32),
            jax.ShapeDtypeStruct((tokens_dev, channels), BF),
        ),
        in_specs=[whole],
        out_specs=(whole,) * 3,
        scratch_shapes=[pltpu.VMEM((9 * channels, own_channels), BF)],
        compiler_params=params,
    )(packed)
    act = lax.all_gather(act, S_AXES, axis=0, tiled=True)

    lower = lax.axis_index("zl") == 0
    pair = jnp.concatenate(
        [jnp.where(lower, embed_weight, other), jnp.where(lower, other, embed_weight)], axis=0
    )
    across = lax.ppermute(pair, "core", [(0, 1), (1, 0)])
    core_index = lax.axis_index("core")
    vocab_dev = unembedding.shape[0]
    ratings = rating_ids.shape[0]
    place = jnp.stack([core_index, lax.axis_index(everyone) * vocab_dev]).astype(jnp.int32)

    chunks = slots * 3 * inner // LANES + 1
    scalars = pl.BlockSpec(memory_space=pltpu.SMEM)
    moved, embed_sum, scale_row, back_unit = pl.pallas_call(
        functools.partial(embed_kernel, n_t, slots),
        name="embed",
        out_shape=(
            jax.ShapeDtypeStruct((n_t * chunks * 2, LANES), BF),
            jax.ShapeDtypeStruct((1, width), F32),
            jax.ShapeDtypeStruct((1, tokens_dev), F32),
            jax.ShapeDtypeStruct((own_channels, tokens_dev), F32),
        ),
        in_specs=[scalars] * 2 + [whole] * 10,
        out_specs=(whole,) * 4,
        scratch_shapes=[pltpu.VMEM((n_t * chunks * 2, LANES), F32)],
        compiler_params=params,
    )(
        place,
        rating_ids,
        act,
        pair,
        across,
        frame_embed,
        attention_gain[None, :],
        query_weight,
        key_weight,
        value_weight,
        embed_weight,
        unembedding,
    )

    moved = moved.reshape(n_t * chunks, 2, LANES)
    moved = lax.all_to_all(moved, T_AXES, 0, 0, tiled=True)
    moved = moved.reshape(n_t * chunks * 2, LANES)

    gain = attention_gain.astype(F32)
    sides = []
    for part in (pair, across):
        upper, lower_half = halves(part.astype(F32) * gain)
        sides.append(
            jnp.concatenate(
                [
                    dot(w, upper, (((0,), (1,)), ((), ())))
                    + dot(w, lower_half, (((0,), (1,)), ((), ())))
                    for w in (query_weight, key_weight, value_weight)
                ],
                axis=0,
            )
        )
    first_core = core_index == 0
    back = jnp.concatenate(
        [jnp.where(first_core, sides[0], sides[1]), jnp.where(first_core, sides[1], sides[0])],
        axis=1,
    )

    lines = width // LANES
    first = lax.axis_size(("x",) + S_AXES)
    qkv, packed = pl.pallas_call(
        functools.partial(forward_kernel, heads),
        name="attend",
        out_shape=(
            jax.ShapeDtypeStruct((slots, all_frames, 3 * inner), BF),
            jax.ShapeDtypeStruct((first, lines + 8, LANES), F32),
        ),
        in_specs=[whole] * 3 + [pl.BlockSpec(memory_space=pl.ANY)],
        out_specs=(whole, whole),
        scratch_shapes=[pltpu.VMEM((n_t * chunks * 2, LANES), F32)],
        compiler_params=params,
    )(moved, output_weight, embed_sum, back)

    packed = lax.all_to_all(packed, ("x",) + S_AXES, 0, 0, tiled=True)
    size_x, size_y, size_z = (lax.axis_size(axis) for axis in ("x", "y", "zh"))
    for axis, before, joint, out_lines, out_size in (
        ("y", 1, n_s, lines + 8, size_y),
        ("zh", size_x, 1, lines + size_x * size_y, size_z),
    ):
        packed = pl.pallas_call(
            functools.partial(combine_kernel, lines, before, joint),
            name="combine_" + axis,
            out_shape=jax.ShapeDtypeStruct((out_size, out_lines, LANES), F32),
            in_specs=[whole],
            out_specs=whole,
            compiler_params=params,
        )(packed)
        packed = lax.all_to_all(packed, axis, 0, 0, tiled=True)

    expected, direct, sent = pl.pallas_call(
        functools.partial(backward_kernel, heads, float(tokens), ratings),
        name="attend_back",
        out_shape=(
            jax.ShapeDtypeStruct((8, LANES), F32),
            jax.ShapeDtypeStruct((own_channels, LANES), F32),
            jax.ShapeDtypeStruct((n_s, slots * n_t + 16, LANES), BF),
        ),
        in_specs=[scalars] + [whole] * 6,
        out_specs=(whole,) * 3,
        compiler_params=params,
    )(
        target_score,
        packed,
        final_gain.reshape(lines, LANES),
        output_weight,
        embed_weight,
        qkv,
        back,
    )

    sent = lax.all_to_all(sent, S_AXES, 0, 0, tiled=True)
    sent = pl.pallas_call(
        functools.partial(gather_kernel, slots),
        name="gather",
        out_shape=jax.ShapeDtypeStruct((n_t * LINES, LANES), BF),
        in_specs=[whole],
        out_specs=whole,
        scratch_shapes=[pltpu.VMEM((n_t * LINES, LANES), F32)],
        compiler_params=params,
    )(sent)
    sent = lax.all_to_all(
        sent.reshape(n_t * LINES // 2, 2, LANES), T_AXES, 0, 0, tiled=True
    ).reshape(n_t * LINES, LANES)

    count = 9 * channels * own_channels // LANES
    per = count // n_t
    out_lines = per + per % 2
    sums = pl.pallas_call(
        functools.partial(stem_back_kernel, cols, count_rows, slots, frames_dev),
        name="stem_back",
        out_shape=jax.ShapeDtypeStruct((n_t * out_lines, LANES), BF),
        in_specs=[whole] * 6,
        out_specs=whole,
        scratch_shapes=[
            pltpu.VMEM((9 * channels, own_channels), F32),
            pltpu.VMEM((count, LANES), F32),
            pltpu.VMEM((n_t * out_lines, LANES), F32),
            pltpu.VMEM((n_t * LINES, LANES), F32),
        ],
        compiler_params=params,
    )(sent, back_unit, scale_row, direct, gelu_slope, patch_tokens)
    sums = sums.reshape(n_t * out_lines // 2, 2, LANES)
    sums = lax.all_to_all(sums, T_AXES, 0, 0, tiled=True)
    sums = jnp.sum(sums.reshape(n_t, out_lines // 2, 2, LANES).astype(F32), axis=0)
    sums = lax.all_gather(sums, S_AXES, axis=0, tiled=False).reshape(n_s, out_lines, LANES)
    flat = sums[:, :per].reshape(n_s, -1, own_channels).transpose(1, 0, 2).reshape(-1)
    length = flat.shape[0] // n_s
    stem_gradient = lax.dynamic_slice_in_dim(flat, space_index * length, length, 0)
    return (expected[0, :1], stem_gradient)


def solution(mesh):
    shape = FACTORS[mesh.shape["tm"]] + (2, 2)
    split = Mesh(mesh.devices.reshape(shape), T_AXES + S_AXES)
    both = T_AXES + S_AXES
    in_specs = (
        P(T_AXES, S_AXES, None, None),
        P(S_AXES, None),
        P(S_AXES, None),
        P(T_AXES, None),
        P(),
        P(),
        P(None, S_AXES),
        P(None, S_AXES),
        P(None, S_AXES),
        P(S_AXES, None),
        P(both, None),
        P(),
        P(),
    )
    return jax.shard_map(
        on_device, mesh=split, in_specs=in_specs, out_specs=(P(), P(both)), check_vma=False
    )
```

```python
import functools
import math

import jax
import jax.numpy as jnp
from jax import lax
from jax.experimental import pallas as pl
from jax.experimental.pallas import tpu as pltpu
from jax.sharding import Mesh, PartitionSpec as P

HEAD = 128
LANES = 128
EPSILON = 1e-05
BF = jnp.bfloat16
F32 = jnp.float32
T_AXES = ("zh", "y", "x")
S_AXES = ("zl", "core")
FACTORS = {128: (4, 8, 4), 8: (2, 2, 2)}
NT = (((1,), (1,)), ((), ()))
TN = (((0,), (0,)), ((), ()))
VMEM_LIMIT = 40 * 1024 * 1024
LINES = 4
FAR = pltpu.HBM
N_S = 4
SPACE_OF_BLOCK = (0, 2, 1, 3)


def dot(lhs, rhs, dims=(((1,), (0,)), ((), ()))):
    return lax.dot_general(lhs, rhs, dims, preferred_element_type=F32)


def kept(array):
    return pltpu.with_memory_space_constraint(array, FAR)


def thirds(row):
    first = row.astype(BF)
    rest = row - first.astype(F32)
    second = rest.astype(BF)
    third = (rest - second.astype(F32)).astype(BF)
    zero = jnp.zeros((5, row.shape[1]), F32)
    parts = [first.astype(F32), second.astype(F32), third.astype(F32), zero]
    return jnp.concatenate(parts, axis=0).astype(BF)


def halves(values):
    first = values.astype(BF)
    return first, (values - first.astype(F32)).astype(BF)


def in_window(lanes, cols, rows, row_off, col_off):
    lane = lax.broadcasted_iota(jnp.int32, (1, lanes), 1) % (rows * cols)
    row = lane // cols + row_off
    col = lane % cols + col_off
    return ((row >= 0) & (row < rows) & (col >= 0) & (col < cols)).astype(F32)


def offsets():
    return [(a, b) for a in (-1, 0, 1) for b in (-1, 0, 1)]


def stem_kernel(
    cols,
    rows,
    packed_ref,
    act_ref,
    slope_far,
    tokens_far,
    slope_ref,
    tokens_ref,
    weight_ref,
    done,
):
    n_s = packed_ref.shape[0]
    lanes, channels = tokens_ref.shape
    own = act_ref.shape[0]
    frames = lanes // (rows * cols)
    block = lanes // (frames * n_s)
    lane_blocks = channels // LANES
    count = lane_blocks * frames * block
    half = packed_ref.shape[1] - count
    for s in range(n_s):
        for part in range(lane_blocks):
            for frame in range(frames):
                source = (part * frames + frame) * block
                target = (frame * n_s + s) * block
                tokens_ref[target : target + block, part * LANES : (part + 1) * LANES] = packed_ref[
                    s, source : source + block, :
                ]
        pairs = packed_ref[s, count:, :]
        at = 2 * s * half
        weight_ref[at : at + half, :] = pairs[:, :own]
        weight_ref[at + half : at + 2 * half, :] = pairs[:, own:]
    tokens_store = pltpu.make_async_copy(tokens_ref, tokens_far, done.at[0])
    tokens_store.start()
    tokens = tokens_ref[...]
    total = jnp.zeros((own, lanes), F32)
    for tap, (row_off, col_off) in enumerate(offsets()):
        weight = weight_ref[tap * channels : (tap + 1) * channels, :]
        part = dot(weight, tokens, (((0,), (1,)), ((), ())))
        shift = row_off * cols + col_off
        if shift:
            part = pltpu.roll(part, (-shift) % lanes, 1)
        total = total + in_window(lanes, cols, rows, row_off, col_off) * part
    root = math.sqrt(2.0 / math.pi)
    square = total * total
    bent = jnp.tanh(root * (total + 0.044715 * (square * total)))
    half_up = 0.5 * (1.0 + bent)
    slope_ref[...] = half_up + 0.5 * total * (1.0 - bent * bent) * (
        root * (1.0 + 3 * 0.044715 * square)
    )
    slope_store = pltpu.make_async_copy(slope_ref, slope_far, done.at[1])
    slope_store.start()
    act_ref[...] = (total * half_up).astype(BF)
    tokens_store.wait()
    slope_store.wait()


def stem_back_kernel(
    cols,
    rows,
    slots,
    frames,
    got_ref,
    back_unit_ref,
    scale_ref,
    direct_ref,
    slope_ref,
    tokens_ref,
    out_ref,
    grad_ref,
    lines_ref,
    wide_ref,
    got_wide_ref,
):
    lanes, channels = tokens_ref.shape
    own = slope_ref.shape[0]
    depth = got_ref.shape[0] // LINES
    got_wide_ref[...] = got_ref[...].astype(F32)
    turned = [got_wide_ref[pl.ds(i, depth, stride=LINES), :].T for i in range(slots + 1)]
    unit = jnp.concatenate(
        [turned[s][f * own : (f + 1) * own] for f in range(frames) for s in range(slots)], axis=1
    )
    mean = jnp.concatenate(
        [
            turned[slots][s * frames + f : s * frames + f + 1]
            for f in range(frames)
            for s in range(slots)
        ],
        axis=1,
    )
    grad_act = scale_ref[...] * (unit - mean * back_unit_ref[...]) + direct_ref[:, :1]
    grad_pre = (slope_ref[...] * grad_act).astype(BF).astype(F32)
    tokens = tokens_ref[...]
    for tap, (row_off, col_off) in enumerate(offsets()):
        moved = in_window(lanes, cols, rows, row_off, col_off) * grad_pre
        shift = row_off * cols + col_off
        if shift:
            moved = pltpu.roll(moved, shift % lanes, 1)
        part = dot(tokens, moved.astype(BF), (((0,), (1,)), ((), ())))
        grad_ref[tap * channels : (tap + 1) * channels, :] = part
    count = lines_ref.shape[0]
    lines_ref[...] = jnp.concatenate(
        [grad_ref[pl.ds(i, count, stride=2), :] for i in range(2)], axis=1
    )
    per, out_lines = count // depth, out_ref.shape[0] // depth
    blank = jnp.zeros((depth, LANES), F32)
    for line in range(out_lines):
        value = blank
        if line < per:
            value = lines_ref[pl.ds(line, depth, stride=per), :]
        wide_ref[pl.ds(line, depth, stride=out_lines), :] = value
    out_ref[...] = wide_ref[...].astype(BF)


def split_heads(block, heads):
    inner = heads * HEAD
    for head in range(heads):
        at = head * HEAD
        yield (
            head,
            block[:, at : at + HEAD],
            block[:, inner + at : inner + at + HEAD],
            block[:, 2 * inner + at : 2 * inner + at + HEAD],
        )


def as_lines(row):
    return jnp.concatenate(
        [row[:, i : i + LANES] for i in range(0, row.shape[1], LANES)], axis=0
    )


def as_row(lines):
    return jnp.concatenate([lines[i : i + 1] for i in range(lines.shape[0])], axis=1)


def pack_kernel(patches_far, stem_far, out_ref, patches_ref, stem_ref, done):
    fetches = [
        pltpu.make_async_copy(patches_far, patches_ref, done.at[0]),
        pltpu.make_async_copy(stem_far, stem_ref, done.at[1]),
    ]
    for fetch in fetches:
        fetch.start()
    for fetch in fetches:
        fetch.wait()
    count = patches_ref.shape[0]
    lane_blocks = patches_ref.shape[1] // LANES
    half = stem_ref.shape[0] // 2
    own = stem_ref.shape[1] // N_S
    for s in range(N_S):
        for i in range(lane_blocks):
            out_ref[s, i * count : (i + 1) * count, :] = patches_ref[:, i * LANES : (i + 1) * LANES]
        pair = [stem_ref[h * half : (h + 1) * half, s * own : (s + 1) * own] for h in range(2)]
        out_ref[s, lane_blocks * count :, :] = jnp.concatenate(pair, axis=1)


def chunk_rows(n_t, chunks, chunk, frame):
    return pl.ds(2 * chunk + frame, n_t, stride=2 * chunks)


def embed_kernel(
    n_t,
    slots,
    place_ref,
    ids_ref,
    act_ref,
    pair_ref,
    across_ref,
    frame_ref,
    gain_ref,
    query_far,
    key_far,
    value_far,
    own_embed_ref,
    vocab_ref,
    moved_ref,
    embed_sum_ref,
    scale_ref,
    back_unit_far,
    wide_ref,
    query_ref,
    key_ref,
    value_ref,
    back_unit_ref,
    done,
):
    fetches = [
        pltpu.make_async_copy(source, target, done.at[i])
        for i, (source, target) in enumerate(
            ((query_far, query_ref), (key_far, key_ref), (value_far, value_ref))
        )
    ]
    for fetch in fetches:
        fetch.start()
    core = place_ref[0]
    width = frame_ref.shape[1]
    frames = frame_ref.shape[0]
    tokens = act_ref.shape[1] // frames
    inner = query_ref.shape[1]
    near = pair_ref.shape[0]
    per = 3 * inner // LANES
    chunks = slots * per + 1
    gain = gain_ref[...].astype(F32)
    own = own_embed_ref.shape[0]

    def rows_of(which, at):
        starts = [pl.multiple_of((zl * 2 + which) * own, own) for zl in range(near // own)]
        return jnp.concatenate([act_ref[pl.ds(i, own), at : at + tokens] for i in starts], axis=0)

    embed_sum = jnp.zeros((1, width), F32)
    for frame in range(frames):
        at = frame * tokens
        made = dot(rows_of(core, at), pair_ref[...], TN)
        made = made + dot(rows_of(1 - core, at), across_ref[...], TN)
        embedded = (made + frame_ref[frame : frame + 1, :].astype(F32)).astype(BF)
        wide = embedded.astype(F32)
        embed_sum = embed_sum + jnp.sum(wide, axis=0, keepdims=True)
        scale = lax.rsqrt(jnp.mean(wide * wide, axis=1, keepdims=True) + EPSILON)
        normed = (wide * scale * gain).astype(BF)
        scale_row = jnp.broadcast_to(scale, (tokens, LANES)).T[:1]
        scale_ref[:, at : at + tokens] = scale_row
        back_unit_ref[:, at : at + tokens] = dot(own_embed_ref[...], embedded, NT) * scale_row
        for part, weight_ref in enumerate((query_ref, key_ref, value_ref)):
            if frame == 0:
                fetches[part].wait()
            made = dot(normed, weight_ref[...])
            for slot in range(slots):
                for i in range(inner // LANES):
                    chunk = slot * per + part * (inner // LANES) + i
                    wide_ref[chunk_rows(n_t, chunks, chunk, frame), :] = made[
                        slot * n_t : (slot + 1) * n_t, i * LANES : (i + 1) * LANES
                    ]
    store = pltpu.make_async_copy(back_unit_ref, back_unit_far, done.at[3])
    store.start()
    embed_sum_ref[...] = embed_sum * (1.0 / N_S)
    vocab = vocab_ref.shape[0]
    ratings = ids_ref.shape[0]
    column = lax.broadcasted_iota(jnp.int32, (1, vocab), 1)
    picks = [(column == ids_ref[r] - place_ref[1]).astype(F32) for r in range(ratings)]
    picks.append(jnp.zeros((8 - ratings, vocab), F32))
    rows = dot(jnp.concatenate(picks, axis=0).astype(BF), vocab_ref[...])
    groups = width // n_t
    lines = [
        rows[r : r + 1, g * n_t : (g + 1) * n_t] for r in range(ratings) for g in range(groups)
    ]
    lines.append(jnp.zeros((LANES - ratings * groups, n_t), F32))
    wide_ref[chunk_rows(n_t, chunks, chunks - 1, 0), :] = jnp.concatenate(lines, axis=0).T
    wide_ref[chunk_rows(n_t, chunks, chunks - 1, 1), :] = jnp.zeros((n_t, LANES), F32)
    moved_ref[...] = wide_ref[...].astype(BF)
    store.wait()


def attention_weights(key, query):
    scores = dot(key, query, NT) * (1.0 / math.sqrt(HEAD))
    raised = jnp.exp(scores - jnp.max(scores, axis=0, keepdims=True))
    return raised / jnp.sum(raised, axis=0, keepdims=True)


def forward_kernel(
    heads,
    moved_ref,
    out_weight_ref,
    embed_sum_ref,
    back_ref,
    qkv_far,
    packed_ref,
    wide_ref,
    qkv_ref,
    done,
):
    del back_ref
    stores = []
    slots, frames = qkv_ref.shape[0], qkv_ref.shape[1]
    n_t = frames // 2
    per = 3 * heads
    chunks = slots * per + 1
    wide_ref[...] = moved_ref[...].astype(F32)
    sums = [0.0] * heads
    for slot in range(slots):
        for chunk in range(per):
            for frame in range(2):
                rows = chunk_rows(n_t, chunks, slot * per + chunk, frame)
                qkv_ref[
                    slot, frame * n_t : (frame + 1) * n_t, chunk * LANES : (chunk + 1) * LANES
                ] = wide_ref[rows, :].astype(BF)
        store = pltpu.make_async_copy(qkv_ref.at[slot], qkv_far.at[slot], done.at[slot])
        store.start()
        stores.append(store)
        for head, query, key, value in split_heads(qkv_ref[slot], heads):
            weights = attention_weights(key, query)
            mixture = dot(weights.astype(BF), value, TN).astype(BF).astype(F32)
            sums[head] = sums[head] + jnp.sum(mixture, axis=0, keepdims=True)
    mixture_sum = thirds(jnp.concatenate(sums, axis=1))
    mixed = jnp.sum(dot(mixture_sum, out_weight_ref[...]), axis=0, keepdims=True)
    pooled = as_lines(embed_sum_ref[...] + mixed)
    rating = jnp.sum(wide_ref[chunk_rows(n_t, chunks, chunks - 1, 0), :], axis=0, keepdims=True)
    blank = jnp.zeros((packed_ref.shape[1] - pooled.shape[0] - 1, LANES), F32)
    packed = jnp.concatenate([pooled, rating, blank], axis=0)
    for i in range(packed_ref.shape[0]):
        packed_ref[i] = packed
    for store in stores:
        store.wait()


def combine_kernel(lines, per, joint, in_ref, out_ref):
    size = in_ref.shape[0]
    pooled = in_ref[0, :lines]
    for i in range(1, size):
        pooled = pooled + in_ref[i, :lines]
    ratings = []
    for i in range(0, size, joint):
        rating = in_ref[i, lines : lines + per]
        for j in range(1, joint):
            rating = rating + in_ref[i + j, lines : lines + per]
        ratings.append(rating)
    parts = [pooled] + ratings
    left = out_ref.shape[1] - lines - per * len(ratings)
    if left:
        parts.append(jnp.zeros((left, LANES), F32))
    packed = jnp.concatenate(parts, axis=0)
    for i in range(out_ref.shape[0]):
        out_ref[i] = packed


def backward_kernel(
    heads,
    tokens,
    ratings,
    target_ref,
    packed_ref,
    gain_ref,
    out_weight_ref,
    own_embed_ref,
    qkv_ref,
    back_ref,
    expected_ref,
    direct_ref,
    sent_ref,
):
    lines = gain_ref.shape[0]
    width = lines * LANES
    pooled = packed_ref[0, :lines]
    for i in range(1, packed_ref.shape[0]):
        pooled = pooled + packed_ref[i, :lines]
    turned = jnp.concatenate([packed_ref[i, lines:] for i in range(packed_ref.shape[0])], axis=0)
    pad = LANES - turned.shape[0]
    if pad:
        turned = jnp.concatenate([turned, jnp.zeros((pad, LANES), F32)], axis=0)
    n_t = packed_ref.shape[0] * (packed_ref.shape[1] - lines)
    turned = turned.T[:, :n_t]
    groups = width // n_t
    rows = [turned[r * groups : (r + 1) * groups] for r in range(ratings)]
    if n_t != LANES:
        rows = [as_lines(as_row(row)) for row in rows]

    def total_of(values):
        return jnp.sum(jnp.sum(values, axis=1, keepdims=True), axis=0, keepdims=True)

    pooled_raw = pooled / tokens
    inverse_rms = lax.rsqrt(total_of(pooled_raw * pooled_raw) / width + EPSILON)
    unit = pooled_raw * inverse_rms
    gain = gain_ref[...].astype(F32)
    gained_unit = unit * gain
    logits = [total_of(row * gained_unit) for row in rows]
    top = functools.reduce(jnp.maximum, logits)
    raised = [jnp.exp(logit - top) for logit in logits]
    norm = sum(raised)
    probs = [value / norm for value in raised]
    expected = sum((r + 1.0) * prob for r, prob in enumerate(probs))
    expected_ref[...] = jnp.broadcast_to(expected, expected_ref.shape)
    target = target_ref[0]
    mixed = sum(
        (prob - jnp.where(target == r + 1, 1.0, 0.0)) * rows[r] for r, prob in enumerate(probs)
    )
    gained = gain * mixed
    centre = total_of(gained * unit) / width
    cotangent = inverse_rms * (gained - unit * centre) / math.sqrt(tokens)
    parts = thirds(as_row(cotangent))
    direct = jnp.sum(dot(own_embed_ref[...], parts, NT), axis=1, keepdims=True)
    direct_ref[...] = jnp.broadcast_to(direct, direct_ref.shape)
    grad_heads = jnp.sum(dot(parts, out_weight_ref[...], NT), axis=0, keepdims=True)
    factor = 1.0 / math.sqrt(HEAD)
    slots, frames = qkv_ref.shape[0], qkv_ref.shape[1]
    depth = frames // 2
    back_upper, back_lower = halves(back_ref[...])
    own = back_ref.shape[1] // N_S
    lane = lax.broadcasted_iota(jnp.int32, (1, LANES), 1)
    means = jnp.zeros((depth, LANES), F32)
    for slot in range(slots):
        grads_q, grads_k, grads_v = [], [], []
        total = jnp.zeros((frames, 1), F32)
        for head, query, key, value in split_heads(qkv_ref[slot], heads):
            grad_mixture = grad_heads[:, head * HEAD : (head + 1) * HEAD]
            weights = attention_weights(key, query)
            wide_value = value.astype(F32)
            grad_weights = jnp.sum(wide_value * grad_mixture, axis=1, keepdims=True)
            centre = jnp.sum(weights * grad_weights, axis=0, keepdims=True)
            upper, lower = halves(weights * (grad_weights - centre) * factor)
            grad_query = dot(upper, key, TN) + dot(lower, key, TN)
            grad_key = dot(upper, query) + dot(lower, query)
            mass = jnp.sum(weights.astype(BF).astype(F32), axis=1, keepdims=True)
            grad_value = mass * grad_mixture
            total = total + jnp.sum(
                grad_query * query.astype(F32)
                + grad_key * key.astype(F32)
                + grad_value * wide_value,
                axis=1,
                keepdims=True,
            )
            grads_q.append(grad_query.astype(BF))
            grads_k.append(grad_key.astype(BF))
            grads_v.append(grad_value.astype(BF))
        grads = jnp.concatenate(grads_q + grads_k + grads_v, axis=1)
        sent = dot(grads, back_upper) + dot(grads, back_lower)
        for block in range(N_S):
            s = SPACE_OF_BLOCK[block]
            both = [
                sent[f * depth : (f + 1) * depth, block * own : (block + 1) * own]
                for f in range(2)
            ]
            sent_ref[s, slot * depth : (slot + 1) * depth, :] = jnp.concatenate(
                both, axis=1
            ).astype(BF)
        for f in range(2):
            column = total[f * depth : (f + 1) * depth] / width
            means = means + jnp.where(lane == slot * 2 + f, 1.0, 0.0) * column
    turned = means.T[:16]
    if depth < LANES:
        turned = jnp.concatenate([turned, jnp.zeros((16, LANES - depth), F32)], axis=1)
    turned = turned.astype(BF)
    for s in range(N_S):
        sent_ref[s, slots * depth :, :] = turned


def gather_kernel(slots, in_ref, out_ref, wide_ref):
    depth = out_ref.shape[0] // LINES
    total = in_ref[0].astype(F32)
    for i in range(1, in_ref.shape[0]):
        total = total + in_ref[i].astype(F32)
    for slot in range(slots):
        wide_ref[pl.ds(slot, depth, stride=LINES), :] = total[slot * depth : (slot + 1) * depth]
    means = total[slots * depth :]
    blank = jnp.zeros((LANES - means.shape[0], LANES), F32)
    means = jnp.concatenate([means, blank], axis=0)
    wide_ref[pl.ds(slots, depth, stride=LINES), :] = means.T[:depth]
    wide_ref[pl.ds(slots + 1, depth, stride=LINES), :] = jnp.zeros((depth, LANES), F32)
    out_ref[...] = wide_ref[...].astype(BF)


def on_device(
    patches,
    stem_weight,
    embed_weight,
    frame_embed,
    attention_gain,
    final_gain,
    query_weight,
    key_weight,
    value_weight,
    output_weight,
    unembedding,
    rating_ids,
    target_score,
):
    n_t = lax.axis_size(T_AXES)
    n_s = lax.axis_size(S_AXES)
    everyone = T_AXES + S_AXES
    space_index = lax.axis_index(S_AXES)
    frames_dev, rows_dev, cols, channels = patches.shape
    own_channels = channels // n_s
    count_rows = rows_dev * n_s
    positions = count_rows * cols
    slots = positions // n_t
    width = embed_weight.shape[1]
    inner = query_weight.shape[1]
    heads = inner // HEAD
    all_frames = frames_dev * n_t
    tokens = all_frames * positions
    tokens_dev = frames_dev * positions
    assert frames_dev == 2 and slots == 2

    whole = pl.BlockSpec(memory_space=pltpu.VMEM)
    far = pl.BlockSpec(memory_space=FAR)
    params = pltpu.CompilerParams(vmem_limit_bytes=VMEM_LIMIT)
    other = lax.ppermute(embed_weight, "zl", [(0, 1), (1, 0)])

    patch_rows = patches.reshape(-1, channels)
    stem_half = stem_weight.shape[0] // 2
    packed_rows = patch_rows.shape[0] * (channels // LANES) + stem_half
    packed = pl.pallas_call(
        pack_kernel,
        name="pack",
        out_shape=jax.ShapeDtypeStruct((n_s, packed_rows, LANES), BF),
        in_specs=[far] * 2,
        out_specs=whole,
        scratch_shapes=[
            pltpu.VMEM(patch_rows.shape, BF),
            pltpu.VMEM(stem_weight.shape, BF),
            pltpu.SemaphoreType.DMA((2,)),
        ],
        compiler_params=params,
    )(kept(patch_rows), kept(stem_weight))
    packed = lax.all_to_all(packed, S_AXES, 0, 0, tiled=True)

    act, gelu_slope, patch_tokens = pl.pallas_call(
        functools.partial(stem_kernel, cols, count_rows),
        name="stem",
        out_shape=(
            jax.ShapeDtypeStruct((own_channels, tokens_dev), BF),
            pltpu.HBM((own_channels, tokens_dev), F32),
            pltpu.HBM((tokens_dev, channels), BF),
        ),
        in_specs=[whole],
        out_specs=(whole, far, far),
        scratch_shapes=[
            pltpu.VMEM((own_channels, tokens_dev), F32),
            pltpu.VMEM((tokens_dev, channels), BF),
            pltpu.VMEM((9 * channels, own_channels), BF),
            pltpu.SemaphoreType.DMA((2,)),
        ],
        compiler_params=params,
    )(packed)
    act = lax.all_gather(act, S_AXES, axis=0, tiled=True)

    lower = lax.axis_index("zl") == 0
    pair = jnp.concatenate(
        [jnp.where(lower, embed_weight, other), jnp.where(lower, other, embed_weight)], axis=0
    )
    across = lax.ppermute(pair, "core", [(0, 1), (1, 0)])
    core_index = lax.axis_index("core")
    vocab_dev = unembedding.shape[0]
    ratings = rating_ids.shape[0]
    place = jnp.stack([core_index, lax.axis_index(everyone) * vocab_dev]).astype(jnp.int32)

    chunks = slots * 3 * inner // LANES + 1
    scalars = pl.BlockSpec(memory_space=pltpu.SMEM)
    moved, embed_sum, scale_row, back_unit = pl.pallas_call(
        functools.partial(embed_kernel, n_t, slots),
        name="embed",
        out_shape=(
            jax.ShapeDtypeStruct((n_t * chunks * 2, LANES), BF),
            jax.ShapeDtypeStruct((1, width), F32),
            jax.ShapeDtypeStruct((1, tokens_dev), F32),
            pltpu.HBM((own_channels, tokens_dev), F32),
        ),
        in_specs=[scalars] * 2 + [whole] * 5 + [far] * 3 + [whole] * 2,
        out_specs=(whole,) * 3 + (far,),
        scratch_shapes=[pltpu.VMEM((n_t * chunks * 2, LANES), F32)]
        + [pltpu.VMEM((width, inner), BF)] * 3
        + [pltpu.VMEM((own_channels, tokens_dev), F32), pltpu.SemaphoreType.DMA((4,))],
        compiler_params=params,
    )(
        place,
        rating_ids,
        act,
        pair,
        across,
        frame_embed,
        attention_gain[None, :],
        kept(query_weight),
        kept(key_weight),
        kept(value_weight),
        embed_weight,
        unembedding,
    )

    moved = moved.reshape(n_t * chunks, 2, LANES)
    moved = lax.all_to_all(moved, T_AXES, 0, 0, tiled=True)
    moved = moved.reshape(n_t * chunks * 2, LANES)

    gain = attention_gain.astype(F32)
    sides = []
    for part in (pair, across):
        upper, lower_half = halves(part.astype(F32) * gain)
        sides.append(
            jnp.concatenate(
                [
                    dot(w, upper, (((0,), (1,)), ((), ())))
                    + dot(w, lower_half, (((0,), (1,)), ((), ())))
                    for w in (query_weight, key_weight, value_weight)
                ],
                axis=0,
            )
        )
    first_core = core_index == 0
    back = jnp.concatenate(
        [jnp.where(first_core, sides[0], sides[1]), jnp.where(first_core, sides[1], sides[0])],
        axis=1,
    )

    lines = width // LANES
    first = lax.axis_size(("x",) + S_AXES)
    qkv, packed = pl.pallas_call(
        functools.partial(forward_kernel, heads),
        name="attend",
        out_shape=(
            pltpu.HBM((slots, all_frames, 3 * inner), BF),
            jax.ShapeDtypeStruct((first, lines + 8, LANES), F32),
        ),
        in_specs=[whole] * 3 + [pl.BlockSpec(memory_space=pl.ANY)],
        out_specs=(far, whole),
        scratch_shapes=[
            pltpu.VMEM((n_t * chunks * 2, LANES), F32),
            pltpu.VMEM((slots, all_frames, 3 * inner), BF),
            pltpu.SemaphoreType.DMA((slots,)),
        ],
        compiler_params=params,
    )(moved, output_weight, embed_sum, back)

    packed = lax.all_to_all(packed, ("x",) + S_AXES, 0, 0, tiled=True)
    size_x, size_y, size_z = (lax.axis_size(axis) for axis in ("x", "y", "zh"))
    for axis, before, joint, out_lines, out_size in (
        ("y", 1, n_s, lines + 8, size_y),
        ("zh", size_x, 1, lines + size_x * size_y, size_z),
    ):
        packed = pl.pallas_call(
            functools.partial(combine_kernel, lines, before, joint),
            name="combine_" + axis,
            out_shape=jax.ShapeDtypeStruct((out_size, out_lines, LANES), F32),
            in_specs=[whole],
            out_specs=whole,
            compiler_params=params,
        )(packed)
        packed = lax.all_to_all(packed, axis, 0, 0, tiled=True)

    expected, direct, sent = pl.pallas_call(
        functools.partial(backward_kernel, heads, float(tokens), ratings),
        name="attend_back",
        out_shape=(
            jax.ShapeDtypeStruct((8, LANES), F32),
            jax.ShapeDtypeStruct((own_channels, LANES), F32),
            jax.ShapeDtypeStruct((n_s, slots * n_t + 16, LANES), BF),
        ),
        in_specs=[scalars] + [whole] * 6,
        out_specs=(whole,) * 3,
        compiler_params=params,
    )(
        target_score,
        packed,
        final_gain.reshape(lines, LANES),
        output_weight,
        embed_weight,
        qkv,
        back,
    )

    sent = lax.all_to_all(sent, S_AXES, 0, 0, tiled=True)
    sent = pl.pallas_call(
        functools.partial(gather_kernel, slots),
        name="gather",
        out_shape=jax.ShapeDtypeStruct((n_t * LINES, LANES), BF),
        in_specs=[whole],
        out_specs=whole,
        scratch_shapes=[pltpu.VMEM((n_t * LINES, LANES), F32)],
        compiler_params=params,
    )(sent)
    sent = lax.all_to_all(
        sent.reshape(n_t * LINES // 2, 2, LANES), T_AXES, 0, 0, tiled=True
    ).reshape(n_t * LINES, LANES)

    count = 9 * channels * own_channels // LANES
    per = count // n_t
    out_lines = per + per % 2
    sums = pl.pallas_call(
        functools.partial(stem_back_kernel, cols, count_rows, slots, frames_dev),
        name="stem_back",
        out_shape=jax.ShapeDtypeStruct((n_t * out_lines, LANES), BF),
        in_specs=[whole] * 6,
        out_specs=whole,
        scratch_shapes=[
            pltpu.VMEM((9 * channels, own_channels), F32),
            pltpu.VMEM((count, LANES), F32),
            pltpu.VMEM((n_t * out_lines, LANES), F32),
            pltpu.VMEM((n_t * LINES, LANES), F32),
        ],
        compiler_params=params,
    )(sent, back_unit, scale_row, direct, gelu_slope, patch_tokens)
    sums = sums.reshape(n_t * out_lines // 2, 2, LANES)
    sums = lax.all_to_all(sums, T_AXES, 0, 0, tiled=True)
    sums = jnp.sum(sums.reshape(n_t, out_lines // 2, 2, LANES).astype(F32), axis=0)
    sums = lax.all_gather(sums, S_AXES, axis=0, tiled=False).reshape(n_s, out_lines, LANES)
    flat = sums[:, :per].reshape(n_s, -1, own_channels).transpose(1, 0, 2).reshape(-1)
    length = flat.shape[0] // n_s
    stem_gradient = lax.dynamic_slice_in_dim(flat, space_index * length, length, 0)
    return (expected[0, :1], stem_gradient)


def solution(mesh):
    shape = FACTORS[mesh.shape["tm"]] + (2, 2)
    split = Mesh(mesh.devices.reshape(shape), T_AXES + S_AXES)
    both = T_AXES + S_AXES
    in_specs = (
        P(T_AXES, S_AXES, None, None),
        P(S_AXES, None),
        P(S_AXES, None),
        P(T_AXES, None),
        P(),
        P(),
        P(None, S_AXES),
        P(None, S_AXES),
        P(None, S_AXES),
        P(S_AXES, None),
        P(both, None),
        P(),
        P(),
    )
    return jax.shard_map(
        on_device, mesh=split, in_specs=in_specs, out_specs=(P(), P(both)), check_vma=False
    )
```

```python
import functools
import math

import jax
import jax.numpy as jnp
from jax import lax
from jax.experimental import pallas as pl
from jax.experimental.pallas import tpu as pltpu
from jax.sharding import Mesh, PartitionSpec as P

HEAD = 128
LANES = 128
EPSILON = 1e-05
BF = jnp.bfloat16
F32 = jnp.float32
T_AXES = ("zh", "y", "x")
S_AXES = ("zl", "core")
FACTORS = {128: (4, 8, 4), 8: (2, 2, 2)}
NT = (((1,), (1,)), ((), ()))
TN = (((0,), (0,)), ((), ()))
VMEM_LIMIT = 40 * 1024 * 1024
LINES = 4
FAR = pltpu.HBM
STORES = 4
N_S = 4
SPACE_OF_BLOCK = (0, 2, 1, 3)


def dot(lhs, rhs, dims=(((1,), (0,)), ((), ()))):
    return lax.dot_general(lhs, rhs, dims, preferred_element_type=F32)


def kept(array):
    return pltpu.with_memory_space_constraint(array, FAR)


def thirds(row):
    first = row.astype(BF)
    rest = row - first.astype(F32)
    second = rest.astype(BF)
    third = (rest - second.astype(F32)).astype(BF)
    zero = jnp.zeros((5, row.shape[1]), F32)
    parts = [first.astype(F32), second.astype(F32), third.astype(F32), zero]
    return jnp.concatenate(parts, axis=0).astype(BF)


def halves(values):
    first = values.astype(BF)
    return first, (values - first.astype(F32)).astype(BF)


def in_window(lanes, cols, rows, row_off, col_off):
    lane = lax.broadcasted_iota(jnp.int32, (1, lanes), 1) % (rows * cols)
    row = lane // cols + row_off
    col = lane % cols + col_off
    return ((row >= 0) & (row < rows) & (col >= 0) & (col < cols)).astype(F32)


def offsets():
    return [(a, b) for a in (-1, 0, 1) for b in (-1, 0, 1)]


def stem_kernel(
    cols,
    rows,
    packed_ref,
    act_ref,
    slope_far,
    tokens_far,
    slope_ref,
    tokens_ref,
    weight_ref,
    done,
):
    n_s = packed_ref.shape[0]
    lanes, channels = tokens_ref.shape
    own = act_ref.shape[0]
    frames = lanes // (rows * cols)
    block = lanes // (frames * n_s)
    lane_blocks = channels // LANES
    count = lane_blocks * frames * block
    half = packed_ref.shape[1] - count
    for s in range(n_s):
        for part in range(lane_blocks):
            for frame in range(frames):
                source = (part * frames + frame) * block
                target = (frame * n_s + s) * block
                tokens_ref[target : target + block, part * LANES : (part + 1) * LANES] = packed_ref[
                    s, source : source + block, :
                ]
        pairs = packed_ref[s, count:, :]
        at = 2 * s * half
        weight_ref[at : at + half, :] = pairs[:, :own]
        weight_ref[at + half : at + 2 * half, :] = pairs[:, own:]
    tokens_store = pltpu.make_async_copy(tokens_ref, tokens_far, done.at[0])
    tokens_store.start()
    tokens = tokens_ref[...]
    total = jnp.zeros((own, lanes), F32)
    for tap, (row_off, col_off) in enumerate(offsets()):
        weight = weight_ref[tap * channels : (tap + 1) * channels, :]
        part = dot(weight, tokens, (((0,), (1,)), ((), ())))
        shift = row_off * cols + col_off
        if shift:
            part = pltpu.roll(part, (-shift) % lanes, 1)
        total = total + in_window(lanes, cols, rows, row_off, col_off) * part
    root = math.sqrt(2.0 / math.pi)
    square = total * total
    bent = jnp.tanh(root * (total + 0.044715 * (square * total)))
    half_up = 0.5 * (1.0 + bent)
    slope_ref[...] = half_up + 0.5 * total * (1.0 - bent * bent) * (
        root * (1.0 + 3 * 0.044715 * square)
    )
    slope_store = pltpu.make_async_copy(slope_ref, slope_far, done.at[1])
    slope_store.start()
    act_ref[...] = (total * half_up).astype(BF)
    tokens_store.wait()
    slope_store.wait()


def stem_back_kernel(
    cols,
    rows,
    slots,
    frames,
    got_ref,
    back_unit_ref,
    scale_ref,
    direct_ref,
    slope_ref,
    tokens_ref,
    out_ref,
    grad_ref,
    lines_ref,
    wide_ref,
    got_wide_ref,
):
    lanes, channels = tokens_ref.shape
    own = slope_ref.shape[0]
    depth = got_ref.shape[0] // LINES
    got_wide_ref[...] = got_ref[...].astype(F32)
    turned = [got_wide_ref[pl.ds(i, depth, stride=LINES), :].T for i in range(slots + 1)]
    unit = jnp.concatenate(
        [turned[s][f * own : (f + 1) * own] for f in range(frames) for s in range(slots)], axis=1
    )
    mean = jnp.concatenate(
        [
            turned[slots][s * frames + f : s * frames + f + 1]
            for f in range(frames)
            for s in range(slots)
        ],
        axis=1,
    )
    grad_act = scale_ref[...] * (unit - mean * back_unit_ref[...]) + direct_ref[:, :1]
    grad_pre = (slope_ref[...] * grad_act).astype(BF).astype(F32)
    tokens = tokens_ref[...]
    for tap, (row_off, col_off) in enumerate(offsets()):
        moved = in_window(lanes, cols, rows, row_off, col_off) * grad_pre
        shift = row_off * cols + col_off
        if shift:
            moved = pltpu.roll(moved, shift % lanes, 1)
        part = dot(moved.astype(BF), tokens).T
        grad_ref[tap * channels : (tap + 1) * channels, :] = part
    count = lines_ref.shape[0]
    lines_ref[...] = jnp.concatenate(
        [grad_ref[pl.ds(i, count, stride=2), :] for i in range(2)], axis=1
    )
    per, out_lines = count // depth, out_ref.shape[0] // depth
    blank = jnp.zeros((depth, LANES), F32)
    for line in range(out_lines):
        value = blank
        if line < per:
            value = lines_ref[pl.ds(line, depth, stride=per), :]
        wide_ref[pl.ds(line, depth, stride=out_lines), :] = value
    out_ref[...] = wide_ref[...].astype(BF)


def split_heads(block, heads):
    inner = heads * HEAD
    for head in range(heads):
        at = head * HEAD
        yield (
            head,
            block[:, at : at + HEAD],
            block[:, inner + at : inner + at + HEAD],
            block[:, 2 * inner + at : 2 * inner + at + HEAD],
        )


def as_lines(row):
    return jnp.concatenate(
        [row[:, i : i + LANES] for i in range(0, row.shape[1], LANES)], axis=0
    )


def as_row(lines):
    return jnp.concatenate([lines[i : i + 1] for i in range(lines.shape[0])], axis=1)


def pack_kernel(patches_far, stem_far, out_ref, patches_ref, stem_ref, done):
    fetches = [
        pltpu.make_async_copy(patches_far, patches_ref, done.at[0]),
        pltpu.make_async_copy(stem_far, stem_ref, done.at[1]),
    ]
    for fetch in fetches:
        fetch.start()
    for fetch in fetches:
        fetch.wait()
    count = patches_ref.shape[0]
    lane_blocks = patches_ref.shape[1] // LANES
    half = stem_ref.shape[0] // 2
    own = stem_ref.shape[1] // N_S
    for s in range(N_S):
        for i in range(lane_blocks):
            out_ref[s, i * count : (i + 1) * count, :] = patches_ref[:, i * LANES : (i + 1) * LANES]
        pair = [stem_ref[h * half : (h + 1) * half, s * own : (s + 1) * own] for h in range(2)]
        out_ref[s, lane_blocks * count :, :] = jnp.concatenate(pair, axis=1)


def chunk_rows(n_t, chunks, chunk, frame):
    return pl.ds(2 * chunk + frame, n_t, stride=2 * chunks)


def embed_kernel(
    n_t,
    slots,
    place_ref,
    ids_ref,
    act_ref,
    pair_ref,
    across_ref,
    frame_ref,
    gain_ref,
    query_far,
    key_far,
    value_far,
    own_embed_ref,
    vocab_ref,
    moved_far,
    embed_sum_ref,
    scale_ref,
    back_unit_far,
    wide_ref,
    moved_ref,
    query_ref,
    key_ref,
    value_ref,
    back_unit_ref,
    done,
):
    fetches = [
        pltpu.make_async_copy(source, target, done.at[i])
        for i, (source, target) in enumerate(
            ((query_far, query_ref), (key_far, key_ref), (value_far, value_ref))
        )
    ]
    for fetch in fetches:
        fetch.start()
    core = place_ref[0]
    width = frame_ref.shape[1]
    frames = frame_ref.shape[0]
    tokens = act_ref.shape[1] // frames
    inner = query_ref.shape[1]
    near = pair_ref.shape[0]
    per = 3 * inner // LANES
    chunks = slots * per + 1
    gain = gain_ref[...].astype(F32)
    own = own_embed_ref.shape[0]

    def rows_of(which, at):
        starts = [pl.multiple_of((zl * 2 + which) * own, own) for zl in range(near // own)]
        return jnp.concatenate([act_ref[pl.ds(i, own), at : at + tokens] for i in starts], axis=0)

    embed_sum = jnp.zeros((1, width), F32)
    normed = []
    for frame in range(frames):
        at = frame * tokens
        made = dot(rows_of(core, at), pair_ref[...], TN)
        made = made + dot(rows_of(1 - core, at), across_ref[...], TN)
        embedded = (made + frame_ref[frame : frame + 1, :].astype(F32)).astype(BF)
        wide = embedded.astype(F32)
        embed_sum = embed_sum + jnp.sum(wide, axis=0, keepdims=True)
        scale = lax.rsqrt(jnp.mean(wide * wide, axis=1, keepdims=True) + EPSILON)
        normed.append((wide * scale * gain).astype(BF))
        scale_row = jnp.broadcast_to(scale, (tokens, LANES)).T[:1]
        scale_ref[:, at : at + tokens] = scale_row
        back_unit_ref[:, at : at + tokens] = dot(own_embed_ref[...], embedded, NT) * scale_row
    store = pltpu.make_async_copy(back_unit_ref, back_unit_far, done.at[3])
    store.start()
    embed_sum_ref[...] = embed_sum * (1.0 / N_S)
    for part, weight_ref in enumerate((query_ref, key_ref, value_ref)):
        fetches[part].wait()
        for frame in range(frames):
            made = dot(normed[frame], weight_ref[...])
            for slot in range(slots):
                for i in range(inner // LANES):
                    chunk = slot * per + part * (inner // LANES) + i
                    wide_ref[chunk_rows(n_t, chunks, chunk, frame), :] = made[
                        slot * n_t : (slot + 1) * n_t, i * LANES : (i + 1) * LANES
                    ]
    vocab = vocab_ref.shape[0]
    ratings = ids_ref.shape[0]
    column = lax.broadcasted_iota(jnp.int32, (1, vocab), 1)
    picks = [(column == ids_ref[r] - place_ref[1]).astype(F32) for r in range(ratings)]
    picks.append(jnp.zeros((8 - ratings, vocab), F32))
    rows = dot(jnp.concatenate(picks, axis=0).astype(BF), vocab_ref[...])
    groups = width // n_t
    lines = [
        rows[r : r + 1, g * n_t : (g + 1) * n_t] for r in range(ratings) for g in range(groups)
    ]
    lines.append(jnp.zeros((LANES - ratings * groups, n_t), F32))
    wide_ref[chunk_rows(n_t, chunks, chunks - 1, 0), :] = jnp.concatenate(lines, axis=0).T
    wide_ref[chunk_rows(n_t, chunks, chunks - 1, 1), :] = jnp.zeros((n_t, LANES), F32)
    stores = [store]
    block = moved_ref.shape[0] // STORES
    for i in range(STORES):
        rows = pl.ds(i * block, block)
        moved_ref[rows, :] = wide_ref[rows, :].astype(BF)
        stores.append(
            pltpu.make_async_copy(moved_ref.at[rows], moved_far.at[rows], done.at[4 + i])
        )
        stores[-1].start()
    for store in stores:
        store.wait()


def attention_weights(key, query):
    scores = dot(key, query, NT) * (1.0 / math.sqrt(HEAD))
    raised = jnp.exp(scores - jnp.max(scores, axis=0, keepdims=True))
    return raised / jnp.sum(raised, axis=0, keepdims=True)


def forward_kernel(
    heads,
    moved_ref,
    out_weight_ref,
    embed_sum_ref,
    back_ref,
    qkv_far,
    packed_ref,
    wide_ref,
    qkv_ref,
    done,
):
    del back_ref
    stores = []
    slots, frames = qkv_ref.shape[0], qkv_ref.shape[1]
    n_t = frames // 2
    per = 3 * heads
    chunks = slots * per + 1
    wide_ref[...] = moved_ref[...].astype(F32)
    sums = [0.0] * heads
    for slot in range(slots):
        for chunk in range(per):
            for frame in range(2):
                rows = chunk_rows(n_t, chunks, slot * per + chunk, frame)
                qkv_ref[
                    slot, frame * n_t : (frame + 1) * n_t, chunk * LANES : (chunk + 1) * LANES
                ] = wide_ref[rows, :].astype(BF)
        store = pltpu.make_async_copy(qkv_ref.at[slot], qkv_far.at[slot], done.at[slot])
        store.start()
        stores.append(store)
        for head, query, key, value in split_heads(qkv_ref[slot], heads):
            weights = attention_weights(key, query)
            mixture = dot(weights.astype(BF), value, TN).astype(BF).astype(F32)
            sums[head] = sums[head] + jnp.sum(mixture, axis=0, keepdims=True)
    mixture_sum = thirds(jnp.concatenate(sums, axis=1))
    mixed = jnp.sum(dot(mixture_sum, out_weight_ref[...]), axis=0, keepdims=True)
    pooled = as_lines(embed_sum_ref[...] + mixed)
    rating = jnp.sum(wide_ref[chunk_rows(n_t, chunks, chunks - 1, 0), :], axis=0, keepdims=True)
    blank = jnp.zeros((packed_ref.shape[1] - pooled.shape[0] - 1, LANES), F32)
    packed = jnp.concatenate([pooled, rating, blank], axis=0)
    for i in range(packed_ref.shape[0]):
        packed_ref[i] = packed
    for store in stores:
        store.wait()


def combine_kernel(lines, per, joint, in_ref, out_ref):
    size = in_ref.shape[0]
    pooled = in_ref[0, :lines]
    for i in range(1, size):
        pooled = pooled + in_ref[i, :lines]
    ratings = []
    for i in range(0, size, joint):
        rating = in_ref[i, lines : lines + per]
        for j in range(1, joint):
            rating = rating + in_ref[i + j, lines : lines + per]
        ratings.append(rating)
    parts = [pooled] + ratings
    left = out_ref.shape[1] - lines - per * len(ratings)
    if left:
        parts.append(jnp.zeros((left, LANES), F32))
    packed = jnp.concatenate(parts, axis=0)
    for i in range(out_ref.shape[0]):
        out_ref[i] = packed


def backward_kernel(
    heads,
    tokens,
    ratings,
    target_ref,
    packed_ref,
    gain_ref,
    out_weight_ref,
    own_embed_ref,
    qkv_ref,
    back_ref,
    expected_ref,
    direct_ref,
    sent_ref,
):
    lines = gain_ref.shape[0]
    width = lines * LANES
    pooled = packed_ref[0, :lines]
    for i in range(1, packed_ref.shape[0]):
        pooled = pooled + packed_ref[i, :lines]
    turned = jnp.concatenate([packed_ref[i, lines:] for i in range(packed_ref.shape[0])], axis=0)
    pad = LANES - turned.shape[0]
    if pad:
        turned = jnp.concatenate([turned, jnp.zeros((pad, LANES), F32)], axis=0)
    n_t = packed_ref.shape[0] * (packed_ref.shape[1] - lines)
    turned = turned.T[:, :n_t]
    groups = width // n_t
    rows = [turned[r * groups : (r + 1) * groups] for r in range(ratings)]
    if n_t != LANES:
        rows = [as_lines(as_row(row)) for row in rows]

    def total_of(values):
        return jnp.sum(jnp.sum(values, axis=1, keepdims=True), axis=0, keepdims=True)

    pooled_raw = pooled / tokens
    inverse_rms = lax.rsqrt(total_of(pooled_raw * pooled_raw) / width + EPSILON)
    unit = pooled_raw * inverse_rms
    gain = gain_ref[...].astype(F32)
    gained_unit = unit * gain
    logits = [total_of(row * gained_unit) for row in rows]
    top = functools.reduce(jnp.maximum, logits)
    raised = [jnp.exp(logit - top) for logit in logits]
    norm = sum(raised)
    probs = [value / norm for value in raised]
    expected = sum((r + 1.0) * prob for r, prob in enumerate(probs))
    expected_ref[...] = jnp.broadcast_to(expected, expected_ref.shape)
    target = target_ref[0]
    mixed = sum(
        (prob - jnp.where(target == r + 1, 1.0, 0.0)) * rows[r] for r, prob in enumerate(probs)
    )
    gained = gain * mixed
    centre = total_of(gained * unit) / width
    cotangent = inverse_rms * (gained - unit * centre) / math.sqrt(tokens)
    parts = thirds(as_row(cotangent))
    direct = jnp.sum(dot(own_embed_ref[...], parts, NT), axis=1, keepdims=True)
    direct_ref[...] = jnp.broadcast_to(direct, direct_ref.shape)
    grad_heads = jnp.sum(dot(parts, out_weight_ref[...], NT), axis=0, keepdims=True)
    factor = 1.0 / math.sqrt(HEAD)
    slots, frames = qkv_ref.shape[0], qkv_ref.shape[1]
    depth = frames // 2
    back_upper, back_lower = halves(back_ref[...])
    own = back_ref.shape[1] // N_S
    lane = lax.broadcasted_iota(jnp.int32, (1, LANES), 1)
    means = jnp.zeros((depth, LANES), F32)
    for slot in range(slots):
        grads_q, grads_k, grads_v = [], [], []
        total = jnp.zeros((frames, 1), F32)
        for head, query, key, value in split_heads(qkv_ref[slot], heads):
            grad_mixture = grad_heads[:, head * HEAD : (head + 1) * HEAD]
            weights = attention_weights(key, query)
            wide_value = value.astype(F32)
            grad_weights = jnp.sum(wide_value * grad_mixture, axis=1, keepdims=True)
            centre = jnp.sum(weights * grad_weights, axis=0, keepdims=True)
            upper, lower = halves(weights * (grad_weights - centre) * factor)
            grad_query = dot(upper, key, TN) + dot(lower, key, TN)
            grad_key = dot(upper, query) + dot(lower, query)
            mass = jnp.sum(weights.astype(BF).astype(F32), axis=1, keepdims=True)
            grad_value = mass * grad_mixture
            total = total + jnp.sum(
                grad_query * query.astype(F32)
                + grad_key * key.astype(F32)
                + grad_value * wide_value,
                axis=1,
                keepdims=True,
            )
            grads_q.append(grad_query.astype(BF))
            grads_k.append(grad_key.astype(BF))
            grads_v.append(grad_value.astype(BF))
        grads = jnp.concatenate(grads_q + grads_k + grads_v, axis=1)
        sent = dot(grads, back_upper) + dot(grads, back_lower)
        for block in range(N_S):
            s = SPACE_OF_BLOCK[block]
            both = [
                sent[f * depth : (f + 1) * depth, block * own : (block + 1) * own]
                for f in range(2)
            ]
            sent_ref[s, slot * depth : (slot + 1) * depth, :] = jnp.concatenate(
                both, axis=1
            ).astype(BF)
        for f in range(2):
            column = total[f * depth : (f + 1) * depth] / width
            means = means + jnp.where(lane == slot * 2 + f, 1.0, 0.0) * column
    turned = means.T[:16]
    if depth < LANES:
        turned = jnp.concatenate([turned, jnp.zeros((16, LANES - depth), F32)], axis=1)
    turned = turned.astype(BF)
    for s in range(N_S):
        sent_ref[s, slots * depth :, :] = turned


def gather_kernel(slots, in_ref, out_ref, wide_ref):
    depth = out_ref.shape[0] // LINES
    total = in_ref[0].astype(F32)
    for i in range(1, in_ref.shape[0]):
        total = total + in_ref[i].astype(F32)
    for slot in range(slots):
        wide_ref[pl.ds(slot, depth, stride=LINES), :] = total[slot * depth : (slot + 1) * depth]
    means = total[slots * depth :]
    blank = jnp.zeros((LANES - means.shape[0], LANES), F32)
    means = jnp.concatenate([means, blank], axis=0)
    wide_ref[pl.ds(slots, depth, stride=LINES), :] = means.T[:depth]
    wide_ref[pl.ds(slots + 1, depth, stride=LINES), :] = jnp.zeros((depth, LANES), F32)
    out_ref[...] = wide_ref[...].astype(BF)


def on_device(
    patches,
    stem_weight,
    embed_weight,
    frame_embed,
    attention_gain,
    final_gain,
    query_weight,
    key_weight,
    value_weight,
    output_weight,
    unembedding,
    rating_ids,
    target_score,
):
    n_t = lax.axis_size(T_AXES)
    n_s = lax.axis_size(S_AXES)
    everyone = T_AXES + S_AXES
    space_index = lax.axis_index(S_AXES)
    frames_dev, rows_dev, cols, channels = patches.shape
    own_channels = channels // n_s
    count_rows = rows_dev * n_s
    positions = count_rows * cols
    slots = positions // n_t
    width = embed_weight.shape[1]
    inner = query_weight.shape[1]
    heads = inner // HEAD
    all_frames = frames_dev * n_t
    tokens = all_frames * positions
    tokens_dev = frames_dev * positions
    assert frames_dev == 2 and slots == 2

    whole = pl.BlockSpec(memory_space=pltpu.VMEM)
    far = pl.BlockSpec(memory_space=FAR)
    params = pltpu.CompilerParams(vmem_limit_bytes=VMEM_LIMIT)
    other = lax.ppermute(embed_weight, "zl", [(0, 1), (1, 0)])

    patch_rows = patches.reshape(-1, channels)
    stem_half = stem_weight.shape[0] // 2
    packed_rows = patch_rows.shape[0] * (channels // LANES) + stem_half
    packed = pl.pallas_call(
        pack_kernel,
        name="pack",
        out_shape=jax.ShapeDtypeStruct((n_s, packed_rows, LANES), BF),
        in_specs=[far] * 2,
        out_specs=whole,
        scratch_shapes=[
            pltpu.VMEM(patch_rows.shape, BF),
            pltpu.VMEM(stem_weight.shape, BF),
            pltpu.SemaphoreType.DMA((2,)),
        ],
        compiler_params=params,
    )(kept(patch_rows), kept(stem_weight))
    packed = lax.all_to_all(packed, S_AXES, 0, 0, tiled=True)

    act, gelu_slope, patch_tokens = pl.pallas_call(
        functools.partial(stem_kernel, cols, count_rows),
        name="stem",
        out_shape=(
            jax.ShapeDtypeStruct((own_channels, tokens_dev), BF),
            pltpu.HBM((own_channels, tokens_dev), F32),
            pltpu.HBM((tokens_dev, channels), BF),
        ),
        in_specs=[whole],
        out_specs=(whole, far, far),
        scratch_shapes=[
            pltpu.VMEM((own_channels, tokens_dev), F32),
            pltpu.VMEM((tokens_dev, channels), BF),
            pltpu.VMEM((9 * channels, own_channels), BF),
            pltpu.SemaphoreType.DMA((2,)),
        ],
        compiler_params=params,
    )(packed)
    act = lax.all_gather(act, S_AXES, axis=0, tiled=True)

    lower = lax.axis_index("zl") == 0
    pair = jnp.concatenate(
        [jnp.where(lower, embed_weight, other), jnp.where(lower, other, embed_weight)], axis=0
    )
    across = lax.ppermute(pair, "core", [(0, 1), (1, 0)])
    core_index = lax.axis_index("core")
    vocab_dev = unembedding.shape[0]
    ratings = rating_ids.shape[0]
    place = jnp.stack([core_index, lax.axis_index(everyone) * vocab_dev]).astype(jnp.int32)

    chunks = slots * 3 * inner // LANES + 1
    scalars = pl.BlockSpec(memory_space=pltpu.SMEM)
    moved, embed_sum, scale_row, back_unit = pl.pallas_call(
        functools.partial(embed_kernel, n_t, slots),
        name="embed",
        out_shape=(
            pltpu.HBM((n_t * chunks * 2, LANES), BF),
            jax.ShapeDtypeStruct((1, width), F32),
            jax.ShapeDtypeStruct((1, tokens_dev), F32),
            pltpu.HBM((own_channels, tokens_dev), F32),
        ),
        in_specs=[scalars] * 2 + [whole] * 5 + [far] * 3 + [whole] * 2,
        out_specs=(far, whole, whole, far),
        scratch_shapes=[pltpu.VMEM((n_t * chunks * 2, LANES), kind) for kind in (F32, BF)]
        + [pltpu.VMEM((width, inner), BF)] * 3
        + [pltpu.VMEM((own_channels, tokens_dev), F32), pltpu.SemaphoreType.DMA((4 + STORES,))],
        compiler_params=params,
    )(
        place,
        rating_ids,
        act,
        pair,
        across,
        frame_embed,
        attention_gain[None, :],
        kept(query_weight),
        kept(key_weight),
        kept(value_weight),
        embed_weight,
        unembedding,
    )

    moved = moved.reshape(n_t * chunks, 2, LANES)
    moved = lax.all_to_all(moved, T_AXES, 0, 0, tiled=True)
    moved = moved.reshape(n_t * chunks * 2, LANES)

    gain = attention_gain.astype(F32)
    sides = []
    for part in (pair, across):
        upper, lower_half = halves(part.astype(F32) * gain)
        sides.append(
            jnp.concatenate(
                [
                    dot(w, upper, (((0,), (1,)), ((), ())))
                    + dot(w, lower_half, (((0,), (1,)), ((), ())))
                    for w in (query_weight, key_weight, value_weight)
                ],
                axis=0,
            )
        )
    first_core = core_index == 0
    back = jnp.concatenate(
        [jnp.where(first_core, sides[0], sides[1]), jnp.where(first_core, sides[1], sides[0])],
        axis=1,
    )

    lines = width // LANES
    first = lax.axis_size(("x",) + S_AXES)
    qkv, packed = pl.pallas_call(
        functools.partial(forward_kernel, heads),
        name="attend",
        out_shape=(
            pltpu.HBM((slots, all_frames, 3 * inner), BF),
            jax.ShapeDtypeStruct((first, lines + 8, LANES), F32),
        ),
        in_specs=[whole] * 3 + [pl.BlockSpec(memory_space=pl.ANY)],
        out_specs=(far, whole),
        scratch_shapes=[
            pltpu.VMEM((n_t * chunks * 2, LANES), F32),
            pltpu.VMEM((slots, all_frames, 3 * inner), BF),
            pltpu.SemaphoreType.DMA((slots,)),
        ],
        compiler_params=params,
    )(moved, output_weight, embed_sum, back)

    packed = lax.all_to_all(packed, ("x",) + S_AXES, 0, 0, tiled=True)
    size_x, size_y, size_z = (lax.axis_size(axis) for axis in ("x", "y", "zh"))
    for axis, before, joint, out_lines, out_size in (
        ("y", 1, n_s, lines + 8, size_y),
        ("zh", size_x, 1, lines + size_x * size_y, size_z),
    ):
        packed = pl.pallas_call(
            functools.partial(combine_kernel, lines, before, joint),
            name="combine_" + axis,
            out_shape=jax.ShapeDtypeStruct((out_size, out_lines, LANES), F32),
            in_specs=[whole],
            out_specs=whole,
            compiler_params=params,
        )(packed)
        packed = lax.all_to_all(packed, axis, 0, 0, tiled=True)

    expected, direct, sent = pl.pallas_call(
        functools.partial(backward_kernel, heads, float(tokens), ratings),
        name="attend_back",
        out_shape=(
            jax.ShapeDtypeStruct((8, LANES), F32),
            jax.ShapeDtypeStruct((own_channels, LANES), F32),
            jax.ShapeDtypeStruct((n_s, slots * n_t + 16, LANES), BF),
        ),
        in_specs=[scalars] + [whole] * 6,
        out_specs=(whole,) * 3,
        compiler_params=params,
    )(
        target_score,
        packed,
        final_gain.reshape(lines, LANES),
        output_weight,
        embed_weight,
        qkv,
        back,
    )

    sent = lax.all_to_all(sent, S_AXES, 0, 0, tiled=True)
    sent = pl.pallas_call(
        functools.partial(gather_kernel, slots),
        name="gather",
        out_shape=jax.ShapeDtypeStruct((n_t * LINES, LANES), BF),
        in_specs=[whole],
        out_specs=whole,
        scratch_shapes=[pltpu.VMEM((n_t * LINES, LANES), F32)],
        compiler_params=params,
    )(sent)
    sent = lax.all_to_all(
        sent.reshape(n_t * LINES // 2, 2, LANES), T_AXES, 0, 0, tiled=True
    ).reshape(n_t * LINES, LANES)

    count = 9 * channels * own_channels // LANES
    per = count // n_t
    out_lines = per + per % 2
    sums = pl.pallas_call(
        functools.partial(stem_back_kernel, cols, count_rows, slots, frames_dev),
        name="stem_back",
        out_shape=jax.ShapeDtypeStruct((n_t * out_lines, LANES), BF),
        in_specs=[whole] * 6,
        out_specs=whole,
        scratch_shapes=[
            pltpu.VMEM((9 * channels, own_channels), F32),
            pltpu.VMEM((count, LANES), F32),
            pltpu.VMEM((n_t * out_lines, LANES), F32),
            pltpu.VMEM((n_t * LINES, LANES), F32),
        ],
        compiler_params=params,
    )(sent, back_unit, scale_row, direct, gelu_slope, patch_tokens)
    sums = sums.reshape(n_t * out_lines // 2, 2, LANES)
    sums = lax.all_to_all(sums, T_AXES, 0, 0, tiled=True)
    sums = jnp.sum(sums.reshape(n_t, out_lines // 2, 2, LANES).astype(F32), axis=0)
    sums = lax.all_gather(sums, S_AXES, axis=0, tiled=False).reshape(n_s, out_lines, LANES)
    flat = sums[:, :per].reshape(n_s, -1, own_channels).transpose(1, 0, 2).reshape(-1)
    length = flat.shape[0] // n_s
    stem_gradient = lax.dynamic_slice_in_dim(flat, space_index * length, length, 0)
    return (expected[0, :1], stem_gradient)


def solution(mesh):
    shape = FACTORS[mesh.shape["tm"]] + (2, 2)
    split = Mesh(mesh.devices.reshape(shape), T_AXES + S_AXES)
    both = T_AXES + S_AXES
    in_specs = (
        P(T_AXES, S_AXES, None, None),
        P(S_AXES, None),
        P(S_AXES, None),
        P(T_AXES, None),
        P(),
        P(),
        P(None, S_AXES),
        P(None, S_AXES),
        P(None, S_AXES),
        P(S_AXES, None),
        P(both, None),
        P(),
        P(),
    )
    return jax.shard_map(
        on_device, mesh=split, in_specs=in_specs, out_specs=(P(), P(both)), check_vma=False
    )
```

```python
import functools
import math

import jax
import jax.numpy as jnp
from jax import lax
from jax.experimental import pallas as pl
from jax.experimental.pallas import tpu as pltpu
from jax.sharding import Mesh, PartitionSpec as P

HEAD = 128
LANES = 128
EPSILON = 1e-05
BF = jnp.bfloat16
F32 = jnp.float32
T_AXES = ("zh", "y", "x")
S_AXES = ("zl", "core")
FACTORS = {128: (4, 8, 4), 8: (2, 2, 2)}
NT = (((1,), (1,)), ((), ()))
TN = (((0,), (0,)), ((), ()))
VMEM_LIMIT = 40 * 1024 * 1024
LINES = 4
FAR = pltpu.HBM
STORES = 4
N_S = 4
SPACE_OF_BLOCK = (0, 2, 1, 3)


def dot(lhs, rhs, dims=(((1,), (0,)), ((), ()))):
    return lax.dot_general(lhs, rhs, dims, preferred_element_type=F32)


def kept(array):
    return pltpu.with_memory_space_constraint(array, FAR)


def thirds(row):
    first = row.astype(BF)
    rest = row - first.astype(F32)
    second = rest.astype(BF)
    third = (rest - second.astype(F32)).astype(BF)
    zero = jnp.zeros((5, row.shape[1]), F32)
    parts = [first.astype(F32), second.astype(F32), third.astype(F32), zero]
    return jnp.concatenate(parts, axis=0).astype(BF)


def halves(values):
    first = values.astype(BF)
    return first, (values - first.astype(F32)).astype(BF)


def in_window(lanes, cols, rows, row_off, col_off):
    lane = lax.broadcasted_iota(jnp.int32, (1, lanes), 1) % (rows * cols)
    row = lane // cols + row_off
    col = lane % cols + col_off
    return ((row >= 0) & (row < rows) & (col >= 0) & (col < cols)).astype(F32)


def offsets():
    return [(a, b) for a in (-1, 0, 1) for b in (-1, 0, 1)]


def stem_kernel(
    cols,
    rows,
    packed_ref,
    act_ref,
    slope_far,
    tokens_far,
    slope_ref,
    tokens_ref,
    weight_ref,
    done,
):
    n_s = packed_ref.shape[0]
    lanes, channels = tokens_ref.shape
    own = act_ref.shape[0]
    frames = lanes // (rows * cols)
    block = lanes // (frames * n_s)
    lane_blocks = channels // LANES
    count = lane_blocks * frames * block
    half = packed_ref.shape[1] - count
    for s in range(n_s):
        for part in range(lane_blocks):
            for frame in range(frames):
                source = (part * frames + frame) * block
                target = (frame * n_s + s) * block
                tokens_ref[target : target + block, part * LANES : (part + 1) * LANES] = packed_ref[
                    s, source : source + block, :
                ]
        pairs = packed_ref[s, count:, :]
        at = 2 * s * half
        weight_ref[at : at + half, :] = pairs[:, :own]
        weight_ref[at + half : at + 2 * half, :] = pairs[:, own:]
    tokens_store = pltpu.make_async_copy(tokens_ref, tokens_far, done.at[0])
    tokens_store.start()
    tokens = tokens_ref[...]
    total = jnp.zeros((own, lanes), F32)
    for tap, (row_off, col_off) in enumerate(offsets()):
        weight = weight_ref[tap * channels : (tap + 1) * channels, :]
        part = dot(weight, tokens, (((0,), (1,)), ((), ())))
        shift = row_off * cols + col_off
        if shift:
            part = pltpu.roll(part, (-shift) % lanes, 1)
        total = total + in_window(lanes, cols, rows, row_off, col_off) * part
    root = math.sqrt(2.0 / math.pi)
    square = total * total
    bent = jnp.tanh(root * (total + 0.044715 * (square * total)))
    half_up = 0.5 * (1.0 + bent)
    slope_ref[...] = half_up + 0.5 * total * (1.0 - bent * bent) * (
        root * (1.0 + 3 * 0.044715 * square)
    )
    slope_store = pltpu.make_async_copy(slope_ref, slope_far, done.at[1])
    slope_store.start()
    act_ref[...] = (total * half_up).astype(BF)
    tokens_store.wait()
    slope_store.wait()


def stem_back_kernel(
    cols,
    rows,
    slots,
    frames,
    got_ref,
    back_unit_ref,
    scale_ref,
    direct_ref,
    slope_ref,
    tokens_ref,
    out_ref,
    grad_ref,
    lines_ref,
    wide_ref,
    got_wide_ref,
):
    lanes, channels = tokens_ref.shape
    own = slope_ref.shape[0]
    depth = got_ref.shape[0] // LINES
    got_wide_ref[...] = got_ref[...].astype(F32)
    turned = [got_wide_ref[pl.ds(i, depth, stride=LINES), :].T for i in range(slots + 1)]
    unit = jnp.concatenate(
        [turned[s][f * own : (f + 1) * own] for f in range(frames) for s in range(slots)], axis=1
    )
    mean = jnp.concatenate(
        [
            turned[slots][s * frames + f : s * frames + f + 1]
            for f in range(frames)
            for s in range(slots)
        ],
        axis=1,
    )
    grad_act = scale_ref[...] * (unit - mean * back_unit_ref[...]) + direct_ref[:, :1]
    grad_pre = (slope_ref[...] * grad_act).astype(BF).astype(F32)
    tokens = tokens_ref[...]
    for tap, (row_off, col_off) in enumerate(offsets()):
        moved = in_window(lanes, cols, rows, row_off, col_off) * grad_pre
        shift = row_off * cols + col_off
        if shift:
            moved = pltpu.roll(moved, shift % lanes, 1)
        part = dot(moved.astype(BF), tokens).T
        grad_ref[tap * channels : (tap + 1) * channels, :] = part
    count = lines_ref.shape[0]
    lines_ref[...] = jnp.concatenate(
        [grad_ref[pl.ds(i, count, stride=2), :] for i in range(2)], axis=1
    )
    per, out_lines = count // depth, out_ref.shape[0] // depth
    blank = jnp.zeros((depth, LANES), F32)
    for line in range(out_lines):
        value = blank
        if line < per:
            value = lines_ref[pl.ds(line, depth, stride=per), :]
        wide_ref[pl.ds(line, depth, stride=out_lines), :] = value
    out_ref[...] = wide_ref[...].astype(BF)


def split_heads(block, heads):
    inner = heads * HEAD
    for head in range(heads):
        at = head * HEAD
        yield (
            head,
            block[:, at : at + HEAD],
            block[:, inner + at : inner + at + HEAD],
            block[:, 2 * inner + at : 2 * inner + at + HEAD],
        )


def as_lines(row):
    return jnp.concatenate(
        [row[:, i : i + LANES] for i in range(0, row.shape[1], LANES)], axis=0
    )


def as_row(lines):
    return jnp.concatenate([lines[i : i + 1] for i in range(lines.shape[0])], axis=1)


def pack_kernel(patches_far, stem_far, out_ref, patches_ref, stem_ref, done):
    fetches = [
        pltpu.make_async_copy(patches_far, patches_ref, done.at[0]),
        pltpu.make_async_copy(stem_far, stem_ref, done.at[1]),
    ]
    for fetch in fetches:
        fetch.start()
    for fetch in fetches:
        fetch.wait()
    count = patches_ref.shape[0]
    lane_blocks = patches_ref.shape[1] // LANES
    half = stem_ref.shape[0] // 2
    own = stem_ref.shape[1] // N_S
    for s in range(N_S):
        for i in range(lane_blocks):
            out_ref[s, i * count : (i + 1) * count, :] = patches_ref[:, i * LANES : (i + 1) * LANES]
        pair = [stem_ref[h * half : (h + 1) * half, s * own : (s + 1) * own] for h in range(2)]
        out_ref[s, lane_blocks * count :, :] = jnp.concatenate(pair, axis=1)


def chunk_rows(n_t, chunks, chunk, frame):
    return pl.ds(2 * chunk + frame, n_t, stride=2 * chunks)


def embed_kernel(
    n_t,
    slots,
    place_ref,
    ids_ref,
    act_ref,
    pair_ref,
    across_ref,
    frame_ref,
    gain_ref,
    query_far,
    key_far,
    value_far,
    own_embed_ref,
    vocab_ref,
    moved_far,
    embed_sum_ref,
    scale_ref,
    back_unit_far,
    wide_ref,
    moved_ref,
    query_ref,
    key_ref,
    value_ref,
    back_unit_ref,
    done,
):
    fetches = [
        pltpu.make_async_copy(source, target, done.at[i])
        for i, (source, target) in enumerate(
            ((query_far, query_ref), (key_far, key_ref), (value_far, value_ref))
        )
    ]
    for fetch in fetches:
        fetch.start()
    core = place_ref[0]
    width = frame_ref.shape[1]
    frames = frame_ref.shape[0]
    tokens = act_ref.shape[1] // frames
    inner = query_ref.shape[1]
    near = pair_ref.shape[0]
    per = 3 * inner // LANES
    chunks = slots * per + 1
    gain = gain_ref[...].astype(F32)
    own = own_embed_ref.shape[0]

    def rows_of(which, at):
        starts = [pl.multiple_of((zl * 2 + which) * own, own) for zl in range(near // own)]
        return jnp.concatenate([act_ref[pl.ds(i, own), at : at + tokens] for i in starts], axis=0)

    embed_sum = jnp.zeros((1, width), F32)
    normed = []
    for frame in range(frames):
        at = frame * tokens
        made = dot(rows_of(core, at), pair_ref[...], TN)
        made = made + dot(rows_of(1 - core, at), across_ref[...], TN)
        embedded = (made + frame_ref[frame : frame + 1, :].astype(F32)).astype(BF)
        wide = embedded.astype(F32)
        embed_sum = embed_sum + jnp.sum(wide, axis=0, keepdims=True)
        scale = lax.rsqrt(jnp.mean(wide * wide, axis=1, keepdims=True) + EPSILON)
        normed.append((wide * scale * gain).astype(BF))
        scale_row = jnp.broadcast_to(scale, (tokens, LANES)).T[:1]
        scale_ref[:, at : at + tokens] = scale_row
        back_unit_ref[:, at : at + tokens] = dot(own_embed_ref[...], embedded, NT) * scale_row
    store = pltpu.make_async_copy(back_unit_ref, back_unit_far, done.at[3])
    store.start()
    embed_sum_ref[...] = embed_sum * (1.0 / N_S)
    for part, weight_ref in enumerate((query_ref, key_ref, value_ref)):
        fetches[part].wait()
        for frame in range(frames):
            made = dot(normed[frame], weight_ref[...])
            for slot in range(slots):
                for i in range(inner // LANES):
                    chunk = slot * per + part * (inner // LANES) + i
                    wide_ref[chunk_rows(n_t, chunks, chunk, frame), :] = made[
                        slot * n_t : (slot + 1) * n_t, i * LANES : (i + 1) * LANES
                    ]
    vocab = vocab_ref.shape[0]
    ratings = ids_ref.shape[0]
    column = lax.broadcasted_iota(jnp.int32, (1, vocab), 1)
    picks = [(column == ids_ref[r] - place_ref[1]).astype(F32) for r in range(ratings)]
    picks.append(jnp.zeros((8 - ratings, vocab), F32))
    rows = dot(jnp.concatenate(picks, axis=0).astype(BF), vocab_ref[...])
    groups = width // n_t
    lines = [
        rows[r : r + 1, g * n_t : (g + 1) * n_t] for r in range(ratings) for g in range(groups)
    ]
    lines.append(jnp.zeros((LANES - ratings * groups, n_t), F32))
    wide_ref[chunk_rows(n_t, chunks, chunks - 1, 0), :] = jnp.concatenate(lines, axis=0).T
    wide_ref[chunk_rows(n_t, chunks, chunks - 1, 1), :] = jnp.zeros((n_t, LANES), F32)
    stores = [store]
    block = moved_ref.shape[0] // STORES
    for i in range(STORES):
        rows = pl.ds(i * block, block)
        moved_ref[rows, :] = wide_ref[rows, :].astype(BF)
        stores.append(
            pltpu.make_async_copy(moved_ref.at[rows], moved_far.at[rows], done.at[4 + i])
        )
        stores[-1].start()
    for store in stores:
        store.wait()


def attention_weights(key, query):
    scores = dot(key, query, NT) * (1.0 / math.sqrt(HEAD))
    raised = jnp.exp(scores - jnp.max(scores, axis=0, keepdims=True))
    return raised / jnp.sum(raised, axis=0, keepdims=True)


def forward_kernel(
    heads,
    moved_ref,
    out_weight_ref,
    embed_sum_ref,
    back_ref,
    qkv_far,
    packed_ref,
    wide_ref,
    qkv_ref,
    done,
):
    del back_ref
    stores = []
    slots, frames = qkv_ref.shape[0], qkv_ref.shape[1]
    n_t = frames // 2
    per = 3 * heads
    chunks = slots * per + 1
    wide_ref[...] = moved_ref[...].astype(F32)
    sums = [0.0] * heads
    for slot in range(slots):
        for chunk in range(per):
            for frame in range(2):
                rows = chunk_rows(n_t, chunks, slot * per + chunk, frame)
                qkv_ref[
                    slot, frame * n_t : (frame + 1) * n_t, chunk * LANES : (chunk + 1) * LANES
                ] = wide_ref[rows, :].astype(BF)
        store = pltpu.make_async_copy(qkv_ref.at[slot], qkv_far.at[slot], done.at[slot])
        store.start()
        stores.append(store)
        for head, query, key, value in split_heads(qkv_ref[slot], heads):
            weights = attention_weights(key, query)
            mixture = dot(weights.astype(BF), value, TN).astype(BF).astype(F32)
            sums[head] = sums[head] + jnp.sum(mixture, axis=0, keepdims=True)
    mixture_sum = thirds(jnp.concatenate(sums, axis=1))
    mixed = jnp.sum(dot(mixture_sum, out_weight_ref[...]), axis=0, keepdims=True)
    pooled = as_lines(embed_sum_ref[...] + mixed)
    rating = jnp.sum(wide_ref[chunk_rows(n_t, chunks, chunks - 1, 0), :], axis=0, keepdims=True)
    blank = jnp.zeros((packed_ref.shape[1] - pooled.shape[0] - 1, LANES), F32)
    packed = jnp.concatenate([pooled, rating, blank], axis=0)
    for i in range(packed_ref.shape[0]):
        packed_ref[i] = packed
    for store in stores:
        store.wait()


def combine_kernel(lines, per, joint, in_ref, out_ref):
    size = in_ref.shape[0]
    pooled = in_ref[0, :lines]
    for i in range(1, size):
        pooled = pooled + in_ref[i, :lines]
    ratings = []
    for i in range(0, size, joint):
        rating = in_ref[i, lines : lines + per]
        for j in range(1, joint):
            rating = rating + in_ref[i + j, lines : lines + per]
        ratings.append(rating)
    parts = [pooled] + ratings
    left = out_ref.shape[1] - lines - per * len(ratings)
    if left:
        parts.append(jnp.zeros((left, LANES), F32))
    packed = jnp.concatenate(parts, axis=0)
    for i in range(out_ref.shape[0]):
        out_ref[i] = packed


def backward_kernel(
    heads,
    tokens,
    ratings,
    target_ref,
    packed_ref,
    gain_ref,
    out_weight_ref,
    own_embed_ref,
    qkv_ref,
    back_ref,
    expected_ref,
    direct_ref,
    sent_ref,
):
    lines = gain_ref.shape[0]
    width = lines * LANES
    pooled = packed_ref[0, :lines]
    for i in range(1, packed_ref.shape[0]):
        pooled = pooled + packed_ref[i, :lines]
    turned = jnp.concatenate([packed_ref[i, lines:] for i in range(packed_ref.shape[0])], axis=0)
    pad = LANES - turned.shape[0]
    if pad:
        turned = jnp.concatenate([turned, jnp.zeros((pad, LANES), F32)], axis=0)
    n_t = packed_ref.shape[0] * (packed_ref.shape[1] - lines)
    turned = turned.T[:, :n_t]
    groups = width // n_t
    rows = [turned[r * groups : (r + 1) * groups] for r in range(ratings)]
    if n_t != LANES:
        rows = [as_lines(as_row(row)) for row in rows]

    def total_of(values):
        return jnp.sum(jnp.sum(values, axis=1, keepdims=True), axis=0, keepdims=True)

    pooled_raw = pooled / tokens
    inverse_rms = lax.rsqrt(total_of(pooled_raw * pooled_raw) / width + EPSILON)
    unit = pooled_raw * inverse_rms
    gain = gain_ref[...].astype(F32)
    gained_unit = unit * gain
    logits = [total_of(row * gained_unit) for row in rows]
    top = functools.reduce(jnp.maximum, logits)
    raised = [jnp.exp(logit - top) for logit in logits]
    norm = sum(raised)
    probs = [value / norm for value in raised]
    expected = sum((r + 1.0) * prob for r, prob in enumerate(probs))
    expected_ref[...] = jnp.broadcast_to(expected, expected_ref.shape)
    target = target_ref[0]
    mixed = sum(
        (prob - jnp.where(target == r + 1, 1.0, 0.0)) * rows[r] for r, prob in enumerate(probs)
    )
    gained = gain * mixed
    centre = total_of(gained * unit) / width
    cotangent = inverse_rms * (gained - unit * centre) / math.sqrt(tokens)
    parts = thirds(as_row(cotangent))
    direct = jnp.sum(dot(own_embed_ref[...], parts, NT), axis=1, keepdims=True)
    direct_ref[...] = jnp.broadcast_to(direct, direct_ref.shape)
    grad_heads = jnp.sum(dot(parts, out_weight_ref[...], NT), axis=0, keepdims=True)
    factor = 1.0 / math.sqrt(HEAD)
    slots, frames = qkv_ref.shape[0], qkv_ref.shape[1]
    depth = frames // 2
    back_upper, back_lower = halves(back_ref[...])
    own = back_ref.shape[1] // N_S
    lane = lax.broadcasted_iota(jnp.int32, (1, LANES), 1)
    means = jnp.zeros((depth, LANES), F32)
    for slot in range(slots):
        grads_q, grads_k, grads_v = [], [], []
        total = jnp.zeros((frames, 1), F32)
        for head, query, key, value in split_heads(qkv_ref[slot], heads):
            grad_mixture = grad_heads[:, head * HEAD : (head + 1) * HEAD]
            weights = attention_weights(key, query)
            wide_value = value.astype(F32)
            grad_weights = jnp.sum(wide_value * grad_mixture, axis=1, keepdims=True)
            centre = jnp.sum(weights * grad_weights, axis=0, keepdims=True)
            upper, lower = halves(weights * (grad_weights - centre) * factor)
            grad_query = dot(upper, key, TN) + dot(lower, key, TN)
            grad_key = dot(upper, query) + dot(lower, query)
            mass = jnp.sum(weights.astype(BF).astype(F32), axis=1, keepdims=True)
            grad_value = mass * grad_mixture
            total = total + jnp.sum(
                grad_query * query.astype(F32)
                + grad_key * key.astype(F32)
                + grad_value * wide_value,
                axis=1,
                keepdims=True,
            )
            grads_q.append(grad_query.astype(BF))
            grads_k.append(grad_key.astype(BF))
            grads_v.append(grad_value.astype(BF))
        grads = jnp.concatenate(grads_q + grads_k + grads_v, axis=1)
        sent = dot(grads, back_upper) + dot(grads, back_lower)
        for block in range(N_S):
            s = SPACE_OF_BLOCK[block]
            both = [
                sent[f * depth : (f + 1) * depth, block * own : (block + 1) * own]
                for f in range(2)
            ]
            sent_ref[s, slot * depth : (slot + 1) * depth, :] = jnp.concatenate(
                both, axis=1
            ).astype(BF)
        for f in range(2):
            column = total[f * depth : (f + 1) * depth] / width
            means = means + jnp.where(lane == slot * 2 + f, 1.0, 0.0) * column
    turned = means.T[:16]
    if depth < LANES:
        turned = jnp.concatenate([turned, jnp.zeros((16, LANES - depth), F32)], axis=1)
    turned = turned.astype(BF)
    for s in range(N_S):
        sent_ref[s, slots * depth :, :] = turned


def gather_kernel(slots, in_ref, out_ref, wide_ref):
    depth = out_ref.shape[0] // LINES
    total = in_ref[0].astype(F32)
    for i in range(1, in_ref.shape[0]):
        total = total + in_ref[i].astype(F32)
    for slot in range(slots):
        wide_ref[pl.ds(slot, depth, stride=LINES), :] = total[slot * depth : (slot + 1) * depth]
    means = total[slots * depth :]
    blank = jnp.zeros((LANES - means.shape[0], LANES), F32)
    means = jnp.concatenate([means, blank], axis=0)
    wide_ref[pl.ds(slots, depth, stride=LINES), :] = means.T[:depth]
    wide_ref[pl.ds(slots + 1, depth, stride=LINES), :] = jnp.zeros((depth, LANES), F32)
    out_ref[...] = wide_ref[...].astype(BF)


def on_device(
    patches,
    stem_weight,
    embed_weight,
    frame_embed,
    attention_gain,
    final_gain,
    query_weight,
    key_weight,
    value_weight,
    output_weight,
    unembedding,
    rating_ids,
    target_score,
):
    n_t = lax.axis_size(T_AXES)
    n_s = lax.axis_size(S_AXES)
    everyone = T_AXES + S_AXES
    space_index = lax.axis_index(S_AXES)
    frames_dev, rows_dev, cols, channels = patches.shape
    own_channels = channels // n_s
    count_rows = rows_dev * n_s
    positions = count_rows * cols
    slots = positions // n_t
    width = embed_weight.shape[1]
    inner = query_weight.shape[1]
    heads = inner // HEAD
    all_frames = frames_dev * n_t
    tokens = all_frames * positions
    tokens_dev = frames_dev * positions
    assert frames_dev == 2 and slots == 2

    whole = pl.BlockSpec(memory_space=pltpu.VMEM)
    far = pl.BlockSpec(memory_space=FAR)
    params = pltpu.CompilerParams(vmem_limit_bytes=VMEM_LIMIT)

    patch_rows = patches.reshape(-1, channels)
    stem_half = stem_weight.shape[0] // 2
    packed_rows = patch_rows.shape[0] * (channels // LANES) + stem_half
    packed = pl.pallas_call(
        pack_kernel,
        name="pack",
        out_shape=jax.ShapeDtypeStruct((n_s, packed_rows, LANES), BF),
        in_specs=[far] * 2,
        out_specs=whole,
        scratch_shapes=[
            pltpu.VMEM(patch_rows.shape, BF),
            pltpu.VMEM(stem_weight.shape, BF),
            pltpu.SemaphoreType.DMA((2,)),
        ],
        compiler_params=params,
    )(kept(patch_rows), kept(stem_weight))
    packed, sent_embed = lax.optimization_barrier((packed, embed_weight))
    packed = lax.all_to_all(packed, S_AXES, 0, 0, tiled=True)
    other = lax.ppermute(sent_embed, "zl", [(0, 1), (1, 0)])

    act, gelu_slope, patch_tokens = pl.pallas_call(
        functools.partial(stem_kernel, cols, count_rows),
        name="stem",
        out_shape=(
            jax.ShapeDtypeStruct((own_channels, tokens_dev), BF),
            pltpu.HBM((own_channels, tokens_dev), F32),
            pltpu.HBM((tokens_dev, channels), BF),
        ),
        in_specs=[whole],
        out_specs=(whole, far, far),
        scratch_shapes=[
            pltpu.VMEM((own_channels, tokens_dev), F32),
            pltpu.VMEM((tokens_dev, channels), BF),
            pltpu.VMEM((9 * channels, own_channels), BF),
            pltpu.SemaphoreType.DMA((2,)),
        ],
        compiler_params=params,
    )(packed)
    act = lax.all_gather(act, S_AXES, axis=0, tiled=True)

    lower = lax.axis_index("zl") == 0
    pair = jnp.concatenate(
        [jnp.where(lower, embed_weight, other), jnp.where(lower, other, embed_weight)], axis=0
    )
    across = lax.ppermute(pair, "core", [(0, 1), (1, 0)])
    core_index = lax.axis_index("core")
    vocab_dev = unembedding.shape[0]
    ratings = rating_ids.shape[0]
    place = jnp.stack([core_index, lax.axis_index(everyone) * vocab_dev]).astype(jnp.int32)

    chunks = slots * 3 * inner // LANES + 1
    scalars = pl.BlockSpec(memory_space=pltpu.SMEM)
    moved, embed_sum, scale_row, back_unit = pl.pallas_call(
        functools.partial(embed_kernel, n_t, slots),
        name="embed",
        out_shape=(
            pltpu.HBM((n_t * chunks * 2, LANES), BF),
            jax.ShapeDtypeStruct((1, width), F32),
            jax.ShapeDtypeStruct((1, tokens_dev), F32),
            pltpu.HBM((own_channels, tokens_dev), F32),
        ),
        in_specs=[scalars] * 2 + [whole] * 5 + [far] * 3 + [whole] * 2,
        out_specs=(far, whole, whole, far),
        scratch_shapes=[pltpu.VMEM((n_t * chunks * 2, LANES), kind) for kind in (F32, BF)]
        + [pltpu.VMEM((width, inner), BF)] * 3
        + [pltpu.VMEM((own_channels, tokens_dev), F32), pltpu.SemaphoreType.DMA((4 + STORES,))],
        compiler_params=params,
    )(
        place,
        rating_ids,
        act,
        pair,
        across,
        frame_embed,
        attention_gain[None, :],
        kept(query_weight),
        kept(key_weight),
        kept(value_weight),
        embed_weight,
        unembedding,
    )

    moved = moved.reshape(n_t * chunks, 2, LANES)
    moved = lax.all_to_all(moved, T_AXES, 0, 0, tiled=True)
    moved = moved.reshape(n_t * chunks * 2, LANES)

    gain = attention_gain.astype(F32)
    sides = []
    for part in (pair, across):
        upper, lower_half = halves(part.astype(F32) * gain)
        sides.append(
            jnp.concatenate(
                [
                    dot(w, upper, (((0,), (1,)), ((), ())))
                    + dot(w, lower_half, (((0,), (1,)), ((), ())))
                    for w in (query_weight, key_weight, value_weight)
                ],
                axis=0,
            )
        )
    first_core = core_index == 0
    back = jnp.concatenate(
        [jnp.where(first_core, sides[0], sides[1]), jnp.where(first_core, sides[1], sides[0])],
        axis=1,
    )

    lines = width // LANES
    first = lax.axis_size(("x",) + S_AXES)
    qkv, packed = pl.pallas_call(
        functools.partial(forward_kernel, heads),
        name="attend",
        out_shape=(
            pltpu.HBM((slots, all_frames, 3 * inner), BF),
            jax.ShapeDtypeStruct((first, lines + 8, LANES), F32),
        ),
        in_specs=[whole] * 3 + [pl.BlockSpec(memory_space=pl.ANY)],
        out_specs=(far, whole),
        scratch_shapes=[
            pltpu.VMEM((n_t * chunks * 2, LANES), F32),
            pltpu.VMEM((slots, all_frames, 3 * inner), BF),
            pltpu.SemaphoreType.DMA((slots,)),
        ],
        compiler_params=params,
    )(moved, output_weight, embed_sum, back)

    packed = lax.all_to_all(packed, ("x",) + S_AXES, 0, 0, tiled=True)
    size_x, size_y, size_z = (lax.axis_size(axis) for axis in ("x", "y", "zh"))
    for axis, before, joint, out_lines, out_size in (
        ("y", 1, n_s, lines + 8, size_y),
        ("zh", size_x, 1, lines + size_x * size_y, size_z),
    ):
        packed = pl.pallas_call(
            functools.partial(combine_kernel, lines, before, joint),
            name="combine_" + axis,
            out_shape=jax.ShapeDtypeStruct((out_size, out_lines, LANES), F32),
            in_specs=[whole],
            out_specs=whole,
            compiler_params=params,
        )(packed)
        packed = lax.all_to_all(packed, axis, 0, 0, tiled=True)

    expected, direct, sent = pl.pallas_call(
        functools.partial(backward_kernel, heads, float(tokens), ratings),
        name="attend_back",
        out_shape=(
            jax.ShapeDtypeStruct((8, LANES), F32),
            jax.ShapeDtypeStruct((own_channels, LANES), F32),
            jax.ShapeDtypeStruct((n_s, slots * n_t + 16, LANES), BF),
        ),
        in_specs=[scalars] + [whole] * 6,
        out_specs=(whole,) * 3,
        compiler_params=params,
    )(
        target_score,
        packed,
        final_gain.reshape(lines, LANES),
        output_weight,
        embed_weight,
        qkv,
        back,
    )

    sent = lax.all_to_all(sent, S_AXES, 0, 0, tiled=True)
    sent = pl.pallas_call(
        functools.partial(gather_kernel, slots),
        name="gather",
        out_shape=jax.ShapeDtypeStruct((n_t * LINES, LANES), BF),
        in_specs=[whole],
        out_specs=whole,
        scratch_shapes=[pltpu.VMEM((n_t * LINES, LANES), F32)],
        compiler_params=params,
    )(sent)
    sent = lax.all_to_all(
        sent.reshape(n_t * LINES // 2, 2, LANES), T_AXES, 0, 0, tiled=True
    ).reshape(n_t * LINES, LANES)

    count = 9 * channels * own_channels // LANES
    per = count // n_t
    out_lines = per + per % 2
    sums = pl.pallas_call(
        functools.partial(stem_back_kernel, cols, count_rows, slots, frames_dev),
        name="stem_back",
        out_shape=jax.ShapeDtypeStruct((n_t * out_lines, LANES), BF),
        in_specs=[whole] * 6,
        out_specs=whole,
        scratch_shapes=[
            pltpu.VMEM((9 * channels, own_channels), F32),
            pltpu.VMEM((count, LANES), F32),
            pltpu.VMEM((n_t * out_lines, LANES), F32),
            pltpu.VMEM((n_t * LINES, LANES), F32),
        ],
        compiler_params=params,
    )(sent, back_unit, scale_row, direct, gelu_slope, patch_tokens)
    sums = sums.reshape(n_t * out_lines // 2, 2, LANES)
    sums = lax.all_to_all(sums, T_AXES, 0, 0, tiled=True)
    sums = jnp.sum(sums.reshape(n_t, out_lines // 2, 2, LANES).astype(F32), axis=0)
    sums = lax.all_gather(sums, S_AXES, axis=0, tiled=False).reshape(n_s, out_lines, LANES)
    flat = sums[:, :per].reshape(n_s, -1, own_channels).transpose(1, 0, 2).reshape(-1)
    length = flat.shape[0] // n_s
    stem_gradient = lax.dynamic_slice_in_dim(flat, space_index * length, length, 0)
    return (expected[0, :1], stem_gradient)


def solution(mesh):
    shape = FACTORS[mesh.shape["tm"]] + (2, 2)
    split = Mesh(mesh.devices.reshape(shape), T_AXES + S_AXES)
    both = T_AXES + S_AXES
    in_specs = (
        P(T_AXES, S_AXES, None, None),
        P(S_AXES, None),
        P(S_AXES, None),
        P(T_AXES, None),
        P(),
        P(),
        P(None, S_AXES),
        P(None, S_AXES),
        P(None, S_AXES),
        P(S_AXES, None),
        P(both, None),
        P(),
        P(),
    )
    return jax.shard_map(
        on_device, mesh=split, in_specs=in_specs, out_specs=(P(), P(both)), check_vma=False
    )
```
